32 devices in a mesh: dp: 16 (over z, y, core), tensor: 2 (over x).
Axes of the slice: x: 2, y: 2, z: 4, core: 2. Of those that a mesh axis runs over, the one named last changes fastest.
Arguments:
- tokens: bfloat16 [8192, 2048], P('dp'), may hold values from -6 to 6
- lengths: int32 [16], P('dp'), may hold values from 128 to 512, as said below
- w_query: float32 [2048, 2048], P('dp', 'tensor'), may hold values from -0.125 to 0.125
- w_key: float32 [2048, 2048], P('dp', 'tensor'), may hold values from -0.125 to 0.125
- w_value: float32 [2048, 2048], P('dp', 'tensor'), may hold values from -0.125 to 0.125
- w_beta: float32 [2048, 16], P('dp', 'tensor'), may hold values from -0.125 to 0.125
- conv_query: float32 [4, 2048], P(None, 'tensor'), may hold values from -3 to 3
- conv_key: float32 [4, 2048], P(None, 'tensor'), may hold values from -3 to 3
- conv_value: float32 [4, 2048], P(None, 'tensor'), may hold values from -3 to 3
- head_gain: float32 [128], replicated, may hold values from 0.25 to 1.75
- w_out: float32 [2048, 2048], P('tensor', 'dp'), may hold values from -0.125 to 0.125
- norm_attn: float32 [2048], replicated, may hold values from 0.25 to 1.75
- norm_ffn: float32 [2048], replicated, may hold values from 0.25 to 1.75
- w_gate: float32 [2048, 5632], P('dp', 'tensor'), may hold values from -0.125 to 0.125
- w_up: float32 [2048, 5632], P('dp', 'tensor'), may hold values from -0.125 to 0.125
- w_down: float32 [5632, 2048], P('tensor', 'dp'), may hold values from -0.078125 to 0.078125
- cotangent: bfloat16 [8192, 2048], P('dp'), may hold values from -6 to 6
Outputs:
- block_out: bfloat16 [8192, 2048], P('dp')
- grad_tokens: float32 [8192, 2048], P('dp')
- grad_query: float32 [2048, 2048], P('dp', 'tensor')
- grad_key: float32 [2048, 2048], P('dp', 'tensor')
- grad_value: float32 [2048, 2048], P('dp', 'tensor')
- grad_beta: float32 [2048, 16], P('dp', 'tensor')
- grad_conv_query: float32 [4, 2048], P(None, 'tensor')
- grad_conv_key: float32 [4, 2048], P(None, 'tensor')
- grad_conv_value: float32 [4, 2048], P(None, 'tensor')
- grad_head_gain: float32 [128], replicated
- grad_out: float32 [2048, 2048], P('tensor', 'dp')
- grad_norm_attn: float32 [2048], replicated
- grad_norm_ffn: float32 [2048], replicated
- grad_gate: float32 [2048, 5632], P('dp', 'tensor')
- grad_up: float32 [2048, 5632], P('dp', 'tensor')
- grad_down: float32 [5632, 2048], P('tensor', 'dp')
The draws below stay inside these ranges and needn't reach their ends.
Inputs may be any that keep to these rules, and one draw needn't show every extreme that they name: `lengths`: how many leading slots of each sequence hold tokens; some sequence is full and some holds 128.
All inputs are finite; a program needn't handle non-finite values.
Results may differ from the reference program's by a relative error of at most 0.012.
The reference program's roundings to bfloat16 on the way (of `first`, `mixed`, `second` and `hidden`) count: a program that leaves them out, or rounds other values in their place, can miss the bound.
Values may be sent and summed in bfloat16 or wider, within the bound.
A program may use at most 256 MiB of HBM per device.

```python
import jax
import jax.numpy as jnp
from jax import lax

D = 2048
HEADS = 16
HEAD = 128
FF = 5632
SPAN = 64
CONV = 4
SLOTS = 512
SEQS = 16
TOKENS = 8192


def draw_lengths(key, part):
    first, second = jax.random.split(jax.random.fold_in(key, 17))
    values = jax.random.randint(first, (SEQS,), SLOTS // 4, SLOTS + 1)
    order = jax.random.permutation(second, SEQS)
    values = values.at[order[0]].set(SLOTS)
    values = values.at[order[1]].set(SLOTS // 4)
    return values.astype(jnp.int32)


def spiked(drawn, rng, source, target, shards_of, factor):
    owner, partner = [(jnp.arange(drawn.shape[dim]) // (drawn.shape[dim] // shards_of)).reshape([-1 if axis == dim else 1 for axis in range(drawn.ndim)]) for dim in (source, target)]
    chosen = jax.random.permutation(rng, shards_of)[partner]
    strong = (owner == chosen) | (owner == (partner + shards_of // 2) % shards_of)
    return jnp.where(strong, factor * drawn, drawn)


def block_scale(key, dims, shards, least, largest):
    level, own = 1.0, jax.random.fold_in(key, 6)
    for dim, parts in shards:
        heights = jnp.exp(jax.random.uniform(jax.random.fold_in(own, dim), (parts,), jnp.float32, least / len(shards), largest / len(shards)))
        level = level * jnp.repeat(heights, dims[dim] // parts).reshape([-1 if axis == dim else 1 for axis in range(len(dims))])
    return level


def gaussian(key, extent, scale, limit, cuts=(), kind=jnp.bfloat16):
    drawn = scale * jax.random.normal(key, extent, jnp.float32)
    if cuts:
        drawn = drawn * block_scale(key, extent, cuts, -0.22, 0.18)
    return jnp.clip(drawn, -limit, limit).astype(kind)


def bell_draw_with(key, dims, deviation, limit, shards, heavy, kind=jnp.bfloat16):
    drawn = deviation * jax.random.normal(key, dims, jnp.float32)
    if shards:
        drawn = drawn * block_scale(key, dims, shards, -0.22, 0.18)
    return jnp.clip(spiked(drawn, jax.random.fold_in(key, 3), *heavy), -limit, limit).astype(kind)


def setup_inputs(seed: int = 0) -> dict:
    key_of = jax.random.split(jax.random.key(seed), 18)
    return {
        "tokens": gaussian(key_of[0], (TOKENS, D), 1.0, 6.0, ((0, 16),)),
        "lengths": draw_lengths(jax.random.fold_in(key_of[17], 71), 0),
        "w_query": gaussian(key_of[2], (D, D), D ** -0.5, 0.125, ((0, 16), (1, 2)), jnp.float32),
        "w_key": gaussian(key_of[3], (D, D), D ** -0.5, 0.125, ((0, 16), (1, 2)), jnp.float32),
        "w_value": gaussian(key_of[4], (D, D), D ** -0.5, 0.125, ((0, 16), (1, 2)), jnp.float32),
        "w_beta": gaussian(key_of[5], (D, HEADS), D ** -0.5, 0.125, ((0, 16), (1, 2)), jnp.float32),
        "conv_query": gaussian(key_of[6], (CONV, D), 0.5, 3.0, ((1, 2),), jnp.float32),
        "conv_key": gaussian(key_of[7], (CONV, D), 0.5, 3.0, ((1, 2),), jnp.float32),
        "conv_value": gaussian(key_of[8], (CONV, D), 0.5, 3.0, ((1, 2),), jnp.float32),
        "head_gain": jnp.clip(1.0 + 0.15 * jax.random.normal(key_of[9], (HEAD,), jnp.float32), 0.25, 1.75),
        "w_out": gaussian(key_of[10], (D, D), D ** -0.5, 0.125, ((0, 2), (1, 16)), jnp.float32),
        "norm_attn": jnp.clip(1.0 + 0.15 * jax.random.normal(key_of[11], (D,), jnp.float32), 0.25, 1.75),
        "norm_ffn": jnp.clip(1.0 + 0.15 * jax.random.normal(key_of[12], (D,), jnp.float32), 0.25, 1.75),
        "w_gate": gaussian(key_of[13], (D, FF), D ** -0.5, 0.125, ((0, 16), (1, 2)), jnp.float32),
        "w_up": gaussian(key_of[14], (D, FF), D ** -0.5, 0.125, ((0, 16), (1, 2)), jnp.float32),
        "w_down": gaussian(key_of[15], (FF, D), FF ** -0.5, 0.078125, ((0, 2), (1, 16)), jnp.float32),
        "cotangent": bell_draw_with(key_of[16], (TOKENS, D), 1.0, 6.0, ((0, 16),), (0, 1, 16, 2.0)),
    }


precise = lax.Precision.HIGHEST
epsilon = 1e-06

@jax.custom_vjp
def low(v):
    return lax.optimization_barrier(v.astype(jnp.bfloat16)).astype(jnp.float32)

@jax.custom_vjp
def low_back(v):
    return v

def low_keep(v):
    return (low(v), None)

def low_pass(kept, grad):
    return (grad,)

def back_keep(v):
    return (v, None)

def back_low(kept, grad):
    return (low(grad),)
low.defvjp(low_keep, low_pass)
low_back.defvjp(back_keep, back_low)

def product(left, right):
    return jnp.dot(left.astype(jnp.float32), right.astype(jnp.float32), precision=precise, preferred_element_type=jnp.float32)

def einsum_high(form, left, right):
    return jnp.einsum(form, left, right, precision=precise)

def row_norm(values, gain):
    return values * lax.rsqrt(lax.optimization_barrier(jnp.mean(values * values, -1, keepdims=True)) + epsilon) * gain

def unit_rows(values):
    return values * lax.rsqrt(lax.optimization_barrier(jnp.sum(values * values, -1, keepdims=True)) + epsilon)

def span_step(state, block):
    query, key, value, strength = block
    size = key.shape[-2]
    width = key.shape[-1]
    rows = lax.broadcasted_iota(jnp.int32, (size, size), 0)
    cols = lax.broadcasted_iota(jnp.int32, (size, size), 1)
    strict = (rows > cols).astype(jnp.float32)
    inner = einsum_high('...ie,...je->...ij', key, key)
    matrix = jnp.eye(size, dtype=jnp.float32) + strict * inner * strength[..., :, None]
    right_side = jnp.concatenate([strength[..., None] * key, strength[..., None] * value], -1)
    solved = jax.scipy.linalg.solve_triangular(matrix, right_side, lower=True, unit_diagonal=True)
    fresh = solved[..., width:] - einsum_high('...ce,...ve->...cv', solved[..., :width], state)
    scores = einsum_high('...ie,...je->...ij', query, key) * (rows >= cols).astype(jnp.float32)
    result = einsum_high('...ce,...ve->...cv', query, state) + einsum_high('...ij,...jv->...iv', scores, fresh)
    state = state + einsum_high('...cv,...ce->...ve', fresh, key)
    return (state, result)

def delta_rule(query, key, value, strength):
    leading = query.shape[:-2]
    length = query.shape[-2]
    width = query.shape[-1]
    count = length // SPAN

    def blocks(values):
        return jnp.moveaxis(values.reshape(leading + (count, SPAN, width)), -3, 0)
    spans_beta = jnp.moveaxis(strength.reshape(leading + (count, SPAN)), -2, 0)
    start = jnp.zeros(leading + (width, width), jnp.float32)
    _, outputs = lax.scan(jax.checkpoint(span_step), start, (blocks(query), blocks(key), blocks(value), spans_beta))
    return jnp.moveaxis(outputs, 0, -3).reshape(leading + (length, width))

def short_conv(values, weight):
    length = values.shape[1]
    padded = jnp.pad(values, ((0, 0), (CONV - 1, 0), (0, 0)))
    total = jnp.zeros_like(values)
    for offset in range(CONV):
        total = total + weight[offset] * padded[:, offset:offset + length]
    return total

def layer(inputs, seq_lengths, weights):
    w_query, w_key, w_value, w_beta, conv_query, conv_key, conv_value, head_gain, w_out, norm_attn, norm_ffn, w_gate, w_up, w_down = weights
    group = seq_lengths.shape[0]
    length = inputs.shape[0] // group
    first = low(row_norm(inputs, norm_attn))
    query_raw = low_back(product(first, w_query))
    key_raw = low_back(product(first, w_key))
    value_raw = low_back(product(first, w_value))
    beta_raw = low_back(product(first, w_beta))

    def heads_first(values):
        return values.reshape(group, length, HEADS, HEAD).transpose(0, 2, 1, 3)

    def conv_silu(values, weight):
        return jax.nn.silu(short_conv(values.reshape(group, length, D), weight))
    query = unit_rows(heads_first(conv_silu(query_raw, conv_query))) * HEAD ** (-0.5)
    key = unit_rows(heads_first(conv_silu(key_raw, conv_key)))
    value = heads_first(conv_silu(value_raw, conv_value))
    beta = jax.nn.sigmoid(beta_raw).reshape(group, length, HEADS).transpose(0, 2, 1)
    result = delta_rule(query, key, value, beta)
    mixed = low(row_norm(result, head_gain).transpose(0, 2, 1, 3).reshape(group * length, D))
    middle = inputs + low_back(product(mixed, w_out))
    second = low(row_norm(middle, norm_ffn))
    gate = low_back(product(second, w_gate))
    up_proj = low_back(product(second, w_up))
    hidden = low(jax.nn.silu(gate) * up_proj)
    final = middle + low_back(product(hidden, w_down))
    positions = jnp.arange(length, dtype=jnp.int32)
    valid = (positions[None, :] < seq_lengths[:, None]).astype(jnp.float32).reshape(group * length, 1)
    return final * valid

def reference(tokens, lengths, w_query, w_key, w_value, w_beta, conv_query, conv_key, conv_value, head_gain, w_out, norm_attn, norm_ffn, w_gate, w_up, w_down, cotangent):
    group = max(1, min(SEQS, 4096 // SLOTS))
    while SEQS % group != 0:
        group = group - 1
    count = SEQS // group
    params = tuple((v.astype(jnp.float32) for v in (w_query, w_key, w_value, w_beta, conv_query, conv_key, conv_value, head_gain, w_out, norm_attn, norm_ffn, w_gate, w_up, w_down)))
    seq_lengths = lengths.astype(jnp.int32).reshape(count, group)

    def forward(inputs, weights):
        lowered = (low(weights[0]), low(weights[1]), low(weights[2]), low(weights[3]), weights[4], weights[5], weights[6], weights[7], low(weights[8]), weights[9], weights[10], low(weights[11]), low(weights[12]), low(weights[13]))

        def one(pair):
            return layer(pair[0], pair[1], lowered)
        grouped = inputs.reshape(count, group * SLOTS, D)
        outputs = lax.map(jax.checkpoint(one), (grouped, seq_lengths))
        return outputs.reshape(TOKENS, D)
    result, pullback = jax.vjp(forward, tokens.astype(jnp.float32), params)
    grad_inputs, grads = pullback(cotangent.astype(jnp.float32))
    return (result.astype(jnp.bfloat16), grad_inputs, grads[0], grads[1], grads[2], grads[3], grads[4], grads[5], grads[6], grads[7], grads[8], grads[9], grads[10], grads[11], grads[12], grads[13])
```

```python
import functools
import jax
import jax.numpy as jnp
from jax import lax
from jax.experimental import pallas as pl
from jax.experimental.pallas import tpu as pltpu
from jax.sharding import PartitionSpec as P

CHUNK = 128
epsilon = 1e-06
HIGH = lax.Precision.HIGHEST
F32 = jnp.float32
BF16 = jnp.bfloat16


def dot(left, right, dims, passes):
    form = (dims, ((), ()))
    if passes == 6:
        return lax.dot_general(left, right, form, precision=HIGH, preferred_element_type=F32)
    left_hi, right_hi = left.astype(BF16), right.astype(BF16)
    total = lax.dot_general(left_hi, right_hi, form, preferred_element_type=F32)
    if passes == 3:
        left_lo = (left - left_hi.astype(F32)).astype(BF16)
        right_lo = (right - right_hi.astype(F32)).astype(BF16)
        total = total + (
            lax.dot_general(left_hi, right_lo, form, preferred_element_type=F32)
            + lax.dot_general(left_lo, right_hi, form, preferred_element_type=F32)
        )
    return total


def nn(left, right, passes):
    return dot(left, right, ((1,), (0,)), passes)


def nt(left, right, passes):
    return dot(left, right, ((1,), (1,)), passes)


def tn(left, right, passes):
    return dot(left, right, ((0,), (0,)), passes)


def sigmoid(x):
    return 1.0 / (1.0 + jnp.exp(-x))


def shift_down(cur, tail, by):
    rolled = pltpu.roll(cur, by, 0)
    rows = lax.broadcasted_iota(jnp.int32, tail.shape, 0)
    top = jnp.where(rows < by, pltpu.roll(tail, by, 0), rolled[:8])
    return jnp.concatenate([top, rolled[8:]], 0)


def shift_up(cur, head, by):
    size = cur.shape[0]
    rolled = pltpu.roll(cur, size - by, 0)
    rows = lax.broadcasted_iota(jnp.int32, head.shape, 0)
    bottom = jnp.where(rows >= 8 - by, pltpu.roll(head, 8 - by, 0), rolled[size - 8 :])
    return jnp.concatenate([rolled[: size - 8], bottom], 0)


def unit_scale(values):
    return lax.rsqrt(jnp.sum(values * values, -1, keepdims=True) + epsilon)


def masks(size):
    rows = lax.broadcasted_iota(jnp.int32, (size, size), 0)
    cols = lax.broadcasted_iota(jnp.int32, (size, size), 1)
    return rows, cols, rows ^ cols


def unit_lower_inverse(lower, passes):
    size = lower.shape[0]
    rows, cols, apart = masks(size)
    inverse = jnp.where(rows == cols, 1.0, jnp.where(apart < 2, -lower, 0.0))
    span = 2
    while span < size:
        corner = jnp.where((apart < 2 * span) & (apart >= span), lower, 0.0)
        inverse = inverse - nn(inverse, nn(corner, inverse, passes), passes)
        span *= 2
    return inverse


def pick(table, column):
    lanes = lax.broadcasted_iota(jnp.int32, table.shape, 1)
    return jnp.sum(jnp.where(lanes == column, table, 0.0), 1, keepdims=True)


def forward_kernel(heads, width, ps, qkv_ref, beta_ref, conv_ref, gain_ref,
                   mixed_ref, out_ref, fresh_ref, state_ref, solve_ref, carry):
    group = pl.program_id(0)
    chunk = CHUNK
    length = qkv_ref.shape[0]
    carry[...] = jnp.zeros_like(carry)
    p_gram, p_inv, p_state, p_out = ps

    def step(c, _):
        base = pl.multiple_of(c * chunk, chunk)
        rows = pl.ds(base, chunk)
        before = pl.ds(pl.multiple_of(jnp.maximum(base - 8, 0), 8), 8)
        beta = sigmoid(beta_ref[rows, :])
        row, col, _ = masks(chunk)
        gain = gain_ref[...]
        for j in range(heads):
            parts = []
            for part in range(3):
                lanes = pl.ds((part * heads + j) * width, width)
                cur = qkv_ref[rows, lanes]
                tail = jnp.where(c > 0, qkv_ref[before, lanes], 0.0)
                taps = conv_ref[:, lanes]
                total = taps[3:4] * cur
                for by in (1, 2, 3):
                    total = total + taps[3 - by : 4 - by] * shift_down(cur, tail, by)
                parts.append(total * sigmoid(total))
            query, key, value = parts
            query = query * (unit_scale(query) * width ** (-0.5))
            key = key * unit_scale(key)
            strength = pick(beta, group * heads + j)
            gram = nt(key, key, p_gram)
            solve = unit_lower_inverse(jnp.where(row > col, gram * strength, 0.0), p_inv)
            state = carry[j]
            error = value - nn(key, state, p_state)
            fresh = nn(solve, strength * error, p_state)
            scores = jnp.where(row >= col, nt(query, key, p_out), 0.0)
            out = nn(query, state, p_out) + nn(scores, fresh, p_out)
            carry[j] = state + tn(key, fresh, p_state)
            state_ref[j, c] = state
            solve_ref[j, c] = solve
            lanes = pl.ds(j * width, width)
            fresh_ref[rows, lanes] = fresh
            out_ref[rows, lanes] = out
            scale = lax.rsqrt(jnp.mean(out * out, -1, keepdims=True) + epsilon)
            mixed_ref[rows, lanes] = (out * scale * gain).astype(BF16)
        return 0

    lax.fori_loop(0, length // chunk, step, 0)


def backward_kernel(heads, width, ps, qkv_ref, beta_ref, conv_ref, gain_ref, grad_ref, out_ref, fresh_ref,
                    state_ref, solve_ref, raw_ref, gbeta_ref, gconv_ref, ggain_ref, carry, ahead):
    group = pl.program_id(0)
    chunk = CHUNK
    length = qkv_ref.shape[0]
    count = length // chunk
    carry[...] = jnp.zeros_like(carry)
    ahead[...] = jnp.zeros_like(ahead)
    gconv_ref[...] = jnp.zeros_like(gconv_ref)
    p_gram, p_chain, p_out = ps

    @pl.when(group == 0)
    def _():
        gbeta_ref[...] = jnp.zeros_like(gbeta_ref)
        ggain_ref[...] = jnp.zeros_like(ggain_ref)

    def step(i, _):
        c = count - 1 - i
        base = pl.multiple_of(c * chunk, chunk)
        rows = pl.ds(base, chunk)
        before = pl.ds(pl.multiple_of(jnp.maximum(base - 8, 0), 8), 8)
        beta = sigmoid(beta_ref[rows, :])
        row, col, _ = masks(chunk)
        gain = gain_ref[...]
        lane = lax.broadcasted_iota(jnp.int32, (chunk, beta_ref.shape[1]), 1)
        gbeta = jnp.zeros((chunk, beta_ref.shape[1]), F32)
        ggain = jnp.zeros_like(gain)
        for j in range(heads):
            pre, sig, shifts, acts, units = [], [], [], [], []
            for part in range(3):
                lanes = pl.ds((part * heads + j) * width, width)
                cur = qkv_ref[rows, lanes]
                tail = jnp.where(c > 0, qkv_ref[before, lanes], 0.0)
                taps = conv_ref[:, lanes]
                moved = [cur] + [shift_down(cur, tail, by) for by in (1, 2, 3)]
                total = taps[3:4] * cur
                for by in (1, 2, 3):
                    total = total + taps[3 - by : 4 - by] * moved[by]
                gate = sigmoid(total)
                pre.append(total)
                sig.append(gate)
                shifts.append(moved)
                acts.append(total * gate)
            query_scale = unit_scale(acts[0])
            key_scale = unit_scale(acts[1])
            query_unit = acts[0] * query_scale
            query = query_unit * width ** (-0.5)
            key = acts[1] * key_scale
            value = acts[2]
            strength = pick(beta, group * heads + j)
            lanes = pl.ds(j * width, width)
            out = out_ref[rows, lanes]
            fresh = fresh_ref[rows, lanes]
            state = state_ref[j, c]
            solve = solve_ref[j, c]
            grad_mixed = grad_ref[rows, lanes]
            scale = lax.rsqrt(jnp.mean(out * out, -1, keepdims=True) + epsilon)
            normal = out * scale
            ggain = ggain + jnp.sum(grad_mixed * normal, 0, keepdims=True)
            scaled = grad_mixed * gain
            grad_out = scale * (scaled - normal * jnp.mean(scaled * normal, -1, keepdims=True))

            grad_state = carry[j]
            gram = nt(key, key, p_gram)
            scores = jnp.where(row >= col, nt(query, key, p_out), 0.0)
            error = value - nn(key, state, p_out)
            grad_scores = jnp.where(row >= col, nt(grad_out, fresh, p_out), 0.0)
            grad_fresh = tn(scores, grad_out, p_chain) + nn(key, grad_state, p_chain)
            pulled = tn(solve, grad_fresh, p_chain)
            grad_error = strength * pulled
            grad_lower = jnp.where(row > col, -nt(pulled, fresh, p_out), 0.0)
            grad_strength = jnp.sum(pulled * error + grad_lower * gram, -1, keepdims=True)
            grad_gram = grad_lower * strength
            grad_query = nt(grad_out, state, p_out) + nn(grad_scores, key, p_out)
            grad_key = (
                nt(fresh, grad_state, p_out)
                - nt(grad_error, state, p_out)
                + tn(grad_scores, query, p_out)
                + nn(grad_gram + grad_gram.T, key, p_out)
            )
            carry[j] = grad_state + tn(query, grad_out, p_chain) - tn(key, grad_error, p_chain)

            gbeta = jnp.where(
                lane == group * heads + j, grad_strength * (strength * (1.0 - strength)), gbeta
            )
            grad_query = grad_query * width ** (-0.5)
            grad_acts = (
                query_scale * (grad_query - query_unit * jnp.sum(grad_query * query_unit, -1, keepdims=True)),
                key_scale * (grad_key - key * jnp.sum(grad_key * key, -1, keepdims=True)),
                grad_error,
            )
            for part in range(3):
                lanes = pl.ds((part * heads + j) * width, width)
                gate = sig[part]
                grad_pre = grad_acts[part] * gate * (1.0 + pre[part] * (1.0 - gate))
                taps = conv_ref[:, lanes]
                after = ahead[:, lanes]
                total = taps[3:4] * grad_pre
                for by in (1, 2, 3):
                    total = total + taps[3 - by : 4 - by] * shift_up(grad_pre, after, by)
                raw_ref[rows, lanes] = total.astype(BF16)
                ahead[:, lanes] = grad_pre[:8]
                sums = [jnp.sum(grad_pre * shifts[part][3 - tap], 0, keepdims=True) for tap in range(4)]
                gconv_ref[:, lanes] += jnp.concatenate(sums, 0)
        gbeta_ref[rows, :] += gbeta.astype(BF16)
        ggain_ref[...] += ggain
        return 0

    lax.fori_loop(0, count, step, 0)


def delta_forward(qkv, conv, gain, heads, block, ps=(6, 6, 6, 6)):
    length = qkv.shape[0]
    width = gain.shape[1]
    groups = heads // block
    span = 3 * block * width
    last = groups * span // 128
    count = length // CHUNK
    return pl.pallas_call(
        functools.partial(forward_kernel, block, width, ps),
        grid=(groups,),
        in_specs=[
            pl.BlockSpec((length, span), lambda g: (0, g)),
            pl.BlockSpec((length, 128), lambda g: (0, last)),
            pl.BlockSpec((4, span), lambda g: (0, g)),
            pl.BlockSpec((1, width), lambda g: (0, 0)),
        ],
        out_specs=[
            pl.BlockSpec((length, block * width), lambda g: (0, g)),
            pl.BlockSpec((length, block * width), lambda g: (0, g)),
            pl.BlockSpec((length, block * width), lambda g: (0, g)),
            pl.BlockSpec((block, count, width, width), lambda g: (g, 0, 0, 0)),
            pl.BlockSpec((block, count, CHUNK, CHUNK), lambda g: (g, 0, 0, 0)),
        ],
        out_shape=[
            jax.ShapeDtypeStruct((length, heads * width), BF16),
            jax.ShapeDtypeStruct((length, heads * width), F32),
            jax.ShapeDtypeStruct((length, heads * width), F32),
            jax.ShapeDtypeStruct((heads, count, width, width), F32),
            jax.ShapeDtypeStruct((heads, count, CHUNK, CHUNK), F32),
        ],
        scratch_shapes=[pltpu.VMEM((block, width, width), F32)],
        compiler_params=pltpu.CompilerParams(vmem_limit_bytes=48 * 2**20),
        name="delta_forward",
    )(qkv, qkv, conv, gain)


def delta_backward(qkv, conv, gain, grad, out, fresh, state, solve, heads, block, ps=(6, 6, 6)):
    length = qkv.shape[0]
    width = gain.shape[1]
    groups = heads // block
    span = 3 * block * width
    last = groups * span // 128
    count = length // CHUNK
    wide = pl.BlockSpec((length, block * width), lambda g: (0, g))
    return pl.pallas_call(
        functools.partial(backward_kernel, block, width, ps),
        grid=(groups,),
        in_specs=[
            pl.BlockSpec((length, span), lambda g: (0, g)),
            pl.BlockSpec((length, 128), lambda g: (0, last)),
            pl.BlockSpec((4, span), lambda g: (0, g)),
            pl.BlockSpec((1, width), lambda g: (0, 0)),
            wide,
            wide,
            wide,
            pl.BlockSpec((block, count, width, width), lambda g: (g, 0, 0, 0)),
            pl.BlockSpec((block, count, CHUNK, CHUNK), lambda g: (g, 0, 0, 0)),
        ],
        out_specs=[
            pl.BlockSpec((length, span), lambda g: (0, g)),
            pl.BlockSpec((length, 128), lambda g: (0, 0)),
            pl.BlockSpec((4, span), lambda g: (0, g)),
            pl.BlockSpec((1, width), lambda g: (0, 0)),
        ],
        out_shape=[
            jax.ShapeDtypeStruct((length, groups * span), BF16),
            jax.ShapeDtypeStruct((length, 128), BF16),
            jax.ShapeDtypeStruct((4, groups * span), F32),
            jax.ShapeDtypeStruct((1, width), F32),
        ],
        scratch_shapes=[
            pltpu.VMEM((block, width, width), F32),
            pltpu.VMEM((8, span), F32),
        ],
        compiler_params=pltpu.CompilerParams(vmem_limit_bytes=56 * 2**20),
        name="delta_backward",
    )(qkv, qkv, conv, gain, grad, out, fresh, state, solve)


def matmul(left, right):
    return jnp.dot(left, right, preferred_element_type=F32)


def left_outer(left, right):
    return lax.dot_general(left, right, (((0,), (0,)), ((), ())), preferred_element_type=F32)


def right_inner(left, right):
    return lax.dot_general(left, right, (((1,), (1,)), ((), ())), preferred_element_type=F32)


def row_norm(values, gain):
    return values * lax.rsqrt(jnp.mean(values * values, -1, keepdims=True) + epsilon) * gain


def norm_back(values, gain, grad):
    scale = lax.rsqrt(jnp.mean(values * values, -1, keepdims=True) + epsilon)
    normal = values * scale
    scaled = grad * gain
    grad_gain = jnp.sum(grad * normal, 0)
    grad_values = scale * (scaled - normal * jnp.mean(scaled * normal, -1, keepdims=True))
    return (grad_values, grad_gain)


def pair_sum(partial, tensor):
    if tensor != 2:
        return lax.psum(partial, "tensor")
    own = lax.reduce_precision(partial, 8, 7)
    other = lax.ppermute(own.astype(BF16), "tensor", [(0, 1), (1, 0)])
    return own + other.astype(F32)


def by_groups(parts, block):
    span = block * WIDTH
    return [part[:, g * span : (g + 1) * span] for g in range(parts[0].shape[1] // span) for part in parts]


def from_groups(whole, block, index, columns):
    span = block * WIDTH
    return jnp.concatenate(
        [whole[:, (3 * g + index) * span : (3 * g + index + 1) * span] for g in range(columns // span)], 1
    )


WIDTH = 128
LANES = 128


def scatter_rows(partial):
    return lax.psum_scatter(partial.astype(BF16), "dp", scatter_dimension=0, tiled=True).astype(F32)


def body(sizes, tokens, lengths, w_query, w_key, w_value, w_beta, conv_query, conv_key, conv_value, head_gain,
         w_out, norm_attn, norm_ffn, w_gate, w_up, w_down, cotangent):
    tensor = sizes["tensor"]
    inputs = tokens.astype(F32)
    length = inputs.shape[0]
    columns = w_query.shape[1]
    hidden_units = w_gate.shape[1]
    heads = w_beta.shape[1]
    block = 4 if heads % 4 == 0 else 1
    strengths = jnp.pad(w_beta.astype(BF16), ((0, 0), (0, LANES - heads)))
    low = [w.astype(BF16) for w in (w_query, w_key, w_value)]
    w_mixer = lax.all_gather(
        jnp.concatenate(by_groups(low, block) + [strengths], 1), "dp", axis=0, tiled=True
    )
    w_rest = lax.all_gather(
        jnp.concatenate([w_out.astype(BF16).T, w_down.astype(BF16).T, w_gate.astype(BF16), w_up.astype(BF16)], 1),
        "dp", axis=0, tiled=True,
    )
    w_out_t = w_rest[:, :columns]
    w_down_t = w_rest[:, columns : columns + hidden_units]
    w_gate_up = w_rest[:, columns + hidden_units :]
    conv = jnp.concatenate(by_groups([conv_query, conv_key, conv_value], block), 1)
    gain = head_gain[None]

    first = row_norm(inputs, norm_attn).astype(BF16)
    qkv = matmul(first, w_mixer)
    mixed, out, fresh, state, solve = delta_forward(qkv, conv, gain, heads, block)
    middle = inputs + pair_sum(right_inner(mixed, w_out_t), tensor)
    second = row_norm(middle, norm_ffn).astype(BF16)
    gate_up = matmul(second, w_gate_up)
    gate, up_proj = gate_up[:, :hidden_units], gate_up[:, hidden_units:]
    sigma = jax.nn.sigmoid(gate)
    activated = gate * sigma
    hidden = (activated * up_proj).astype(BF16)
    positions = lax.broadcasted_iota(jnp.int32, (length, 1), 0)
    valid = (positions < lengths[0]).astype(F32)
    upstream = cotangent.astype(F32) * valid
    upstream_low = upstream.astype(BF16)
    grad_hidden = matmul(upstream_low, w_down_t)
    grad_gate_act = (grad_hidden * up_proj * sigma * (1.0 + gate * (1.0 - sigma))).astype(BF16)
    grad_up_act = (grad_hidden * activated).astype(BF16)
    grad_gate_up_act = jnp.concatenate([grad_gate_act, grad_up_act], 1)
    grad_second = pair_sum(right_inner(grad_gate_up_act, w_gate_up), tensor)
    final = middle + pair_sum(right_inner(hidden, w_down_t), tensor)
    block_out = (final * valid).astype(BF16)
    grad_middle_norm, grad_norm_ffn = norm_back(middle, norm_ffn, grad_second)
    grad_middle = upstream + grad_middle_norm
    grad_middle_low = grad_middle.astype(BF16)
    ffn_grads = scatter_rows(
        jnp.concatenate([left_outer(upstream_low, hidden).astype(BF16), left_outer(second, grad_gate_up_act).astype(BF16)], 1)
    )
    grad_mixed = matmul(grad_middle_low, w_out_t)
    raw, graw_beta, grad_conv, grad_head = delta_backward(
        qkv, conv, gain, grad_mixed, out, fresh, state, solve, heads, block
    )
    raw = jnp.concatenate([raw, graw_beta], 1)
    grad_first = pair_sum(right_inner(raw, w_mixer), tensor)
    grad_inputs_norm, grad_norm_attn = norm_back(inputs, norm_attn, grad_first)
    grad_tokens = grad_middle + grad_inputs_norm
    attn_grads = scatter_rows(
        jnp.concatenate([left_outer(first, raw).astype(BF16), left_outer(grad_middle_low, mixed).astype(BF16)], 1)
    )
    smalls = lax.psum(
        (grad_conv, lax.psum(grad_head[0], "tensor"), grad_norm_attn, grad_norm_ffn), "dp"
    )
    span = 3 * columns
    qkv_grads = attn_grads[:, :span]
    return (
        block_out,
        grad_tokens,
        from_groups(qkv_grads, block, 0, columns),
        from_groups(qkv_grads, block, 1, columns),
        from_groups(qkv_grads, block, 2, columns),
        attn_grads[:, span : span + heads],
        from_groups(smalls[0], block, 0, columns),
        from_groups(smalls[0], block, 1, columns),
        from_groups(smalls[0], block, 2, columns),
        smalls[1],
        attn_grads[:, span + LANES :].T,
        smalls[2],
        smalls[3],
        ffn_grads[:, hidden_units : 2 * hidden_units],
        ffn_grads[:, 2 * hidden_units :],
        ffn_grads[:, :hidden_units].T,
    )


def solution(mesh):
    rows, both, cols = P("dp", None), P("dp", "tensor"), P("tensor", "dp")
    taps = P(None, "tensor")
    in_specs = (rows, P("dp"), both, both, both, both, taps, taps, taps, P(), cols, P(), P(), both, both, cols, rows)
    out_specs = (rows, rows, both, both, both, both, taps, taps, taps, P(), cols, P(), P(), both, both, cols)
    return jax.shard_map(
        functools.partial(body, dict(mesh.shape)), mesh=mesh, in_specs=in_specs, out_specs=out_specs, check_vma=False
    )
```

```python
import functools
import jax
import jax.numpy as jnp
from jax import lax
from jax.experimental import pallas as pl
from jax.experimental.pallas import tpu as pltpu
from jax.sharding import PartitionSpec as P

CHUNK = 128
WIDTH = 128
LANES = 128
epsilon = 1e-06
HIGH = lax.Precision.HIGHEST
F32 = jnp.float32
BF16 = jnp.bfloat16


def dot(left, right, dims, passes):
    form = (dims, ((), ()))
    if passes == 6:
        return lax.dot_general(left, right, form, precision=HIGH, preferred_element_type=F32)
    left_hi, right_hi = left.astype(BF16), right.astype(BF16)
    total = lax.dot_general(left_hi, right_hi, form, preferred_element_type=F32)
    if passes == 3:
        left_lo = (left - left_hi.astype(F32)).astype(BF16)
        right_lo = (right - right_hi.astype(F32)).astype(BF16)
        total = total + (
            lax.dot_general(left_hi, right_lo, form, preferred_element_type=F32)
            + lax.dot_general(left_lo, right_hi, form, preferred_element_type=F32)
        )
    return total


def nn(left, right, passes):
    return dot(left, right, ((1,), (0,)), passes)


def nt(left, right, passes):
    return dot(left, right, ((1,), (1,)), passes)


def tn(left, right, passes):
    return dot(left, right, ((0,), (0,)), passes)


def sigmoid(x):
    return 1.0 / (1.0 + jnp.exp(-x))


def shift_down(cur, tail, by):
    rolled = pltpu.roll(cur, by, 0)
    rows = lax.broadcasted_iota(jnp.int32, tail.shape, 0)
    top = jnp.where(rows < by, pltpu.roll(tail, by, 0), rolled[:8])
    return jnp.concatenate([top, rolled[8:]], 0)


def shift_up(cur, head, by):
    size = cur.shape[0]
    rolled = pltpu.roll(cur, size - by, 0)
    rows = lax.broadcasted_iota(jnp.int32, head.shape, 0)
    bottom = jnp.where(rows >= 8 - by, pltpu.roll(head, 8 - by, 0), rolled[size - 8 :])
    return jnp.concatenate([rolled[: size - 8], bottom], 0)


def unit_scale(values):
    return lax.rsqrt(jnp.sum(values * values, -1, keepdims=True) + epsilon)


def masks(size):
    rows = lax.broadcasted_iota(jnp.int32, (size, size), 0)
    cols = lax.broadcasted_iota(jnp.int32, (size, size), 1)
    return rows, cols, rows ^ cols


def unit_lower_inverse(lower, passes):
    size = lower.shape[0]
    rows, cols, apart = masks(size)
    inverse = jnp.where(rows == cols, 1.0, jnp.where(apart < 2, -lower, 0.0))
    span = 2
    while span < size:
        corner = jnp.where((apart < 2 * span) & (apart >= span), lower, 0.0)
        inverse = inverse - nn(inverse, nn(corner, inverse, passes), passes)
        span *= 2
    return inverse


def pick(table, column):
    lanes = lax.broadcasted_iota(jnp.int32, table.shape, 1)
    return jnp.sum(jnp.where(lanes == column, table, 0.0), 1, keepdims=True)


def forward_kernel(heads, width, ps, qkv_ref, beta_ref, conv_ref, gain_ref,
                   mixed_ref, out_ref, fresh_ref, state_ref, solve_ref, carry):
    group = pl.program_id(0)
    chunk = CHUNK
    length = qkv_ref.shape[0]
    carry[...] = jnp.zeros_like(carry)
    p_gram, p_inv, p_state, p_out = ps

    def step(c, _):
        base = pl.multiple_of(c * chunk, chunk)
        rows = pl.ds(base, chunk)
        before = pl.ds(pl.multiple_of(jnp.maximum(base - 8, 0), 8), 8)
        beta = sigmoid(beta_ref[rows, :])
        row, col, _ = masks(chunk)
        gain = gain_ref[...]
        for j in range(heads):
            parts = []
            for part in range(3):
                lanes = pl.ds((part * heads + j) * width, width)
                cur = qkv_ref[rows, lanes]
                tail = jnp.where(c > 0, qkv_ref[before, lanes], 0.0)
                taps = conv_ref[:, lanes]
                total = taps[3:4] * cur
                for by in (1, 2, 3):
                    total = total + taps[3 - by : 4 - by] * shift_down(cur, tail, by)
                parts.append(total * sigmoid(total))
            query, key, value = parts
            query = query * (unit_scale(query) * width ** (-0.5))
            key = key * unit_scale(key)
            strength = pick(beta, group * heads + j)
            gram = nt(key, key, p_gram)
            solve = unit_lower_inverse(jnp.where(row > col, gram * strength, 0.0), p_inv)
            state = carry[j]
            error = value - nn(key, state, p_state)
            fresh = nn(solve, strength * error, p_state)
            scores = jnp.where(row >= col, nt(query, key, p_out), 0.0)
            out = nn(query, state, p_out) + nn(scores, fresh, p_out)
            carry[j] = state + tn(key, fresh, p_state)
            state_ref[j, c] = state
            solve_ref[j, c] = solve
            lanes = pl.ds(j * width, width)
            fresh_ref[rows, lanes] = fresh
            out_ref[rows, lanes] = out
            scale = lax.rsqrt(jnp.mean(out * out, -1, keepdims=True) + epsilon)
            mixed_ref[rows, lanes] = (out * scale * gain).astype(BF16)
        return 0

    lax.fori_loop(0, length // chunk, step, 0)


def backward_kernel(heads, width, ps, group, qkv_ref, beta_ref, conv_ref, gain_ref, grad_ref, out_ref, fresh_ref,
                    state_ref, solve_ref, raw_ref, gbeta_ref, gconv_ref, ggain_ref, carry, ahead):
    chunk = CHUNK
    length = qkv_ref.shape[0]
    count = length // chunk
    carry[...] = jnp.zeros_like(carry)
    ahead[...] = jnp.zeros_like(ahead)
    gconv_ref[...] = jnp.zeros_like(gconv_ref)
    p_gram, p_chain, p_out = ps

    ggain_ref[...] = jnp.zeros_like(ggain_ref)

    def step(i, _):
        c = count - 1 - i
        base = pl.multiple_of(c * chunk, chunk)
        rows = pl.ds(base, chunk)
        before = pl.ds(pl.multiple_of(jnp.maximum(base - 8, 0), 8), 8)
        beta = sigmoid(beta_ref[rows, :])
        row, col, _ = masks(chunk)
        gain = gain_ref[...]
        lane = lax.broadcasted_iota(jnp.int32, (chunk, beta_ref.shape[1]), 1)
        gbeta = jnp.zeros((chunk, beta_ref.shape[1]), F32)
        ggain = jnp.zeros_like(gain)
        for j in range(heads):
            pre, sig, shifts, acts, units = [], [], [], [], []
            for part in range(3):
                lanes = pl.ds((part * heads + j) * width, width)
                cur = qkv_ref[rows, lanes]
                tail = jnp.where(c > 0, qkv_ref[before, lanes], 0.0)
                taps = conv_ref[:, lanes]
                moved = [cur] + [shift_down(cur, tail, by) for by in (1, 2, 3)]
                total = taps[3:4] * cur
                for by in (1, 2, 3):
                    total = total + taps[3 - by : 4 - by] * moved[by]
                gate = sigmoid(total)
                pre.append(total)
                sig.append(gate)
                shifts.append(moved)
                acts.append(total * gate)
            query_scale = unit_scale(acts[0])
            key_scale = unit_scale(acts[1])
            query_unit = acts[0] * query_scale
            query = query_unit * width ** (-0.5)
            key = acts[1] * key_scale
            value = acts[2]
            strength = pick(beta, group * heads + j)
            lanes = pl.ds(j * width, width)
            out = out_ref[rows, lanes]
            fresh = fresh_ref[rows, lanes]
            state = state_ref[j, c]
            solve = solve_ref[j, c]
            grad_mixed = grad_ref[rows, lanes]
            scale = lax.rsqrt(jnp.mean(out * out, -1, keepdims=True) + epsilon)
            normal = out * scale
            ggain = ggain + jnp.sum(grad_mixed * normal, 0, keepdims=True)
            scaled = grad_mixed * gain
            grad_out = scale * (scaled - normal * jnp.mean(scaled * normal, -1, keepdims=True))

            grad_state = carry[j]
            gram = nt(key, key, p_gram)
            scores = jnp.where(row >= col, nt(query, key, p_out), 0.0)
            error = value - nn(key, state, p_out)
            grad_scores = jnp.where(row >= col, nt(grad_out, fresh, p_out), 0.0)
            grad_fresh = tn(scores, grad_out, p_chain) + nn(key, grad_state, p_chain)
            pulled = tn(solve, grad_fresh, p_chain)
            grad_error = strength * pulled
            grad_lower = jnp.where(row > col, -nt(pulled, fresh, p_out), 0.0)
            grad_strength = jnp.sum(pulled * error + grad_lower * gram, -1, keepdims=True)
            grad_gram = grad_lower * strength
            grad_query = nt(grad_out, state, p_out) + nn(grad_scores, key, p_out)
            grad_key = (
                nt(fresh, grad_state, p_out)
                - nt(grad_error, state, p_out)
                + tn(grad_scores, query, p_out)
                + nn(grad_gram + grad_gram.T, key, p_out)
            )
            carry[j] = grad_state + tn(query, grad_out, p_chain) - tn(key, grad_error, p_chain)

            gbeta = jnp.where(
                lane == group * heads + j, grad_strength * (strength * (1.0 - strength)), gbeta
            )
            grad_query = grad_query * width ** (-0.5)
            grad_acts = (
                query_scale * (grad_query - query_unit * jnp.sum(grad_query * query_unit, -1, keepdims=True)),
                key_scale * (grad_key - key * jnp.sum(grad_key * key, -1, keepdims=True)),
                grad_error,
            )
            for part in range(3):
                lanes = pl.ds((part * heads + j) * width, width)
                gate = sig[part]
                grad_pre = grad_acts[part] * gate * (1.0 + pre[part] * (1.0 - gate))
                taps = conv_ref[:, lanes]
                after = ahead[:, lanes]
                total = taps[3:4] * grad_pre
                for by in (1, 2, 3):
                    total = total + taps[3 - by : 4 - by] * shift_up(grad_pre, after, by)
                raw_ref[rows, lanes] = total.astype(BF16)
                ahead[:, lanes] = grad_pre[:8]
                sums = [jnp.sum(grad_pre * shifts[part][3 - tap], 0, keepdims=True) for tap in range(4)]
                gconv_ref[:, lanes] += jnp.concatenate(sums, 0)
        gbeta_ref[rows, :] = gbeta.astype(BF16)
        ggain_ref[...] += ggain
        return 0

    lax.fori_loop(0, count, step, 0)


def delta_forward(qkv, conv, gain, heads, block, ps=(6, 6, 6, 6)):
    length = qkv.shape[0]
    width = gain.shape[1]
    groups = heads // block
    span = 3 * block * width
    last = groups * span // 128
    count = length // CHUNK
    return pl.pallas_call(
        functools.partial(forward_kernel, block, width, ps),
        grid=(groups,),
        in_specs=[
            pl.BlockSpec((length, span), lambda g: (0, g)),
            pl.BlockSpec((length, 128), lambda g: (0, last)),
            pl.BlockSpec((4, span), lambda g: (0, g)),
            pl.BlockSpec((1, width), lambda g: (0, 0)),
        ],
        out_specs=[
            pl.BlockSpec((length, block * width), lambda g: (0, g)),
            pl.BlockSpec((length, block * width), lambda g: (0, g)),
            pl.BlockSpec((length, block * width), lambda g: (0, g)),
            pl.BlockSpec((block, count, width, width), lambda g: (g, 0, 0, 0)),
            pl.BlockSpec((block, count, CHUNK, CHUNK), lambda g: (g, 0, 0, 0)),
        ],
        out_shape=[
            jax.ShapeDtypeStruct((length, heads * width), BF16),
            jax.ShapeDtypeStruct((length, heads * width), F32),
            jax.ShapeDtypeStruct((length, heads * width), F32),
            jax.ShapeDtypeStruct((heads, count, width, width), F32),
            jax.ShapeDtypeStruct((heads, count, CHUNK, CHUNK), F32),
        ],
        scratch_shapes=[pltpu.VMEM((block, width, width), F32)],
        compiler_params=pltpu.CompilerParams(vmem_limit_bytes=48 * 2**20),
        name="delta_forward",
    )(qkv, qkv, conv, gain)


def delta_backward(qkv, conv, gain, grad, out, fresh, state, solve, heads, block, group, ps=(6, 6, 6)):
    length = qkv.shape[0]
    width = gain.shape[1]
    span = 3 * block * width
    last = heads // block * span // LANES
    count = length // CHUNK
    wide = pl.BlockSpec((length, block * width), lambda g: (0, group))
    whole = lambda *shape: pl.BlockSpec(shape, lambda g: (0,) * len(shape))
    return pl.pallas_call(
        functools.partial(backward_kernel, block, width, ps, group),
        grid=(1,),
        in_specs=[
            pl.BlockSpec((length, span), lambda g: (0, group)),
            pl.BlockSpec((length, LANES), lambda g: (0, last)),
            pl.BlockSpec((4, span), lambda g: (0, group)),
            pl.BlockSpec((1, width), lambda g: (0, 0)),
            wide,
            wide,
            wide,
            pl.BlockSpec((block, count, width, width), lambda g: (group, 0, 0, 0)),
            pl.BlockSpec((block, count, CHUNK, CHUNK), lambda g: (group, 0, 0, 0)),
        ],
        out_specs=[whole(length, span), whole(length, LANES), whole(4, span), whole(1, width)],
        out_shape=[
            jax.ShapeDtypeStruct((length, span), BF16),
            jax.ShapeDtypeStruct((length, LANES), BF16),
            jax.ShapeDtypeStruct((4, span), F32),
            jax.ShapeDtypeStruct((1, width), F32),
        ],
        scratch_shapes=[
            pltpu.VMEM((block, width, width), F32),
            pltpu.VMEM((8, span), F32),
        ],
        compiler_params=pltpu.CompilerParams(vmem_limit_bytes=40 * 2**20),
        cost_estimate=pl.CostEstimate(flops=2**34, bytes_accessed=2**25, transcendentals=2**21),
        name="delta_backward",
    )(qkv, qkv, conv, gain, grad, out, fresh, state, solve)


def matmul(left, right):
    return jnp.dot(left, right, preferred_element_type=F32)


def left_outer(left, right):
    return lax.dot_general(left, right, (((0,), (0,)), ((), ())), preferred_element_type=F32)


def right_inner(left, right):
    return lax.dot_general(left, right, (((1,), (1,)), ((), ())), preferred_element_type=F32)


def row_norm(values, gain):
    return values * lax.rsqrt(jnp.mean(values * values, -1, keepdims=True) + epsilon) * gain


def norm_back(values, gain, grad):
    scale = lax.rsqrt(jnp.mean(values * values, -1, keepdims=True) + epsilon)
    normal = values * scale
    scaled = grad * gain
    grad_gain = jnp.sum(grad * normal, 0)
    grad_values = scale * (scaled - normal * jnp.mean(scaled * normal, -1, keepdims=True))
    return (grad_values, grad_gain)


def swap(values, axis, size, by):
    return lax.ppermute(values, axis, [(d, d ^ by) for d in range(size)])


def exchange(partial):
    own = lax.reduce_precision(partial, 8, 7)
    return own, swap(own.astype(BF16), "tensor", 2, 1)

def radices(size):
    digits = []
    while size > 1:
        digits.append(2 if len(digits) < 2 else min(4, size))
        size //= digits[-1]
    return digits


def offsets(size):
    found, stride = [0], 1
    for digit in radices(size):
        found = [old + value * stride for old in found for value in range(digit)]
        stride *= digit
    return found


def flipped(index, bits, size):
    result, unit = 0, 1
    while unit < size:
        result = result + (index // unit + bits // unit) % 2 * unit
        unit *= 2
    return result


def place_kernel(bits, block, where_ref, *refs):
    me = where_ref[0]
    target = refs[-1]
    for which, source in enumerate(refs[:-1]):
        for place, bit in enumerate(bits):
            owner = pl.multiple_of((me ^ bit) * block, block)
            target[which, place * block : (place + 1) * block] = source[pl.ds(owner, block)]


def by_place(arrays, size):
    me = lax.axis_index("dp")
    rows, depth = arrays[0].shape
    return pl.pallas_call(
        functools.partial(place_kernel, offsets(size), rows // size),
        in_specs=[pl.BlockSpec(memory_space=pltpu.SMEM)] + [pl.BlockSpec(memory_space=pltpu.VMEM)] * len(arrays),
        out_specs=pl.BlockSpec(memory_space=pltpu.VMEM),
        out_shape=jax.ShapeDtypeStruct((len(arrays), rows, depth), arrays[0].dtype),
        compiler_params=pltpu.CompilerParams(vmem_limit_bytes=24 * 2**20),
        name="by_place",
    )(me[None].astype(jnp.int32), *arrays)


def scatter_kernel(size, count, tiles, tile, which, lags, left_ref, right_ref, out_ref, *refs):
    digits = radices(size)
    stages = len(digits)
    block = left_ref.shape[1] // size
    wide = tiles * tile
    landed, sent, held_in = refs[:stages], refs[stages : 2 * stages], refs[2 * stages : 3 * stages]
    send_sems, recv_sems = refs[3 * stages : 4 * stages], refs[4 * stages : 5 * stages]
    load_sem = refs[5 * stages]
    me = lax.axis_index("dp")
    strides, keeps, rest, stride = [], [], size, 1
    for digit in digits:
        strides.append(stride)
        stride *= digit
        rest //= digit
        keeps.append(rest * block)

    barrier = pltpu.get_barrier_semaphore()
    peers = 0
    for stage, digit in enumerate(digits):
        for value in range(1, digit):
            pl.semaphore_signal(
                barrier, inc=1, device_id={"dp": flipped(me, value * strides[stage], size)},
                device_id_type=pl.DeviceIdType.MESH,
            )
            peers += 1
    pl.semaphore_wait(barrier, peers)

    def remote(stage, value, chunk):
        rows = keeps[stage]
        return pltpu.make_async_remote_copy(
            src_ref=sent[stage].at[chunk % 2, pl.ds((value - 1) * rows, rows)],
            dst_ref=landed[stage].at[chunk, value - 1],
            send_sem=send_sems[stage].at[chunk % 2, value - 1],
            recv_sem=recv_sems[stage].at[chunk, value - 1],
            device_id={"dp": flipped(me, value * strides[stage], size)},
            device_id_type=pl.DeviceIdType.MESH,
        )

    def load(stage, chunk, first, rows):
        if stage:
            for value in range(1, digits[stage - 1]):
                remote(stage - 1, value, chunk).wait_recv()
        target = held_in[stage - 1]
        copies = []
        for early in range(stage):
            for value in range(1, digits[early]):
                place = len(copies)
                copies.append(
                    pltpu.make_async_copy(
                        landed[early].at[chunk, value - 1, pl.ds(first, rows)], target.at[place], load_sem.at[place]
                    )
                )
        for copy in copies:
            copy.start()
        return copies, target

    def product(chunk, first, rows, extra, extras, store):
        part = next(p for p in (512, 384, 256, 128, 96, 64, 32) if rows % p == 0)

        @pl.loop(0, tiles)
        def _(t):
            at = chunk * tiles + t
            right = right_ref[:, pl.ds(pl.multiple_of(at * tile, tile), tile)]
            inside = pl.ds(pl.multiple_of(t * tile, tile), tile)
            for begin in range(0, rows, part):
                left = left_ref[which(at), first + begin : first + begin + part, :]
                total = jnp.dot(left, right, preferred_element_type=F32)
                for place in range(extras):
                    total = total + extra[place, begin : begin + part, inside].astype(F32)
                store(begin, part, inside, at, total)

    def run_stage(stage, chunk):
        rows = keeps[stage] * (digits[stage] - 1)
        first = keeps[stage]
        copies, extra = load(stage, chunk, first, rows)

        @pl.when(chunk >= 2)
        def _():
            for value in range(1, digits[stage]):
                remote(stage, value, chunk - 2).wait_send()

        for copy in copies:
            copy.wait()

        def store(begin, part, inside, at, total):
            sent[stage][chunk % 2, begin : begin + part, inside] = total.astype(BF16)

        product(chunk, first, rows, extra, len(copies), store)
        for value in range(1, digits[stage]):
            remote(stage, value, chunk).start()

    def run_last(chunk):
        copies, extra = load(stages, chunk, 0, block)
        for copy in copies:
            copy.wait()

        def store(begin, part, inside, at, total):
            out_ref[begin : begin + part, pl.ds(pl.multiple_of(at * tile, tile), tile)] = total

        product(chunk, 0, block, extra, len(copies), store)

    def step(i, carry):
        for stage, lag in enumerate(lags):

            @pl.when((i >= lag) & (i < count + lag))
            def _():
                if stage < stages:
                    run_stage(stage, i - lag)
                else:
                    run_last(i - lag)

        return carry

    lax.fori_loop(0, count + lags[-1], step, 0)
    for chunk in range(max(count - 2, 0), count):
        for stage in range(stages):
            for value in range(1, digits[stage]):
                remote(stage, value, chunk).wait_send()


def scatter_products(lefts, right, size, count, tile, which, name, collective_id):
    depth, columns = right.shape
    block = lefts.shape[1] // size
    wide = columns // count
    digits = radices(size)
    stages = len(digits)
    keeps, rest = [], size
    for digit in digits:
        rest //= digit
        keeps.append(rest * block)
    sends = [keep * (digit - 1) for keep, digit in zip(keeps, digits)]
    early = [sum(digit - 1 for digit in digits[: stage + 1]) for stage in range(stages)]
    reads = sends[1:] + [block]
    lags = tuple([0, 1] + [3 + 2 * stage for stage in range(stages - 1)])[: stages + 1]
    places = [jax.ShapeDtypeStruct((count, digit - 1, keep, wide), BF16) for keep, digit in zip(keeps, digits)]
    return pl.pallas_call(
        functools.partial(scatter_kernel, size, count, wide // tile, tile, which, lags),
        in_specs=[pl.BlockSpec(memory_space=pltpu.VMEM)] * 2,
        out_specs=[pl.BlockSpec(memory_space=pltpu.VMEM)] + [pl.BlockSpec(memory_space=pl.ANY)] * stages,
        out_shape=[jax.ShapeDtypeStruct((block, columns), F32)] + places,
        scratch_shapes=[pltpu.VMEM((2, rows, wide), BF16) for rows in sends]
        + [pltpu.VMEM((number, rows, wide), BF16) for number, rows in zip(early, reads)]
        + [pltpu.SemaphoreType.DMA((2, digit - 1)) for digit in digits]
        + [pltpu.SemaphoreType.DMA((count, digit - 1)) for digit in digits]
        + [pltpu.SemaphoreType.DMA((early[-1],))],
        compiler_params=pltpu.CompilerParams(
            collective_id=collective_id, has_side_effects=True, vmem_limit_bytes=52 * 2**20
        ),
        cost_estimate=pl.CostEstimate(flops=2**36, bytes_accessed=2**27, transcendentals=0),
        name=name,
    )(lefts, right)[0]


def butterfly(values, size):
    by = 1
    while by < size:
        values = values + swap(values, "dp", size, by)
        by *= 2
    return values


def by_groups(parts, block):
    span = block * WIDTH
    return [part[:, g * span : (g + 1) * span] for g in range(parts[0].shape[1] // span) for part in parts]


def from_groups(groups, block, index):
    span = block * WIDTH
    return jnp.concatenate([group[:, index * span : (index + 1) * span] for group in groups], 1)


def body(size, tokens, lengths, w_query, w_key, w_value, w_beta, conv_query, conv_key, conv_value, head_gain,
         w_out, norm_attn, norm_ffn, w_gate, w_up, w_down, cotangent):
    inputs = tokens.astype(F32)
    length = inputs.shape[0]
    columns = w_query.shape[1]
    units = w_gate.shape[1]
    heads = w_beta.shape[1]
    block = 4 if heads % 4 == 0 else 1
    groups = heads // block
    span = 3 * block * WIDTH
    strengths = jnp.pad(w_beta.astype(BF16), ((0, 0), (0, LANES - heads)))
    low = [w.astype(BF16) for w in (w_query, w_key, w_value)]
    w_mixer = lax.all_gather(
        jnp.concatenate(by_groups(low, block) + [strengths], 1), "dp", axis=0, tiled=True
    )
    w_rest = lax.all_gather(
        jnp.concatenate([w_out.astype(BF16).T, w_down.astype(BF16).T, w_gate.astype(BF16), w_up.astype(BF16)], 1),
        "dp", axis=0, tiled=True,
    )
    w_out_t = w_rest[:, :columns]
    w_down_t = w_rest[:, columns : columns + units]
    w_gate_up = w_rest[:, columns + units :]
    conv = jnp.concatenate(by_groups([conv_query, conv_key, conv_value], block), 1)
    gain = head_gain[None]

    first = row_norm(inputs, norm_attn).astype(BF16)
    qkv = matmul(first, w_mixer)
    mixed, out, fresh, state, solve = delta_forward(qkv, conv, gain, heads, block)
    own, other = exchange(right_inner(mixed, w_out_t))
    middle = inputs + (own + other.astype(F32))
    second = row_norm(middle, norm_ffn).astype(BF16)
    positions = lax.broadcasted_iota(jnp.int32, (length, 1), 0)
    valid = (positions < lengths[0]).astype(F32)
    upstream = cotangent.astype(F32) * valid
    upstream_low = upstream.astype(BF16)
    grad_hidden = matmul(upstream_low, w_down_t)
    gate_up = matmul(second, w_gate_up)
    gate, up_proj = gate_up[:, :units], gate_up[:, units:]
    sigma = jax.nn.sigmoid(gate)
    activated = gate * sigma
    hidden = (activated * up_proj).astype(BF16)
    grad_gate_act = (grad_hidden * up_proj * sigma * (1.0 + gate * (1.0 - sigma))).astype(BF16)
    grad_up_act = (grad_hidden * activated).astype(BF16)
    grad_second_own, grad_second_other = exchange(
        right_inner(grad_gate_act, w_gate_up[:, :units]) + right_inner(grad_up_act, w_gate_up[:, units:])
    )

    ffn_lefts = by_place([upstream_low.T, second.T], size)
    ffn_grads = scatter_products(
        ffn_lefts, jnp.concatenate([hidden, grad_gate_act, grad_up_act], 1), size, 11, 256,
        lambda at: (at // (units // 256) + 1) // 2, "ffn_grads", 0,
    )
    grad_second = grad_second_own + grad_second_other.astype(F32)
    grad_middle_norm, grad_norm_ffn = norm_back(middle, norm_ffn, grad_second)
    grad_middle = upstream + grad_middle_norm
    grad_middle_low = grad_middle.astype(BF16)
    grad_mixed = matmul(grad_middle_low, w_out_t)
    final_own, final_other = exchange(right_inner(hidden, w_down_t))
    raws, strength_raws, grad_convs = [], [], []
    grad_head = jnp.zeros((1, WIDTH), F32)
    for g in range(groups):
        raw, strength_raw, grad_conv, grad_gain = delta_backward(
            qkv, conv, gain, grad_mixed, out, fresh, state, solve, heads, block, g
        )
        raws.append(raw)
        strength_raws.append(strength_raw)
        grad_convs.append(grad_conv)
        grad_head = grad_head + grad_gain
    raw = jnp.concatenate(raws + [functools.reduce(jnp.add, strength_raws)], 1)
    grad_first_own, grad_first_other = exchange(right_inner(raw, w_mixer))
    grad_head = grad_head + swap(grad_head, "tensor", 2, 1)
    mixer_lefts = by_place([first.T, grad_middle_low.T], size)
    raw_columns = raw.shape[1]
    mixer_grads = scatter_products(
        mixer_lefts, jnp.concatenate([raw, mixed], 1), size, 11, 128,
        lambda at: at // (raw_columns // 128), "mixer_grads", 1,
    )
    final = middle + (final_own + final_other.astype(F32))
    block_out = (final * valid).astype(BF16)
    grad_inputs_norm, grad_norm_attn = norm_back(
        inputs, norm_attn, grad_first_own + grad_first_other.astype(F32)
    )
    grad_tokens = grad_middle + grad_inputs_norm
    small = jnp.concatenate(
        [g.reshape(-1) for g in grad_convs] + [grad_head[0], grad_norm_ffn, grad_norm_attn]
    ).reshape(-1, LANES)
    small = butterfly(small, size).reshape(-1)
    taps = 4 * span
    convs = [small[g * taps : (g + 1) * taps].reshape(4, span) for g in range(groups)]
    small = small[groups * taps :]
    model = inputs.shape[1]
    attn_grads = [mixer_grads[:, g * span : (g + 1) * span] for g in range(groups)]
    strength_at = groups * span
    return (
        block_out,
        grad_tokens,
        from_groups(attn_grads, block, 0),
        from_groups(attn_grads, block, 1),
        from_groups(attn_grads, block, 2),
        mixer_grads[:, strength_at : strength_at + heads],
        from_groups(convs, block, 0),
        from_groups(convs, block, 1),
        from_groups(convs, block, 2),
        small[:WIDTH],
        mixer_grads[:, strength_at + LANES :].T,
        small[WIDTH + model :],
        small[WIDTH : WIDTH + model],
        ffn_grads[:, units : 2 * units],
        ffn_grads[:, 2 * units :],
        ffn_grads[:, :units].T,
    )


def solution(mesh):
    rows, both, cols = P("dp", None), P("dp", "tensor"), P("tensor", "dp")
    taps = P(None, "tensor")
    in_specs = (rows, P("dp"), both, both, both, both, taps, taps, taps, P(), cols, P(), P(), both, both, cols, rows)
    out_specs = (rows, rows, both, both, both, both, taps, taps, taps, P(), cols, P(), P(), both, both, cols)
    return jax.shard_map(
        functools.partial(body, mesh.shape["dp"]), mesh=mesh, in_specs=in_specs, out_specs=out_specs, check_vma=False
    )
```

```python
import functools
import jax
import jax.numpy as jnp
from jax import lax
from jax.experimental import pallas as pl
from jax.experimental.pallas import tpu as pltpu
from jax.sharding import PartitionSpec as P

CHUNK = 128
WIDTH = 128
LANES = 128
epsilon = 1e-06
HIGH = lax.Precision.HIGHEST
F32 = jnp.float32
BF16 = jnp.bfloat16
MESH = pl.DeviceIdType.MESH


def dot(left, right, dims, passes):
    form = (dims, ((), ()))
    if passes == 6:
        return lax.dot_general(left, right, form, precision=HIGH, preferred_element_type=F32)
    left_hi, right_hi = left.astype(BF16), right.astype(BF16)
    total = lax.dot_general(left_hi, right_hi, form, preferred_element_type=F32)
    if passes == 3:
        left_lo = (left - left_hi.astype(F32)).astype(BF16)
        right_lo = (right - right_hi.astype(F32)).astype(BF16)
        total = total + (
            lax.dot_general(left_hi, right_lo, form, preferred_element_type=F32)
            + lax.dot_general(left_lo, right_hi, form, preferred_element_type=F32)
        )
    return total


def nn(left, right, passes):
    return dot(left, right, ((1,), (0,)), passes)


def nt(left, right, passes):
    return dot(left, right, ((1,), (1,)), passes)


def tn(left, right, passes):
    return dot(left, right, ((0,), (0,)), passes)


def sigmoid(x):
    return 1.0 / (1.0 + jnp.exp(-x))


def shift_down(cur, tail, by):
    rolled = pltpu.roll(cur, by, 0)
    rows = lax.broadcasted_iota(jnp.int32, tail.shape, 0)
    top = jnp.where(rows < by, pltpu.roll(tail, by, 0), rolled[:8])
    return jnp.concatenate([top, rolled[8:]], 0)


def shift_up(cur, head, by):
    size = cur.shape[0]
    rolled = pltpu.roll(cur, size - by, 0)
    rows = lax.broadcasted_iota(jnp.int32, head.shape, 0)
    bottom = jnp.where(rows >= 8 - by, pltpu.roll(head, 8 - by, 0), rolled[size - 8 :])
    return jnp.concatenate([rolled[: size - 8], bottom], 0)


def unit_scale(values):
    return lax.rsqrt(jnp.sum(values * values, -1, keepdims=True) + epsilon)


def masks(size):
    rows = lax.broadcasted_iota(jnp.int32, (size, size), 0)
    cols = lax.broadcasted_iota(jnp.int32, (size, size), 1)
    return rows, cols, rows ^ cols


def unit_lower_inverses(lowers, passes):
    size = lowers[0].shape[0]
    rows, cols, apart = masks(size)
    inverses = [jnp.where(rows == cols, 1.0, jnp.where(apart < 2, -lower, 0.0)) for lower in lowers]
    span = 2
    while span < size:
        corner = (apart < 2 * span) & (apart >= span)
        halves = [nn(jnp.where(corner, a, 0.0), x, passes) for a, x in zip(lowers, inverses)]
        inverses = [x - nn(x, half, passes) for x, half in zip(inverses, halves)]
        span *= 2
    return inverses


def pick(table, column):
    lanes = lax.broadcasted_iota(jnp.int32, table.shape, 1)
    return jnp.sum(jnp.where(lanes == column, table, 0.0), 1, keepdims=True)


def forward_kernel(heads, width, ps, qkv_ref, beta_ref, conv_ref, gain_ref,
                   mixed_ref, out_ref, fresh_ref, state_ref, solve_ref, carry):
    group = pl.program_id(0)
    chunk = CHUNK
    length = qkv_ref.shape[0]
    carry[...] = jnp.zeros_like(carry)
    p_gram, p_inv, p_state, p_out = ps

    def step(c, _):
        base = pl.multiple_of(c * chunk, chunk)
        rows = pl.ds(base, chunk)
        before = pl.ds(pl.multiple_of(jnp.maximum(base - 8, 0), 8), 8)
        beta = sigmoid(beta_ref[rows, :])
        row, col, _ = masks(chunk)
        gain = gain_ref[...]
        queries, keys, values, strengths = [], [], [], []
        for j in range(heads):
            parts = []
            for part in range(3):
                lanes = pl.ds((part * heads + j) * width, width)
                cur = qkv_ref[rows, lanes]
                tail = jnp.where(c > 0, qkv_ref[before, lanes], 0.0)
                taps = conv_ref[:, lanes]
                total = taps[3:4] * cur
                for by in (1, 2, 3):
                    total = total + taps[3 - by : 4 - by] * shift_down(cur, tail, by)
                parts.append(total * sigmoid(total))
            query, key, value = parts
            queries.append(query * (unit_scale(query) * width ** (-0.5)))
            keys.append(key * unit_scale(key))
            values.append(value)
            strengths.append(pick(beta, group * heads + j))
        grams = [nt(key, key, p_gram) for key in keys]
        solves = unit_lower_inverses(
            [jnp.where(row > col, gram * strength, 0.0) for gram, strength in zip(grams, strengths)], p_inv
        )
        states = [carry[j] for j in range(heads)]
        errors = [value - nn(key, state, p_state) for value, key, state in zip(values, keys, states)]
        freshes = [nn(solve, s * e, p_state) for solve, s, e in zip(solves, strengths, errors)]
        for j in range(heads):
            carry[j] = states[j] + tn(keys[j], freshes[j], p_state)
        scores = [jnp.where(row >= col, nt(q, k, p_out), 0.0) for q, k in zip(queries, keys)]
        outs = [
            nn(q, s, p_out) + nn(score, f, p_out) for q, s, score, f in zip(queries, states, scores, freshes)
        ]
        for j, out in enumerate(outs):
            state_ref[j, c] = states[j]
            solve_ref[j, c] = solves[j]
            lanes = pl.ds(j * width, width)
            fresh_ref[rows, lanes] = freshes[j]
            out_ref[rows, lanes] = out
            scale = lax.rsqrt(jnp.mean(out * out, -1, keepdims=True) + epsilon)
            mixed_ref[rows, lanes] = (out * scale * gain).astype(BF16)
        return 0

    lax.fori_loop(0, length // chunk, step, 0)


def delta_forward(qkv, conv, gain, heads, block, ps=(6, 6, 6, 6)):
    length = qkv.shape[0]
    width = gain.shape[1]
    groups = heads // block
    span = 3 * block * width
    last = groups * span // 128
    count = length // CHUNK
    return pl.pallas_call(
        functools.partial(forward_kernel, block, width, ps),
        grid=(groups,),
        in_specs=[
            pl.BlockSpec((length, span), lambda g: (0, g)),
            pl.BlockSpec((length, 128), lambda g: (0, last)),
            pl.BlockSpec((4, span), lambda g: (0, g)),
            pl.BlockSpec((1, width), lambda g: (0, 0)),
        ],
        out_specs=[
            pl.BlockSpec((length, block * width), lambda g: (0, g)),
            pl.BlockSpec((length, block * width), lambda g: (0, g)),
            pl.BlockSpec((length, block * width), lambda g: (0, g)),
            pl.BlockSpec((block, count, width, width), lambda g: (g, 0, 0, 0)),
            pl.BlockSpec((block, count, CHUNK, CHUNK), lambda g: (g, 0, 0, 0)),
        ],
        out_shape=[
            jax.ShapeDtypeStruct((length, heads * width), BF16),
            jax.ShapeDtypeStruct((length, heads * width), F32),
            jax.ShapeDtypeStruct((length, heads * width), F32),
            jax.ShapeDtypeStruct((heads, count, width, width), F32),
            jax.ShapeDtypeStruct((heads, count, CHUNK, CHUNK), F32),
        ],
        scratch_shapes=[pltpu.VMEM((block, width, width), F32)],
        compiler_params=pltpu.CompilerParams(vmem_limit_bytes=48 * 2**20),
        name="delta_forward",
    )(qkv, qkv, conv, gain)


def backward_piece(heads, width, passes, group, c, cur_ref, tail_ref, beta_ref, conv_ref, gain_ref, grad_ref, out_ref,
                   fresh_ref, state_ref, solve_ref, raw_ref, gbeta_ref, gconv_ref, ggain_ref, carry, ahead):
    chunk = CHUNK
    span = 3 * heads * width
    rows = pl.ds(pl.multiple_of(c * chunk, chunk), chunk)
    beta = sigmoid(beta_ref[...])
    row, col, _ = masks(chunk)
    gain = gain_ref[...]
    lane = lax.broadcasted_iota(jnp.int32, beta.shape, 1)
    every = range(heads)

    def lanes_of(part, j):
        return pl.ds((part * heads + j) * width, width)

    def wide_lanes(part, j):
        return pl.ds(pl.multiple_of(group * span + (part * heads + j) * width, width), width)

    def before_silu(part, j, keep):
        cur = cur_ref[:, lanes_of(part, j)]
        tail = jnp.where(c > 0, tail_ref[:, lanes_of(part, j)], 0.0)
        taps = conv_ref[:, wide_lanes(part, j)]
        moved = [cur] + [shift_down(cur, tail, by) for by in (1, 2, 3)]
        total = taps[3:4] * cur
        for by in (1, 2, 3):
            total = total + taps[3 - by : 4 - by] * moved[by]
        return moved if keep else total

    queries, keys, errors, strengths, grad_outs, freshes = [], [], [], [], [], []
    ggain = jnp.zeros_like(gain)
    for j in every:
        acts = []
        for part in range(3):
            pre = before_silu(part, j, False)
            acts.append(pre * sigmoid(pre))
        queries.append(acts[0] * (unit_scale(acts[0]) * width ** (-0.5)))
        keys.append(acts[1] * unit_scale(acts[1]))
        errors.append(acts[2])
        strengths.append(pick(beta, group * heads + j))
        lanes = pl.ds(j * width, width)
        out = out_ref[:, lanes]
        freshes.append(fresh_ref[:, lanes])
        grad_mixed = grad_ref[rows, pl.ds(pl.multiple_of((group * heads + j) * width, width), width)]
        scale = lax.rsqrt(jnp.mean(out * out, -1, keepdims=True) + epsilon)
        normal = out * scale
        ggain = ggain + jnp.sum(grad_mixed * normal, 0, keepdims=True)
        scaled = grad_mixed * gain
        grad_outs.append(scale * (scaled - normal * jnp.mean(scaled * normal, -1, keepdims=True)))
    ggain_ref[...] += ggain

    scores = [jnp.where(row >= col, nt(queries[j], keys[j], passes), 0.0) for j in every]
    grad_freshes = [tn(scores[j], grad_outs[j], passes) + nn(keys[j], carry[j], passes) for j in every]
    pulled = [tn(solve_ref[j], grad_freshes[j], passes) for j in every]
    grad_errors = [strengths[j] * pulled[j] for j in every]
    grad_keys = [nt(freshes[j], carry[j], passes) - nt(grad_errors[j], state_ref[j], passes) for j in every]
    for j in every:
        carry[j] = carry[j] + (tn(queries[j], grad_outs[j], passes) - tn(keys[j], grad_errors[j], passes))
    grams = [nt(keys[j], keys[j], passes) for j in every]
    errors = [errors[j] - nn(keys[j], state_ref[j], passes) for j in every]
    grad_scores = [jnp.where(row >= col, nt(grad_outs[j], freshes[j], passes), 0.0) for j in every]
    grad_lowers = [jnp.where(row > col, -nt(pulled[j], freshes[j], passes), 0.0) for j in every]
    grad_queries = [nt(grad_outs[j], state_ref[j], passes) + nn(grad_scores[j], keys[j], passes) for j in every]
    grad_grams = [grad_lowers[j] * strengths[j] for j in every]
    grad_keys = [
        grad_keys[j] + tn(grad_scores[j], queries[j], passes) + nn(grad_grams[j] + grad_grams[j].T, keys[j], passes)
        for j in every
    ]
    gbeta = jnp.zeros(beta.shape, F32)
    for j in every:
        grad_strength = jnp.sum(pulled[j] * errors[j] + grad_lowers[j] * grams[j], -1, keepdims=True)
        grad_strength = grad_strength * (strengths[j] * (1.0 - strengths[j]))
        gbeta = jnp.where(lane == group * heads + j, grad_strength, gbeta)
    gbeta_ref[rows, :] += gbeta.astype(BF16)

    for j in every:
        for part in range(3):
            moved = before_silu(part, j, True)
            taps = conv_ref[:, wide_lanes(part, j)]
            pre = taps[3:4] * moved[0]
            for by in (1, 2, 3):
                pre = pre + taps[3 - by : 4 - by] * moved[by]
            gate = sigmoid(pre)
            act = pre * gate
            if part == 0:
                scale = unit_scale(act)
                unit = act * scale
                grad = grad_queries[j] * width ** (-0.5)
                grad = scale * (grad - unit * jnp.sum(grad * unit, -1, keepdims=True))
            elif part == 1:
                grad = grad_keys[j]
                unit = keys[j]
                grad = unit_scale(act) * (grad - unit * jnp.sum(grad * unit, -1, keepdims=True))
            else:
                grad = grad_errors[j]
            grad = grad * gate * (1.0 + pre * (1.0 - gate))
            after = ahead[:, lanes_of(part, j)]
            total = taps[3:4] * grad
            for by in (1, 2, 3):
                total = total + taps[3 - by : 4 - by] * shift_up(grad, after, by)
            raw_ref[rows, wide_lanes(part, j)] = total.astype(BF16)
            ahead[:, lanes_of(part, j)] = grad[:8]
            sums = [jnp.sum(grad * moved[3 - tap], 0, keepdims=True) for tap in range(4)]
            gconv_ref[:, wide_lanes(part, j)] += jnp.concatenate(sums, 0)


def radices(size):
    digits = []
    while size > 1:
        digits.append(2 if len(digits) < 2 else min(4, size))
        size //= digits[-1]
    return digits


def offsets(size):
    found, stride = [0], 1
    for digit in radices(size):
        found = [old + value * stride for old in found for value in range(digit)]
        stride *= digit
    return found


def flipped(index, bits, size):
    result, unit = 0, 1
    while unit < size:
        result = result + (index // unit + bits // unit) % 2 * unit
        unit *= 2
    return result


class Scatter:
    def __init__(self, size, me, count, tiles, tile, which, left_ref, right_ref, out_ref, refs):
        self.digits = radices(size)
        self.stages = stages = len(self.digits)
        self.size, self.me, self.count, self.tiles, self.tile, self.which = size, me, count, tiles, tile, which
        self.left_ref, self.right_ref, self.out_ref = left_ref, right_ref, out_ref
        self.landed, self.sent, self.early = refs[:stages], refs[stages : 2 * stages], refs[2 * stages : 3 * stages]
        self.send_sems, self.recv_sems = refs[3 * stages : 4 * stages], refs[4 * stages : 5 * stages]
        self.load_sem, self.staged, self.store_sem = refs[5 * stages : 5 * stages + 3]
        self.block = left_ref.shape[1] // size
        self.keeps, self.strides = kept_rows(size, self.block), strides_of(size)

    @staticmethod
    def scratch(size, block, count, wide):
        digits = radices(size)
        keeps = kept_rows(size, block)
        sends = [keep * (digit - 1) for keep, digit in zip(keeps, digits)]
        early = [sum(digit - 1 for digit in digits[: stage + 1]) for stage in range(len(digits))]
        landed = [jax.ShapeDtypeStruct((count, d - 1, keep, wide), BF16) for keep, d in zip(keeps, digits)]
        rest = (
            [pltpu.VMEM((2, rows, wide), BF16) for rows in sends]
            + [pltpu.VMEM((number, rows, wide), BF16) for number, rows in zip(early, sends[1:] + [block])]
            + [pltpu.SemaphoreType.DMA((2, digit - 1)) for digit in digits]
            + [pltpu.SemaphoreType.DMA((count, digit - 1)) for digit in digits]
            + [pltpu.SemaphoreType.DMA((early[-1],)), pltpu.VMEM((2, block, wide), F32), pltpu.SemaphoreType.DMA((2,))]
        )
        return landed, rest

    def remote(self, stage, value, chunk):
        rows = self.keeps[stage]
        return pltpu.make_async_remote_copy(
            src_ref=self.sent[stage].at[chunk % 2, pl.ds((value - 1) * rows, rows)],
            dst_ref=self.landed[stage].at[chunk, value - 1],
            send_sem=self.send_sems[stage].at[chunk % 2, value - 1],
            recv_sem=self.recv_sems[stage].at[chunk, value - 1],
            device_id={"dp": flipped(self.me, value * self.strides[stage], self.size)},
            device_id_type=MESH,
        )

    def load(self, stage, chunk, first, rows):
        if stage:
            for value in range(1, self.digits[stage - 1]):
                self.remote(stage - 1, value, chunk).wait_recv()
        copies = []
        for early in range(stage):
            for value in range(1, self.digits[early]):
                place = len(copies)
                copies.append(
                    pltpu.make_async_copy(
                        self.landed[early].at[chunk, value - 1, pl.ds(first, rows)],
                        self.early[stage - 1].at[place],
                        self.load_sem.at[place],
                    )
                )
        for copy in copies:
            copy.start()
        return copies

    def product(self, chunk, first, rows, extra, extras, store):
        tile = self.tile
        part = next(p for p in (512, 384, 256, 128, 96, 64, 32) if rows % p == 0)

        @pl.loop(0, self.tiles)
        def _(t):
            at = chunk * self.tiles + t
            right = self.right_ref[:, pl.ds(pl.multiple_of(at * tile, tile), tile)]
            inside = pl.ds(pl.multiple_of(t * tile, tile), tile)
            for begin in range(0, rows, part):
                left = self.left_ref[self.which(at), first + begin : first + begin + part, :]
                total = jnp.dot(left, right, preferred_element_type=F32)
                for place in range(extras):
                    total = total + extra[place, begin : begin + part, inside].astype(F32)
                store(begin, part, inside, total)

    def run_stage(self, stage, chunk):
        first = self.keeps[stage]
        rows = first * (self.digits[stage] - 1)
        copies = self.load(stage, chunk, first, rows)

        @pl.when(chunk >= 2)
        def _():
            for value in range(1, self.digits[stage]):
                self.remote(stage, value, chunk - 2).wait_send()

        for copy in copies:
            copy.wait()

        def store(begin, part, inside, total):
            self.sent[stage][chunk % 2, begin : begin + part, inside] = total.astype(BF16)

        self.product(chunk, first, rows, self.early[max(stage - 1, 0)], len(copies), store)
        for value in range(1, self.digits[stage]):
            self.remote(stage, value, chunk).start()

    def write(self, chunk):
        wide = self.tiles * self.tile
        return pltpu.make_async_copy(
            self.staged.at[chunk % 2],
            self.out_ref.at[:, pl.ds(pl.multiple_of(chunk * wide, LANES), wide)],
            self.store_sem.at[chunk % 2],
        )

    def run_last(self, chunk):
        copies = self.load(self.stages, chunk, 0, self.block)

        @pl.when(chunk >= 2)
        def _():
            self.write(chunk - 2).wait()

        for copy in copies:
            copy.wait()

        def store(begin, part, inside, total):
            self.staged[chunk % 2, begin : begin + part, inside] = total

        self.product(chunk, 0, self.block, self.early[self.stages - 1], len(copies), store)
        self.write(chunk).start()

    def step(self, i, lags):
        for stage, lag in enumerate(lags):

            @pl.when((i >= lag) & (i < self.count + lag))
            def _():
                if stage < self.stages:
                    self.run_stage(stage, i - lag)
                else:
                    self.run_last(i - lag)

    def drain(self):
        for chunk in range(max(self.count - 2, 0), self.count):
            for stage in range(self.stages):
                for value in range(1, self.digits[stage]):
                    self.remote(stage, value, chunk).wait_send()
            self.write(chunk).wait()


def strides_of(size):
    strides, stride = [], 1
    for digit in radices(size):
        strides.append(stride)
        stride *= digit
    return strides


def kept_rows(size, block):
    keeps, rest = [], size
    for digit in radices(size):
        rest //= digit
        keeps.append(rest * block)
    return keeps


class Streamed:
    def __init__(self, left_ref, left_at, depth, weight_ref, weight_at, own_ref, other_ref, recv_sems, shared):
        self.left_ref, self.left_at, self.depth = left_ref, left_at, depth
        self.weight_ref, self.weight_at = weight_ref, weight_at
        self.own_ref, self.other_ref, self.recv_sems = own_ref, other_ref, recv_sems
        self.slots, self.slot_sems, self.made, self.send_sems, self.own_sems = shared
        self.count = weight_ref.shape[0] // LANES

    def fetch(self, tile):
        return pltpu.make_async_copy(
            self.weight_ref.at[pl.ds(pl.multiple_of(tile * LANES, LANES), LANES), pl.ds(self.weight_at, self.depth)],
            self.slots.at[tile % 2, :, pl.ds(0, self.depth)],
            self.slot_sems.at[tile % 2],
        )

    def columns(self, ref, tile):
        return ref.at[:, pl.ds(pl.multiple_of(tile * LANES, LANES), LANES)]

    def keep(self, tile):
        return pltpu.make_async_copy(self.made.at[tile], self.columns(self.own_ref, tile), self.own_sems.at[tile])

    def send(self, tile):
        return pltpu.make_async_remote_copy(
            src_ref=self.made.at[tile],
            dst_ref=self.columns(self.other_ref, tile),
            send_sem=self.send_sems.at[tile],
            recv_sem=self.recv_sems.at[tile],
            device_id={"tensor": 1 - lax.axis_index("tensor")},
            device_id_type=MESH,
        )

    def run(self, first, number):
        @pl.when(first == 0)
        def _():
            self.fetch(0).start()

        @pl.loop(0, number)
        def _(k):
            tile = first + k
            self.fetch(tile).wait()

            @pl.when(tile + 1 < self.count)
            def _():
                self.fetch(tile + 1).start()

            left = self.left_ref[:, pl.ds(self.left_at, self.depth)]
            weights = self.slots[tile % 2, :, pl.ds(0, self.depth)]
            self.made[tile] = lax.dot_general(
                left, weights, (((1,), (1,)), ((), ())), preferred_element_type=F32
            ).astype(BF16)
            self.keep(tile).start()
            self.send(tile).start()

    def sent(self):
        @pl.loop(0, self.count)
        def _(tile):
            self.keep(tile).wait()
            self.send(tile).wait_send()

    def received(self):
        @pl.loop(0, self.count)
        def _(tile):
            self.send(tile).wait_recv()


def backward_kernel(plan, *refs):
    size, heads, block_heads, units, passes, shapes = plan
    (up_t, second_t, first_t, ffn_right, mixed_hbm, conv_ref, gain_ref, norm_ref, w_mixer, w_ffn, qkv_hbm, out_hbm,
     fresh_hbm, state_hbm, solve_hbm, middle_hbm, upstream_hbm) = refs[:17]
    (ffn_out, mix_out, gmiddle_hbm, gs_own, gs_other, final_own, final_other, gf_own, gf_other,
     gconv_ref, ggain_ref, gnorm_ref) = refs[17:29]
    digits = radices(size)
    stages = len(digits)
    landed_ffn, landed_mix = refs[29 : 29 + stages], refs[29 + stages : 29 + 2 * stages]
    rest = list(refs[29 + 2 * stages :])
    take = lambda number: [rest.pop(0) for _ in range(number)]
    ffn_refs = list(landed_ffn) + take(4 * stages + 3)
    mix_refs = list(landed_mix) + take(4 * stages + 3)
    (lefts, mix_right, slots, slot_sems, made, send_sems, own_sems, recv_sems, w_out, grad_mixed, gm_t, carry, ahead,
     place_sems, misc_sems, tile_sems) = rest
    length = ffn_right.shape[0]
    model = up_t.shape[0]
    block = model // size
    span = 3 * block_heads * WIDTH
    groups = heads // block_heads
    columns = heads * WIDTH
    raw_columns = groups * span + LANES
    count = length // CHUNK
    me = lax.axis_index("dp")
    strides = strides_of(size)

    barrier = pltpu.get_barrier_semaphore()
    peers = 1
    pl.semaphore_signal(barrier, inc=1, device_id={"tensor": 1 - lax.axis_index("tensor")}, device_id_type=MESH)
    for stage, digit in enumerate(digits):
        for value in range(1, digit):
            pl.semaphore_signal(
                barrier, inc=1, device_id={"dp": flipped(me, value * strides[stage], size)}, device_id_type=MESH
            )
            peers += 1

    places = []
    for which, source in enumerate((up_t, second_t, first_t)):
        for place, bits in enumerate(offsets(size)):
            owner = pl.multiple_of(flipped(me, bits, size) * block, block)
            places.append(
                pltpu.make_async_copy(
                    source.at[pl.ds(owner, block)],
                    lefts.at[which, pl.ds(place * block, block)],
                    place_sems.at[which, place],
                )
            )
    for copy in places:
        copy.start()
    bring_mixed = pltpu.make_async_copy(mixed_hbm, mix_right.at[:, pl.ds(raw_columns, columns)], misc_sems.at[0])
    bring_mixed.start()
    bring_w_out = pltpu.make_async_copy(
        w_mixer.at[:, pl.ds(raw_columns, columns)], w_out, misc_sems.at[1]
    )
    bring_w_out.start()
    gconv_ref[...] = jnp.zeros_like(gconv_ref)
    ggain_ref[...] = jnp.zeros_like(ggain_ref)
    gnorm_ref[...] = jnp.zeros_like(gnorm_ref)
    strength_lanes = pl.ds(groups * span, LANES)
    mix_right[:, strength_lanes] = jnp.zeros((length, LANES), BF16)
    pl.semaphore_wait(barrier, peers)
    for copy in places:
        copy.wait()

    (ffn_count, ffn_tiles, ffn_tile), (mix_count, mix_tiles, mix_tile) = shapes
    per_matrix = units // ffn_tile
    ffn = Scatter(size, me, ffn_count, ffn_tiles, ffn_tile, lambda at: (at // per_matrix + 1) // 2, lefts, ffn_right,
                  ffn_out, ffn_refs)
    raw_tiles = raw_columns // mix_tile
    mix = Scatter(size, me, mix_count, mix_tiles, mix_tile, lambda at: 2 + at // raw_tiles, lefts, mix_right,
                  mix_out, mix_refs)
    shared = (slots, slot_sems, made, send_sems, own_sems)
    gs = Streamed(ffn_right, units, 2 * units, w_ffn, units, gs_own, gs_other, recv_sems.at[0], shared)
    final = Streamed(ffn_right, 0, units, w_ffn, 0, final_own, final_other, recv_sems.at[1], shared)
    gf = Streamed(mix_right, 0, raw_columns, w_mixer, 0, gf_own, gf_other, recv_sems.at[2], shared)

    def middle_part():
        gs.received()

        def scoped(own, other, middle, upstream, result, low):
            def fetches(t):
                rows = pl.ds(pl.multiple_of(t * CHUNK, CHUNK), CHUNK)
                return [
                    pltpu.make_async_copy(source.at[rows], target, tile_sems.at[k])
                    for k, (source, target) in enumerate(
                        ((gs_own, own), (gs_other, other), (middle_hbm, middle), (upstream_hbm, upstream))
                    )
                ]

            @pl.loop(0, count)
            def _(t):
                rows = pl.ds(pl.multiple_of(t * CHUNK, CHUNK), CHUNK)
                for copy in fetches(t):
                    copy.start()
                for copy in fetches(t):
                    copy.wait()

                @pl.loop(0, CHUNK // 16)
                def _(k):
                    here = pl.ds(pl.multiple_of(k * 16, 16), 16)
                    grad = own[here].astype(F32) + other[here].astype(F32)
                    values = middle[here]
                    scale = lax.rsqrt(jnp.mean(values * values, -1, keepdims=True) + epsilon)
                    normal = values * scale
                    scaled = grad * norm_ref[...]
                    gnorm_ref[...] += jnp.sum(grad * normal, 0, keepdims=True)
                    total = upstream[here].astype(F32) + scale * (
                        scaled - normal * jnp.mean(scaled * normal, -1, keepdims=True)
                    )
                    result[here] = total
                    low[here] = total.astype(BF16)

                write = pltpu.make_async_copy(result, gmiddle_hbm.at[rows], tile_sems.at[4])
                write.start()
                grad_mixed[rows] = jnp.dot(low[...], w_out[...], preferred_element_type=F32)

                @pl.loop(0, model // LANES)
                def _(k):
                    lanes = pl.ds(pl.multiple_of(k * LANES, LANES), LANES)
                    gm_t[lanes, rows] = result[:, lanes].T.astype(BF16)

                write.wait()

        pl.run_scoped(
            scoped,
            pltpu.VMEM((CHUNK, model), BF16),
            pltpu.VMEM((CHUNK, model), BF16),
            pltpu.VMEM((CHUNK, model), F32),
            pltpu.VMEM((CHUNK, model), BF16),
            pltpu.VMEM((CHUNK, model), F32),
            pltpu.VMEM((CHUNK, model), BF16),
        )
        for place, bits in enumerate(offsets(size)):
            owner = pl.multiple_of(flipped(me, bits, size) * block, block)
            lefts[3, place * block : (place + 1) * block] = gm_t[pl.ds(owner, block)]

    def delta_part(piece):
        group = piece // count
        c = count - 1 - piece % count

        def scoped(cur, tail, beta, out, fresh, state, solve):
            rows = pl.ds(pl.multiple_of(c * CHUNK, CHUNK), CHUNK)
            before = pl.ds(pl.multiple_of((c * CHUNK + length - 8) % length // 8 * 8, 8), 8)
            lanes = pl.ds(pl.multiple_of(group * span, LANES), span)
            narrow = pl.ds(pl.multiple_of(group * block_heads * WIDTH, LANES), block_heads * WIDTH)
            ours = pl.ds(group * block_heads, block_heads)
            copies = [
                pltpu.make_async_copy(source, target, tile_sems.at[k])
                for k, (source, target) in enumerate(
                    (
                        (qkv_hbm.at[rows, lanes], cur),
                        (qkv_hbm.at[before, lanes], tail),
                        (qkv_hbm.at[rows, strength_lanes], beta),
                        (out_hbm.at[rows, narrow], out),
                        (fresh_hbm.at[rows, narrow], fresh),
                        (state_hbm.at[ours, c], state),
                        (solve_hbm.at[ours, c], solve),
                    )
                )
            ]
            for copy in copies:
                copy.start()

            @pl.when(piece % count == 0)
            def _():
                carry[...] = jnp.zeros_like(carry)
                ahead[...] = jnp.zeros_like(ahead)

            for copy in copies:
                copy.wait()
            backward_piece(
                block_heads, WIDTH, passes, group, c, cur, tail, beta, conv_ref, gain_ref, grad_mixed, out, fresh,
                state, solve, mix_right, mix_right.at[:, strength_lanes], gconv_ref, ggain_ref, carry, ahead,
            )

        pl.run_scoped(
            scoped,
            pltpu.VMEM((CHUNK, span), F32),
            pltpu.VMEM((8, span), F32),
            pltpu.VMEM((CHUNK, LANES), F32),
            pltpu.VMEM((CHUNK, block_heads * WIDTH), F32),
            pltpu.VMEM((CHUNK, block_heads * WIDTH), F32),
            pltpu.VMEM((block_heads, WIDTH, WIDTH), F32),
            pltpu.VMEM((block_heads, CHUNK, CHUNK), F32),
        )

    tail_lags = [3 + 2 * stage for stage in range(stages - 1)]
    lags = ([0, 1] + tail_lags)[: stages + 1]
    quarter = gs.count // 4
    at_final, at_middle, at_delta = 4, 8, 9
    pieces = groups * count
    at_gf = at_delta + -(-pieces // 2)

    def step(i, carried):
        ffn.step(i, lags)
        mix.step(i - ffn_count - 1, lags)

        @pl.when(i < 4)
        def _():
            gs.run(i * quarter, quarter)

        @pl.when(i == at_final)
        def _():
            gs.sent()

        @pl.when((i >= at_final) & (i < at_final + 4))
        def _():
            final.run((i - at_final) * quarter, quarter)

        @pl.when(i == at_middle)
        def _():
            bring_w_out.wait()
            bring_mixed.wait()
            middle_part()

        @pl.when((i >= at_delta) & (i < at_gf))
        def _():
            @pl.loop(0, 2)
            def _(k):
                @pl.when((i - at_delta) * 2 + k < pieces)
                def _():
                    delta_part((i - at_delta) * 2 + k)

        @pl.when(i == at_gf)
        def _():
            final.sent()

        @pl.when((i >= at_gf) & (i < at_gf + 4))
        def _():
            gf.run((i - at_gf) * quarter, quarter)

        return carried

    lax.fori_loop(0, ffn_count + 1 + mix_count + lags[-1], step, 0)
    ffn.drain()
    mix.drain()
    gf.sent()
    final.received()
    gf.received()


def backward_all(size, heads, block_heads, up_t, second_t, first_t, ffn_right, mixed, conv, gain, norm_ffn, w_mixer,
                 w_ffn, qkv, out, fresh, state, solve, middle, upstream, passes=3):
    length = qkv.shape[0]
    model = up_t.shape[0]
    units = ffn_right.shape[1] // 3
    block = model // size
    groups = heads // block_heads
    span = 3 * block_heads * WIDTH
    columns = heads * WIDTH
    raw_columns = groups * span + LANES
    mix_columns = raw_columns + columns
    ffn_tile = 256 if units % 256 == 0 else 128
    shapes = []
    for total, tile in ((3 * units, ffn_tile), (mix_columns, 128)):
        tiles = next(t for t in (3, 2, 1) if total // tile % t == 0)
        shapes.append((total // tile // tiles, tiles, tile))
    landed, scratch = [], []
    for number, tiles, tile in shapes:
        more_landed, more_scratch = Scatter.scratch(size, block, number, tiles * tile)
        landed += more_landed
        scratch += more_scratch
    tiles = model // LANES
    scratch += [
        pltpu.VMEM((4, model, length), BF16),
        pltpu.VMEM((length, mix_columns), BF16),
        pltpu.VMEM((2, LANES, max(2 * units, raw_columns)), BF16),
        pltpu.SemaphoreType.DMA((2,)),
        pltpu.VMEM((tiles, length, LANES), BF16),
        pltpu.SemaphoreType.DMA((tiles,)),
        pltpu.SemaphoreType.DMA((tiles,)),
        pltpu.SemaphoreType.DMA((3, tiles)),
        pltpu.VMEM((model, columns), BF16),
        pltpu.VMEM((length, columns), F32),
        pltpu.VMEM((model, length), BF16),
        pltpu.VMEM((block_heads, WIDTH, WIDTH), F32),
        pltpu.VMEM((8, span), F32),
        pltpu.SemaphoreType.DMA((3, size)),
        pltpu.SemaphoreType.DMA((2,)),
        pltpu.SemaphoreType.DMA((7,)),
    ]
    vmem, hbm = pl.BlockSpec(memory_space=pltpu.VMEM), pl.BlockSpec(memory_space=pl.ANY)
    shape = jax.ShapeDtypeStruct
    exchanged = [shape((length, model), BF16)] * 6
    return pl.pallas_call(
        functools.partial(backward_kernel, (size, heads, block_heads, units, passes, shapes)),
        in_specs=[hbm] * 3 + [vmem, hbm] + [vmem] * 3 + [hbm] * 9,
        out_specs=[hbm] * 9 + [vmem] * 3 + [hbm] * len(landed),
        out_shape=[shape((block, 3 * units), F32), shape((block, mix_columns), F32), shape((length, model), F32)]
        + exchanged
        + [shape((4, groups * span), F32), shape((1, WIDTH), F32), shape((1, model), F32)]
        + landed,
        scratch_shapes=scratch,
        compiler_params=pltpu.CompilerParams(
            collective_id=0, has_side_effects=True, vmem_limit_bytes=62 * 2**20
        ),
        name="backward_all",
    )(up_t, second_t, first_t, ffn_right, mixed, conv, gain, norm_ffn, w_mixer, w_ffn, qkv, out, fresh, state, solve,
      middle, upstream)[:12]


def matmul(left, right):
    return jnp.dot(left, right, preferred_element_type=F32)


def right_inner(left, right):
    return lax.dot_general(left, right, (((1,), (1,)), ((), ())), preferred_element_type=F32)


def row_norm(values, gain):
    return values * lax.rsqrt(jnp.mean(values * values, -1, keepdims=True) + epsilon) * gain


def norm_back(values, gain, grad):
    scale = lax.rsqrt(jnp.mean(values * values, -1, keepdims=True) + epsilon)
    normal = values * scale
    scaled = grad * gain
    grad_gain = jnp.sum(grad * normal, 0)
    grad_values = scale * (scaled - normal * jnp.mean(scaled * normal, -1, keepdims=True))
    return (grad_values, grad_gain)


def swap(values, axis, size, by):
    return lax.ppermute(values, axis, [(d, d ^ by) for d in range(size)])


def exchange(partial):
    own = lax.reduce_precision(partial, 8, 7)
    return own, swap(own.astype(BF16), "tensor", 2, 1)


def add_all(values, size):
    for digit, stride in zip(radices(size), strides_of(size)):
        if digit == 2:
            values = values + swap(values, "dp", size, stride)
        else:
            others = [swap(values, "dp", size, value * stride) for value in range(1, digit)]
            values = (values + others[0]) + (others[1] + others[2])
    return values


def by_groups(parts, block):
    span = block * WIDTH
    return [part[:, g * span : (g + 1) * span] for g in range(parts[0].shape[1] // span) for part in parts]


def from_groups(whole, block, index, columns):
    span = block * WIDTH
    return jnp.concatenate(
        [whole[:, (3 * g + index) * span : (3 * g + index + 1) * span] for g in range(columns // span)], 1
    )


def body(size, tokens, lengths, w_query, w_key, w_value, w_beta, conv_query, conv_key, conv_value, head_gain,
         w_out, norm_attn, norm_ffn, w_gate, w_up, w_down, cotangent):
    inputs = tokens.astype(F32)
    length, model = inputs.shape
    columns = w_query.shape[1]
    units = w_gate.shape[1]
    heads = w_beta.shape[1]
    block = 4 if heads % 4 == 0 else 1
    raw_columns = 3 * columns + LANES
    strengths = jnp.pad(w_beta.astype(BF16), ((0, 0), (0, LANES - heads)))
    low = [w.astype(BF16) for w in (w_query, w_key, w_value)]
    w_mixer = lax.all_gather(
        jnp.concatenate(by_groups(low, block) + [strengths, w_out.astype(BF16).T], 1), "dp", axis=0, tiled=True
    )
    w_ffn = lax.all_gather(
        jnp.concatenate([w_down.astype(BF16).T, w_gate.astype(BF16), w_up.astype(BF16)], 1), "dp", axis=0, tiled=True
    )
    conv = jnp.concatenate(by_groups([conv_query, conv_key, conv_value], block), 1)
    gain = head_gain[None]

    first = row_norm(inputs, norm_attn).astype(BF16)
    qkv = matmul(first, w_mixer[:, :raw_columns])
    mixed, out, fresh, state, solve = delta_forward(qkv, conv, gain, heads, block, (3, 3, 3, 3))
    own, other = exchange(right_inner(mixed, w_mixer[:, raw_columns:]))
    middle = inputs + (own + other.astype(F32))
    second = row_norm(middle, norm_ffn).astype(BF16)
    positions = lax.broadcasted_iota(jnp.int32, (length, 1), 0)
    valid = (positions < lengths[0]).astype(F32)
    upstream = (cotangent.astype(F32) * valid).astype(BF16)
    grad_hidden = matmul(upstream, w_ffn[:, :units])
    gate_up = matmul(second, w_ffn[:, units:])
    gate, up_proj = gate_up[:, :units], gate_up[:, units:]
    sigma = jax.nn.sigmoid(gate)
    activated = gate * sigma
    hidden = (activated * up_proj).astype(BF16)
    grad_gate_act = (grad_hidden * up_proj * sigma * (1.0 + gate * (1.0 - sigma))).astype(BF16)
    grad_up_act = (grad_hidden * activated).astype(BF16)

    (ffn_grads, mixer_grads, grad_middle, _, _, final_own, final_other, first_own, first_other, grad_conv, grad_gain,
     grad_norm_ffn) = backward_all(
        size, heads, block, upstream.T, second.T, first.T,
        jnp.concatenate([hidden, grad_gate_act, grad_up_act], 1),
        mixed, conv, gain, norm_ffn[None], w_mixer, w_ffn, qkv, out, fresh, state, solve, middle, upstream,
    )
    final = middle + (final_own.astype(F32) + final_other.astype(F32))
    block_out = (final * valid).astype(BF16)
    grad_inputs_norm, grad_norm_attn = norm_back(
        inputs, norm_attn, first_own.astype(F32) + first_other.astype(F32)
    )
    grad_tokens = grad_middle + grad_inputs_norm
    grad_gain = grad_gain + swap(grad_gain, "tensor", 2, 1)
    small = jnp.concatenate([grad_conv.reshape(-1), grad_gain[0], grad_norm_ffn[0], grad_norm_attn])
    small = add_all(small.reshape(-1, LANES), size).reshape(-1)
    taps = 4 * 3 * columns
    convs = small[:taps].reshape(4, 3 * columns)
    small = small[taps:]
    return (
        block_out,
        grad_tokens,
        from_groups(mixer_grads, block, 0, columns),
        from_groups(mixer_grads, block, 1, columns),
        from_groups(mixer_grads, block, 2, columns),
        mixer_grads[:, 3 * columns : 3 * columns + heads],
        from_groups(convs, block, 0, columns),
        from_groups(convs, block, 1, columns),
        from_groups(convs, block, 2, columns),
        small[:WIDTH],
        mixer_grads[:, raw_columns:].T,
        small[WIDTH + model :],
        small[WIDTH : WIDTH + model],
        ffn_grads[:, units : 2 * units],
        ffn_grads[:, 2 * units :],
        ffn_grads[:, :units].T,
    )


def solution(mesh):
    rows, both, cols = P("dp", None), P("dp", "tensor"), P("tensor", "dp")
    taps = P(None, "tensor")
    in_specs = (rows, P("dp"), both, both, both, both, taps, taps, taps, P(), cols, P(), P(), both, both, cols, rows)
    out_specs = (rows, rows, both, both, both, both, taps, taps, taps, P(), cols, P(), P(), both, both, cols)
    return jax.shard_map(
        functools.partial(body, mesh.shape["dp"]), mesh=mesh, in_specs=in_specs, out_specs=out_specs, check_vma=False
    )
```

```python
import functools
import jax
import jax.numpy as jnp
from jax import lax
from jax.experimental import pallas as pl
from jax.experimental.pallas import tpu as pltpu
from jax.sharding import PartitionSpec as P

CHUNK = 128
WIDTH = 128
LANES = 128
epsilon = 1e-06
HIGH = lax.Precision.HIGHEST
F32 = jnp.float32
BF16 = jnp.bfloat16
MESH = pl.DeviceIdType.MESH


def dot(left, right, dims, passes):
    form = (dims, ((), ()))
    if passes == 6:
        return lax.dot_general(left, right, form, precision=HIGH, preferred_element_type=F32)
    left_hi, right_hi = left.astype(BF16), right.astype(BF16)
    total = lax.dot_general(left_hi, right_hi, form, preferred_element_type=F32)
    if passes == 3:
        left_lo = (left - left_hi.astype(F32)).astype(BF16)
        right_lo = (right - right_hi.astype(F32)).astype(BF16)
        total = total + (
            lax.dot_general(left_hi, right_lo, form, preferred_element_type=F32)
            + lax.dot_general(left_lo, right_hi, form, preferred_element_type=F32)
        )
    return total


def nn(left, right, passes):
    return dot(left, right, ((1,), (0,)), passes)


def nt(left, right, passes):
    return dot(left, right, ((1,), (1,)), passes)


def tn(left, right, passes):
    return dot(left, right, ((0,), (0,)), passes)


def sigmoid(x):
    return 1.0 / (1.0 + jnp.exp(-x))


def shift_down(cur, tail, by):
    rolled = pltpu.roll(cur, by, 0)
    rows = lax.broadcasted_iota(jnp.int32, tail.shape, 0)
    top = jnp.where(rows < by, pltpu.roll(tail, by, 0), rolled[:8])
    return jnp.concatenate([top, rolled[8:]], 0)


def shift_up(cur, head, by):
    size = cur.shape[0]
    rolled = pltpu.roll(cur, size - by, 0)
    rows = lax.broadcasted_iota(jnp.int32, head.shape, 0)
    bottom = jnp.where(rows >= 8 - by, pltpu.roll(head, 8 - by, 0), rolled[size - 8 :])
    return jnp.concatenate([rolled[: size - 8], bottom], 0)


def unit_scale(values):
    return lax.rsqrt(jnp.sum(values * values, -1, keepdims=True) + epsilon)


def masks(size):
    rows = lax.broadcasted_iota(jnp.int32, (size, size), 0)
    cols = lax.broadcasted_iota(jnp.int32, (size, size), 1)
    return rows, cols, rows ^ cols


def unit_lower_inverses(lowers, passes):
    size = lowers[0].shape[0]
    rows, cols, apart = masks(size)
    inverses = [jnp.where(rows == cols, 1.0, jnp.where(apart < 2, -lower, 0.0)) for lower in lowers]
    span = 2
    while span < size:
        corner = (apart < 2 * span) & (apart >= span)
        halves = [nn(jnp.where(corner, a, 0.0), x, passes) for a, x in zip(lowers, inverses)]
        inverses = [x - nn(x, half, passes) for x, half in zip(inverses, halves)]
        span *= 2
    return inverses


def pick(table, column):
    lanes = lax.broadcasted_iota(jnp.int32, table.shape, 1)
    return jnp.sum(jnp.where(lanes == column, table, 0.0), 1, keepdims=True)


def forward_kernel(heads, width, ps, qkv_ref, beta_ref, conv_ref, gain_ref,
                   mixed_ref, out_ref, fresh_ref, state_ref, solve_ref, carry):
    group = pl.program_id(0)
    chunk = CHUNK
    length = qkv_ref.shape[0]
    carry[...] = jnp.zeros_like(carry)
    p_gram, p_inv, p_state, p_out = ps

    def step(c, _):
        base = pl.multiple_of(c * chunk, chunk)
        rows = pl.ds(base, chunk)
        before = pl.ds(pl.multiple_of(jnp.maximum(base - 8, 0), 8), 8)
        beta = sigmoid(beta_ref[rows, :])
        row, col, _ = masks(chunk)
        gain = gain_ref[...]
        queries, keys, values, strengths = [], [], [], []
        for j in range(heads):
            parts = []
            for part in range(3):
                lanes = pl.ds((part * heads + j) * width, width)
                cur = qkv_ref[rows, lanes]
                tail = jnp.where(c > 0, qkv_ref[before, lanes], 0.0)
                taps = conv_ref[:, lanes]
                total = taps[3:4] * cur
                for by in (1, 2, 3):
                    total = total + taps[3 - by : 4 - by] * shift_down(cur, tail, by)
                parts.append(total * sigmoid(total))
            query, key, value = parts
            queries.append(query * (unit_scale(query) * width ** (-0.5)))
            keys.append(key * unit_scale(key))
            values.append(value)
            strengths.append(pick(beta, group * heads + j))
        grams = [nt(key, key, p_gram) for key in keys]
        solves = unit_lower_inverses(
            [jnp.where(row > col, gram * strength, 0.0) for gram, strength in zip(grams, strengths)], p_inv
        )
        states = [carry[j] for j in range(heads)]
        errors = [value - nn(key, state, p_state) for value, key, state in zip(values, keys, states)]
        freshes = [nn(solve, s * e, p_state) for solve, s, e in zip(solves, strengths, errors)]
        for j in range(heads):
            carry[j] = states[j] + tn(keys[j], freshes[j], p_state)
        scores = [jnp.where(row >= col, nt(q, k, p_out), 0.0) for q, k in zip(queries, keys)]
        outs = [
            nn(q, s, p_out) + nn(score, f, p_out) for q, s, score, f in zip(queries, states, scores, freshes)
        ]
        for j, out in enumerate(outs):
            state_ref[j, c] = states[j]
            solve_ref[j, c] = solves[j]
            lanes = pl.ds(j * width, width)
            fresh_ref[rows, lanes] = freshes[j]
            out_ref[rows, lanes] = out
            scale = lax.rsqrt(jnp.mean(out * out, -1, keepdims=True) + epsilon)
            mixed_ref[rows, lanes] = (out * scale * gain).astype(BF16)
        return 0

    lax.fori_loop(0, length // chunk, step, 0)


def delta_forward(qkv, conv, gain, heads, block, ps=(6, 6, 6, 6)):
    length = qkv.shape[0]
    width = gain.shape[1]
    groups = heads // block
    span = 3 * block * width
    last = groups * span // 128
    count = length // CHUNK
    return pl.pallas_call(
        functools.partial(forward_kernel, block, width, ps),
        grid=(groups,),
        in_specs=[
            pl.BlockSpec((length, span), lambda g: (0, g)),
            pl.BlockSpec((length, 128), lambda g: (0, last)),
            pl.BlockSpec((4, span), lambda g: (0, g)),
            pl.BlockSpec((1, width), lambda g: (0, 0)),
        ],
        out_specs=[
            pl.BlockSpec((length, block * width), lambda g: (0, g)),
            pl.BlockSpec((length, block * width), lambda g: (0, g)),
            pl.BlockSpec((length, block * width), lambda g: (0, g)),
            pl.BlockSpec((block, count, width, width), lambda g: (g, 0, 0, 0)),
            pl.BlockSpec((block, count, CHUNK, CHUNK), lambda g: (g, 0, 0, 0)),
        ],
        out_shape=[
            jax.ShapeDtypeStruct((length, heads * width), BF16),
            jax.ShapeDtypeStruct((length, heads * width), F32),
            jax.ShapeDtypeStruct((length, heads * width), F32),
            jax.ShapeDtypeStruct((heads, count, width, width), F32),
            jax.ShapeDtypeStruct((heads, count, CHUNK, CHUNK), F32),
        ],
        scratch_shapes=[pltpu.VMEM((block, width, width), F32)],
        compiler_params=pltpu.CompilerParams(vmem_limit_bytes=48 * 2**20),
        name="delta_forward",
    )(qkv, qkv, conv, gain)


def backward_piece(heads, width, passes, group, c, cur_ref, tail_ref, beta_ref, conv_ref, gain_ref, grad_ref, out_ref,
                   fresh_ref, state_ref, solve_ref, raw_ref, gbeta_ref, gconv_ref, ggain_ref, carry, ahead):
    chunk = CHUNK
    span = 3 * heads * width
    rows = pl.ds(pl.multiple_of(c * chunk, chunk), chunk)
    beta = sigmoid(beta_ref[...])
    row, col, _ = masks(chunk)
    gain = gain_ref[...]
    lane = lax.broadcasted_iota(jnp.int32, beta.shape, 1)
    every = range(heads)

    def lanes_of(part, j):
        return pl.ds((part * heads + j) * width, width)

    def wide_lanes(part, j):
        return pl.ds(pl.multiple_of(group * span + (part * heads + j) * width, width), width)

    def before_silu(part, j, keep):
        cur = cur_ref[:, lanes_of(part, j)]
        tail = jnp.where(c > 0, tail_ref[:, lanes_of(part, j)], 0.0)
        taps = conv_ref[:, wide_lanes(part, j)]
        moved = [cur] + [shift_down(cur, tail, by) for by in (1, 2, 3)]
        total = taps[3:4] * cur
        for by in (1, 2, 3):
            total = total + taps[3 - by : 4 - by] * moved[by]
        return moved if keep else total

    queries, keys, errors, strengths, grad_outs, freshes = [], [], [], [], [], []
    ggain = jnp.zeros_like(gain)
    for j in every:
        acts = []
        for part in range(3):
            pre = before_silu(part, j, False)
            acts.append(pre * sigmoid(pre))
        queries.append(acts[0] * (unit_scale(acts[0]) * width ** (-0.5)))
        keys.append(acts[1] * unit_scale(acts[1]))
        errors.append(acts[2])
        strengths.append(pick(beta, group * heads + j))
        lanes = pl.ds(j * width, width)
        out = out_ref[:, lanes]
        freshes.append(fresh_ref[:, lanes])
        grad_mixed = grad_ref[rows, pl.ds(pl.multiple_of((group * heads + j) * width, width), width)]
        scale = lax.rsqrt(jnp.mean(out * out, -1, keepdims=True) + epsilon)
        normal = out * scale
        ggain = ggain + jnp.sum(grad_mixed * normal, 0, keepdims=True)
        scaled = grad_mixed * gain
        grad_outs.append(scale * (scaled - normal * jnp.mean(scaled * normal, -1, keepdims=True)))
    ggain_ref[...] += ggain

    scores = [jnp.where(row >= col, nt(queries[j], keys[j], passes), 0.0) for j in every]
    grad_freshes = [tn(scores[j], grad_outs[j], passes) + nn(keys[j], carry[j], passes) for j in every]
    pulled = [tn(solve_ref[j], grad_freshes[j], passes) for j in every]
    grad_errors = [strengths[j] * pulled[j] for j in every]
    grad_keys = [nt(freshes[j], carry[j], passes) - nt(grad_errors[j], state_ref[j], passes) for j in every]
    for j in every:
        carry[j] = carry[j] + (tn(queries[j], grad_outs[j], passes) - tn(keys[j], grad_errors[j], passes))
    grams = [nt(keys[j], keys[j], passes) for j in every]
    errors = [errors[j] - nn(keys[j], state_ref[j], passes) for j in every]
    grad_scores = [jnp.where(row >= col, nt(grad_outs[j], freshes[j], passes), 0.0) for j in every]
    grad_lowers = [jnp.where(row > col, -nt(pulled[j], freshes[j], passes), 0.0) for j in every]
    grad_queries = [nt(grad_outs[j], state_ref[j], passes) + nn(grad_scores[j], keys[j], passes) for j in every]
    grad_grams = [grad_lowers[j] * strengths[j] for j in every]
    grad_keys = [
        grad_keys[j] + tn(grad_scores[j], queries[j], passes) + nn(grad_grams[j] + grad_grams[j].T, keys[j], passes)
        for j in every
    ]
    gbeta = jnp.zeros(beta.shape, F32)
    for j in every:
        grad_strength = jnp.sum(pulled[j] * errors[j] + grad_lowers[j] * grams[j], -1, keepdims=True)
        grad_strength = grad_strength * (strengths[j] * (1.0 - strengths[j]))
        gbeta = jnp.where(lane == group * heads + j, grad_strength, gbeta)
    gbeta_ref[rows, :] += gbeta.astype(BF16)

    for j in every:
        for part in range(3):
            moved = before_silu(part, j, True)
            taps = conv_ref[:, wide_lanes(part, j)]
            pre = taps[3:4] * moved[0]
            for by in (1, 2, 3):
                pre = pre + taps[3 - by : 4 - by] * moved[by]
            gate = sigmoid(pre)
            act = pre * gate
            if part == 0:
                scale = unit_scale(act)
                unit = act * scale
                grad = grad_queries[j] * width ** (-0.5)
                grad = scale * (grad - unit * jnp.sum(grad * unit, -1, keepdims=True))
            elif part == 1:
                grad = grad_keys[j]
                unit = keys[j]
                grad = unit_scale(act) * (grad - unit * jnp.sum(grad * unit, -1, keepdims=True))
            else:
                grad = grad_errors[j]
            grad = grad * gate * (1.0 + pre * (1.0 - gate))
            after = ahead[:, lanes_of(part, j)]
            total = taps[3:4] * grad
            for by in (1, 2, 3):
                total = total + taps[3 - by : 4 - by] * shift_up(grad, after, by)
            raw_ref[rows, wide_lanes(part, j)] = total.astype(BF16)
            ahead[:, lanes_of(part, j)] = grad[:8]
            sums = [jnp.sum(grad * moved[3 - tap], 0, keepdims=True) for tap in range(4)]
            gconv_ref[:, wide_lanes(part, j)] += jnp.concatenate(sums, 0)


def orders(size):
    bits, unit = [], 1
    while unit < size:
        bits.append(unit)
        unit *= 2
    return bits, bits[:1] + bits[2:] + bits[1:2]


def offsets(size):
    found = [0]
    for bit in orders(size)[0]:
        found = [old + value for old in found for value in (0, bit)]
    return found


def flipped(index, bits, size):
    result, unit = 0, 1
    while unit < size:
        result = result + (index // unit + bits // unit) % 2 * unit
        unit *= 2
    return result


def sent_places(size):
    owners = offsets(size)
    tables = []
    for order in orders(size):
        held, table = list(range(size)), []
        for bit in order:
            table.append([place for place in held if owners[place] & bit])
            held = [place for place in held if not owners[place] & bit]
        tables.append(table)
    stages = []
    for both in zip(*tables):
        length = len(both[0])
        while not all(
            places[at : at + length] == list(range(places[at], places[at] + length))
            for places in both
            for at in range(0, len(places), length)
        ):
            length //= 2
        stages.append((length, [places[::length] for places in both]))
    return stages, tables


def slots_of(stage):
    return 3 if stage else 2


class Scatter:
    def __init__(self, size, me, count, tiles, tile, which, left_ref, right_of, out_ref, refs):
        self.orders = orders(size)
        self.stages = stages = len(self.orders[0])
        self.runs, self.tables = sent_places(size)
        self.owners = offsets(size)
        self.size, self.me, self.count, self.tiles, self.tile, self.which = size, me, count, tiles, tile, which
        self.left_ref, self.right_of, self.out_ref = left_ref, right_of, out_ref
        self.landed, self.sent, self.early = refs[:stages], refs[stages : 2 * stages], refs[2 * stages : 3 * stages]
        self.send_sems, self.recv_sems, self.load_sems, self.staged, self.store_sem = refs[3 * stages : 3 * stages + 5]
        self.block = left_ref.shape[1] // size

    @staticmethod
    def scratch(size, block, count, wide):
        stages = len(orders(size)[0])
        sends = [(size >> (stage + 1)) * block for stage in range(stages)]
        landed = [jax.ShapeDtypeStruct((count, rows, wide), BF16) for rows in sends]
        rest = (
            [pltpu.VMEM((slots_of(stage), rows, wide), BF16) for stage, rows in enumerate(sends)]
            + [pltpu.VMEM((stage + 1, rows, wide), BF16) for stage, rows in enumerate(sends[1:] + [block])]
            + [
                pltpu.SemaphoreType.DMA((slots_of(1), stages)),
                pltpu.SemaphoreType.DMA((count, stages)),
                pltpu.SemaphoreType.DMA((stages, 2 * stages)),
                pltpu.VMEM((2, block, wide), F32),
                pltpu.SemaphoreType.DMA((2,)),
            ]
        )
        return landed, rest

    @staticmethod
    def other_order(chunk):
        return (chunk + 3) % 6 // 5

    def chosen(self, chunk, pair):
        first, second = pair
        return first if first == second else first + self.other_order(chunk) * (second - first)

    def remote(self, stage, chunk):
        bit = self.chosen(chunk, [order[stage] for order in self.orders])
        return pltpu.make_async_remote_copy(
            src_ref=self.sent[stage].at[chunk % slots_of(stage)],
            dst_ref=self.landed[stage].at[chunk],
            send_sem=self.send_sems.at[chunk % slots_of(stage), stage],
            recv_sem=self.recv_sems.at[chunk, stage],
            device_id={"dp": flipped(self.me, bit, self.size)},
            device_id_type=MESH,
        )

    def places(self, stage):
        return self.runs[stage] if stage < self.stages else (1, [[0], [0]])

    def loads(self, stage, chunk):
        length, both = self.places(stage)
        rows = length * self.block
        copies = []
        for early in range(stage):
            for k in range(len(both[0])):
                found = []
                for order in range(2):
                    bit = self.orders[order][early]
                    wanted = self.owners[both[order][k]] | bit
                    found.append([self.owners[p] for p in self.tables[order][early]].index(wanted))
                at = pl.multiple_of(self.chosen(chunk, found) * self.block, self.block)
                copies.append(
                    pltpu.make_async_copy(
                        self.landed[early].at[chunk, pl.ds(at, rows)],
                        self.early[stage - 1].at[early, pl.ds(k * rows, rows)],
                        self.load_sems.at[stage - 1, len(copies)],
                    )
                )
        return copies

    def begin(self, stage, chunk):
        self.remote(stage - 1, chunk).wait_recv()
        for copy in self.loads(stage, chunk):
            copy.start()

    def product(self, stage, chunk, store):
        tile = self.tile
        length, both = self.places(stage)
        rows = length * self.block
        part = rows if rows <= 512 else 512

        @pl.loop(0, self.tiles)
        def _(t):
            at = chunk * self.tiles + t
            right = self.right_of(at)
            inside = pl.ds(pl.multiple_of(t * tile, tile), tile)
            for k, pair in enumerate(zip(*both)):
                first = self.chosen(chunk, pair) * self.block
                for begin in range(0, rows, part):
                    here = pl.ds(pl.multiple_of(first + begin, self.block), part)
                    there = pl.ds(k * rows + begin, part)
                    total = jnp.dot(self.left_ref[self.which(at), here, :], right, preferred_element_type=F32)
                    for early in range(stage):
                        total = total + self.early[stage - 1][early, there, inside].astype(F32)
                    store(there, inside, total)

    def write(self, chunk):
        wide = self.tiles * self.tile
        return pltpu.make_async_copy(
            self.staged.at[chunk % 2],
            self.out_ref.at[:, pl.ds(pl.multiple_of(chunk * wide, LANES), wide)],
            self.store_sem.at[chunk % 2],
        )

    def run(self, stage, chunk):
        last = stage == self.stages
        slots = 2 if last else slots_of(stage)

        @pl.when(chunk >= slots)
        def _():
            if last:
                self.write(chunk - slots).wait()
            else:
                self.remote(stage, chunk - slots).wait_send()

        for copy in self.loads(stage, chunk):
            copy.wait()

        def store(there, inside, total):
            if last:
                self.staged[chunk % 2, there, inside] = total
            else:
                self.sent[stage][chunk % slots_of(stage), there, inside] = total.astype(BF16)

        self.product(stage, chunk, store)
        if last:
            self.write(chunk).start()
        else:
            self.remote(stage, chunk).start()

    def step(self, i, lags):
        for work in (self.begin, self.run):
            for stage, lag in enumerate(lags):
                if stage == 0 and work == self.begin:
                    continue

                @pl.when((i >= lag) & (i < self.count + lag))
                def _():
                    work(stage, i - lag)

    def drain(self):
        for stage in range(self.stages):
            for chunk in range(max(self.count - slots_of(stage), 0), self.count):
                self.remote(stage, chunk).wait_send()
        for chunk in range(max(self.count - 2, 0), self.count):
            self.write(chunk).wait()


class Streamed:
    def __init__(self, lefts, widths, weight_ref, weight_at, own_ref, other_ref, recv_sems, shared, aside=None):
        self.aside = aside
        self.lefts, self.widths, self.depth = lefts, widths, sum(widths)
        self.weight_ref, self.weight_at = weight_ref, weight_at
        self.own_ref, self.other_ref, self.recv_sems = own_ref, other_ref, recv_sems
        self.slots, self.slot_sems, self.made, self.send_sems, self.own_sems = shared
        self.count = weight_ref.shape[0] // LANES

    def fetch(self, tile):
        return pltpu.make_async_copy(
            self.weight_ref.at[pl.ds(pl.multiple_of(tile * LANES, LANES), LANES), pl.ds(self.weight_at, self.depth)],
            self.slots.at[tile % 2, :, pl.ds(0, self.depth)],
            self.slot_sems.at[tile % 2],
        )

    def columns(self, ref, tile):
        return ref.at[:, pl.ds(pl.multiple_of(tile * LANES, LANES), LANES)]

    def keep(self, tile):
        return pltpu.make_async_copy(self.made.at[tile], self.columns(self.own_ref, tile), self.own_sems.at[tile])

    def send(self, tile):
        return pltpu.make_async_remote_copy(
            src_ref=self.made.at[tile],
            dst_ref=self.columns(self.other_ref, tile),
            send_sem=self.send_sems.at[tile],
            recv_sem=self.recv_sems.at[tile],
            device_id={"tensor": 1 - lax.axis_index("tensor")},
            device_id_type=MESH,
        )

    def run(self, first, number):
        def fetches(tile):
            return [self.fetch(tile)] + ([self.aside.fetch(tile)] if self.aside else [])

        @pl.when(first == 0)
        def _():
            for copy in fetches(0):
                copy.start()

        @pl.loop(0, number)
        def _(k):
            tile = first + k
            for copy in fetches(tile):
                copy.wait()

            @pl.when(tile + 1 < self.count)
            def _():
                for copy in fetches(tile + 1):
                    copy.start()

            total, at = 0.0, 0
            for left, width in zip(self.lefts, self.widths):
                weights = self.slots[tile % 2, :, pl.ds(at, width)]
                total = total + lax.dot_general(
                    left[...], weights, (((1,), (1,)), ((), ())), preferred_element_type=F32
                )
                at += width
            self.made[tile] = total.astype(BF16)
            if self.aside:
                self.aside.use(tile, total)
            self.keep(tile).start()
            self.send(tile).start()

    def sent(self):
        @pl.loop(0, self.count)
        def _(tile):
            self.keep(tile).wait()
            self.send(tile).wait_send()

    def received(self):
        @pl.loop(0, self.count)
        def _(tile):
            self.send(tile).wait_recv()


class FirstGain:
    def __init__(self, tokens, scale_ref, slots, sems, target):
        self.tokens, self.scale_ref, self.slots, self.sems, self.target = tokens, scale_ref, slots, sems, target

    def fetch(self, tile):
        columns = pl.ds(pl.multiple_of(tile * LANES, LANES), LANES)
        return pltpu.make_async_copy(self.tokens.at[:, columns], self.slots.at[tile % 2], self.sems.at[tile % 2])

    def use(self, tile, grad):
        columns = pl.ds(pl.multiple_of(tile * LANES, LANES), LANES)
        normal = self.slots[tile % 2].astype(F32) * self.scale_ref[...]
        self.target[0:1, columns] = jnp.sum(grad * normal, 0, keepdims=True)


class Smalls:
    def __init__(self, size, me, gconv_ref, gnorm_ref, ggain_ref, pair, sums, got, total_ref, sems):
        self.size, self.me, self.bits = size, me, orders(size)[0]
        self.gconv_ref, self.gnorm_ref, self.ggain_ref = gconv_ref, gnorm_ref, ggain_ref
        self.pair, self.sums, self.got, self.total_ref = pair, sums, got, total_ref
        self.pair_sems, self.send_sems, self.recv_sems = sems

    def across(self):
        return pltpu.make_async_remote_copy(
            src_ref=self.pair.at[0],
            dst_ref=self.pair.at[1],
            send_sem=self.pair_sems.at[0],
            recv_sem=self.pair_sems.at[1],
            device_id={"tensor": 1 - lax.axis_index("tensor")},
            device_id_type=MESH,
        )

    def swap(self, stage):
        return pltpu.make_async_remote_copy(
            src_ref=self.sums.at[stage],
            dst_ref=self.got.at[stage],
            send_sem=self.send_sems.at[stage],
            recv_sem=self.recv_sems.at[stage],
            device_id={"dp": flipped(self.me, self.bits[stage], self.size)},
            device_id_type=MESH,
        )

    def run(self, step):
        model, lanes = self.gnorm_ref.shape[1], self.ggain_ref.shape[1]

        @pl.when(step == 0)
        def _():
            self.pair[0, 1:2, 0:lanes] = self.ggain_ref[...]
            self.across().start()

        @pl.when(step == 1)
        def _():
            self.across().wait()
            self.sums[0, 0:4, 0 : self.gconv_ref.shape[1]] = self.gconv_ref[...]
            self.sums[0, 4:5, 0:model] = self.gnorm_ref[...]
            self.sums[0, 5:7, 0:model] = self.pair[0, 0:2] + self.pair[1, 0:2]
            self.swap(0).start()

        for stage in range(len(self.bits)):

            @pl.when(step == stage + 2)
            def _():
                self.swap(stage).wait()
                total = self.sums[stage] + self.got[stage]
                if stage + 1 < len(self.bits):
                    self.sums[stage + 1] = total
                    self.swap(stage + 1).start()
                else:
                    self.total_ref[...] = total


def backward_kernel(plan, *refs):
    size, heads, block_heads, units, passes, shapes = plan
    (up_t, second_t, first_t, ffn_right, mixed_hbm, conv_ref, gain_ref, norm_ref, w_mixer, w_ffn, qkv_hbm, out_hbm,
     fresh_hbm, state_hbm, solve_hbm, middle_hbm, upstream_hbm, tokens_hbm, scale_ref) = refs[:19]
    (ffn_out, mix_out, beta_out, gmiddle_hbm, gs_own, gs_other, final_own, final_other, gf_own, gf_other,
     small_ref) = refs[19:30]
    stages = len(orders(size)[0])
    landed_ffn, landed_mix, landed_beta = [refs[30 + k * stages : 30 + (k + 1) * stages] for k in range(3)]
    rest = list(refs[30 + 3 * stages :])
    take = lambda number: [rest.pop(0) for _ in range(number)]
    ffn_refs = list(landed_ffn) + take(2 * stages + 5)
    mix_refs = list(landed_mix) + take(2 * stages + 5)
    beta_refs = list(landed_beta) + take(2 * stages + 5)
    (lefts, mix_right, slots, slot_sems, made, send_sems, own_sems, recv_sems, w_out, grad_mixed, gm_t, carry, ahead,
     place_sems, misc_sems, tile_sems, gconv_ref, ggain_ref, gnorm_ref, token_slots, token_sems, pair, sums, got,
     pair_sems, small_send, small_recv) = rest
    length = mix_right.shape[0]
    model = up_t.shape[0]
    block = model // size
    span = 3 * block_heads * WIDTH
    groups = heads // block_heads
    columns = heads * WIDTH
    raw_columns = groups * span + LANES
    count = length // CHUNK
    me = lax.axis_index("dp")

    barrier = pltpu.get_barrier_semaphore()
    peers = 1
    pl.semaphore_signal(barrier, inc=1, device_id={"tensor": 1 - lax.axis_index("tensor")}, device_id_type=MESH)
    for bit in orders(size)[0]:
        pl.semaphore_signal(barrier, inc=1, device_id={"dp": flipped(me, bit, size)}, device_id_type=MESH)
        peers += 1

    places = []
    for which, source in enumerate((up_t, second_t, first_t)):
        for place, bits in enumerate(offsets(size)):
            owner = pl.multiple_of(flipped(me, bits, size) * block, block)
            places.append(
                pltpu.make_async_copy(
                    source.at[pl.ds(owner, block)],
                    lefts.at[which, pl.ds(place * block, block)],
                    place_sems.at[which, place],
                )
            )
    for copy in places:
        copy.start()
    bring_mixed = pltpu.make_async_copy(mixed_hbm, mix_right.at[:, pl.ds(raw_columns, columns)], misc_sems.at[0])
    bring_mixed.start()
    bring_w_out = pltpu.make_async_copy(
        w_mixer.at[:, pl.ds(raw_columns, columns)], w_out, misc_sems.at[1]
    )
    bring_w_out.start()
    gconv_ref[...] = jnp.zeros_like(gconv_ref)
    ggain_ref[...] = jnp.zeros_like(ggain_ref)
    gnorm_ref[...] = jnp.zeros_like(gnorm_ref)
    pair[...] = jnp.zeros_like(pair)
    sums[...] = jnp.zeros_like(sums)
    strength_lanes = pl.ds(groups * span, LANES)
    mix_right[:, strength_lanes] = jnp.zeros((length, LANES), BF16)
    pl.semaphore_wait(barrier, peers)
    for copy in places:
        copy.wait()

    (ffn_count, ffn_tiles, ffn_tile), (mix_count, mix_tiles, mix_tile), _ = shapes
    per_matrix = units // ffn_tile

    def ffn_columns(at):
        return ffn_right[at // per_matrix, :, pl.ds(pl.multiple_of(at % per_matrix * ffn_tile, ffn_tile), ffn_tile)]

    ffn = Scatter(size, me, ffn_count, ffn_tiles, ffn_tile, lambda at: (at // per_matrix + 1) // 2, lefts, ffn_columns,
                  ffn_out, ffn_refs)
    raw_tiles = groups * span // mix_tile

    def mix_columns(at):
        return mix_right[:, pl.ds(pl.multiple_of(at * mix_tile + at // raw_tiles * LANES, LANES), mix_tile)]

    mix = Scatter(size, me, mix_count, mix_tiles, mix_tile, lambda at: 2 + at // raw_tiles, lefts, mix_columns,
                  mix_out, mix_refs)
    beta = Scatter(size, me, 1, 1, LANES, lambda at: 2, lefts, lambda at: mix_right[:, strength_lanes],
                   beta_out, beta_refs)
    shared = (slots, slot_sems, made, send_sems, own_sems)
    gs = Streamed([ffn_right.at[1], ffn_right.at[2]], [units] * 2, w_ffn, units, gs_own, gs_other, recv_sems.at[0],
                  shared)
    final = Streamed([ffn_right.at[0]], [units], w_ffn, 0, final_own, final_other, recv_sems.at[1], shared)
    gf = Streamed([mix_right.at[:, pl.ds(0, raw_columns)]], [raw_columns], w_mixer, 0, gf_own, gf_other,
                  recv_sems.at[2], shared, FirstGain(tokens_hbm, scale_ref, token_slots, token_sems, pair.at[0]))
    smalls = Smalls(size, me, gconv_ref, gnorm_ref, ggain_ref, pair, sums, got, small_ref,
                    (pair_sems, small_send, small_recv))

    def middle_part():
        gs.received()

        def scoped(own, other, middle, upstream, result, low):
            def fetches(t):
                rows = pl.ds(pl.multiple_of(t * CHUNK, CHUNK), CHUNK)
                return [
                    pltpu.make_async_copy(source.at[rows], target, tile_sems.at[k])
                    for k, (source, target) in enumerate(
                        ((gs_own, own), (gs_other, other), (middle_hbm, middle), (upstream_hbm, upstream))
                    )
                ]

            @pl.loop(0, count)
            def _(t):
                rows = pl.ds(pl.multiple_of(t * CHUNK, CHUNK), CHUNK)
                for copy in fetches(t):
                    copy.start()
                for copy in fetches(t):
                    copy.wait()

                @pl.loop(0, CHUNK // 16)
                def _(k):
                    here = pl.ds(pl.multiple_of(k * 16, 16), 16)
                    grad = own[here].astype(F32) + other[here].astype(F32)
                    values = middle[here]
                    scale = lax.rsqrt(jnp.mean(values * values, -1, keepdims=True) + epsilon)
                    normal = values * scale
                    scaled = grad * norm_ref[...]
                    gnorm_ref[...] += jnp.sum(grad * normal, 0, keepdims=True)
                    total = upstream[here].astype(F32) + scale * (
                        scaled - normal * jnp.mean(scaled * normal, -1, keepdims=True)
                    )
                    result[here] = total
                    low[here] = total.astype(BF16)

                write = pltpu.make_async_copy(result, gmiddle_hbm.at[rows], tile_sems.at[4])
                write.start()
                grad_mixed[rows] = jnp.dot(low[...], w_out[...], preferred_element_type=F32)

                @pl.loop(0, model // LANES)
                def _(k):
                    lanes = pl.ds(pl.multiple_of(k * LANES, LANES), LANES)
                    gm_t[lanes, rows] = result[:, lanes].T.astype(BF16)

                write.wait()

        pl.run_scoped(
            scoped,
            pltpu.VMEM((CHUNK, model), BF16),
            pltpu.VMEM((CHUNK, model), BF16),
            pltpu.VMEM((CHUNK, model), F32),
            pltpu.VMEM((CHUNK, model), BF16),
            pltpu.VMEM((CHUNK, model), F32),
            pltpu.VMEM((CHUNK, model), BF16),
        )
        for place, bits in enumerate(offsets(size)):
            owner = pl.multiple_of(flipped(me, bits, size) * block, block)
            lefts[3, place * block : (place + 1) * block] = gm_t[pl.ds(owner, block)]

    def delta_part(piece):
        group = piece // count
        c = count - 1 - piece % count

        def scoped(cur, tail, beta, out, fresh, state, solve):
            rows = pl.ds(pl.multiple_of(c * CHUNK, CHUNK), CHUNK)
            before = pl.ds(pl.multiple_of((c * CHUNK + length - 8) % length // 8 * 8, 8), 8)
            lanes = pl.ds(pl.multiple_of(group * span, LANES), span)
            narrow = pl.ds(pl.multiple_of(group * block_heads * WIDTH, LANES), block_heads * WIDTH)
            ours = pl.ds(group * block_heads, block_heads)
            copies = [
                pltpu.make_async_copy(source, target, tile_sems.at[k])
                for k, (source, target) in enumerate(
                    (
                        (qkv_hbm.at[rows, lanes], cur),
                        (qkv_hbm.at[before, lanes], tail),
                        (qkv_hbm.at[rows, strength_lanes], beta),
                        (out_hbm.at[rows, narrow], out),
                        (fresh_hbm.at[rows, narrow], fresh),
                        (state_hbm.at[ours, c], state),
                        (solve_hbm.at[ours, c], solve),
                    )
                )
            ]
            for copy in copies:
                copy.start()

            @pl.when(piece % count == 0)
            def _():
                carry[...] = jnp.zeros_like(carry)
                ahead[...] = jnp.zeros_like(ahead)

            for copy in copies:
                copy.wait()
            backward_piece(
                block_heads, WIDTH, passes, group, c, cur, tail, beta, conv_ref, gain_ref, grad_mixed, out, fresh,
                state, solve, mix_right, mix_right.at[:, strength_lanes], gconv_ref, ggain_ref, carry, ahead,
            )

        pl.run_scoped(
            scoped,
            pltpu.VMEM((CHUNK, span), F32),
            pltpu.VMEM((8, span), F32),
            pltpu.VMEM((CHUNK, LANES), F32),
            pltpu.VMEM((CHUNK, block_heads * WIDTH), F32),
            pltpu.VMEM((CHUNK, block_heads * WIDTH), F32),
            pltpu.VMEM((block_heads, WIDTH, WIDTH), F32),
            pltpu.VMEM((block_heads, CHUNK, CHUNK), F32),
        )

    lags = [0, 1] + [4 + 2 * stage for stage in range(stages - 1)]
    quarter = gs.count // 4
    at_final, at_middle, at_delta = 16, 6, 7
    pieces = groups * count
    at_gf = at_delta + -(-pieces // 2)

    def step(i, carried):
        ffn.step(i, lags)
        mix.step(i - ffn_count - 0, lags)
        beta.step(i - at_gf - 1, lags)

        @pl.when(i < 4)
        def _():
            gs.run(i * quarter, quarter)

        @pl.when(i == at_middle)
        def _():
            gs.sent()
            bring_w_out.wait()
            bring_mixed.wait()
            middle_part()

        @pl.when((i >= at_delta) & (i < at_gf))
        def _():
            @pl.loop(0, 2)
            def _(k):
                @pl.when((i - at_delta) * 2 + k < pieces)
                def _():
                    delta_part((i - at_delta) * 2 + k)

        @pl.when((i >= at_gf) & (i < at_gf + 4))
        def _():
            gf.run((i - at_gf) * quarter, quarter)

        smalls.run(i - at_gf - 4)

        @pl.when(i == at_final)
        def _():
            gf.sent()

        @pl.when((i >= at_final) & (i < at_final + 4))
        def _():
            final.run((i - at_final) * quarter, quarter)

        return carried

    steps = max(ffn_count + 0 + mix_count + lags[-1], at_final + 4, at_gf + 2 + lags[-1], at_gf + 6 + stages)
    lax.fori_loop(0, steps, step, 0)
    ffn.drain()
    mix.drain()
    beta.drain()
    final.sent()
    final.received()
    gf.received()


def feed_forward_kernel(second_ref, upstream_ref, down_ref, gate_ref, up_ref, result_ref):
    part = 256
    for begin in range(0, second_ref.shape[0], part):
        rows = slice(begin, begin + part)
        gate = jnp.dot(second_ref[rows], gate_ref[...], preferred_element_type=F32)
        up = jnp.dot(second_ref[rows], up_ref[...], preferred_element_type=F32)
        grad_hidden = jnp.dot(upstream_ref[rows], down_ref[...], preferred_element_type=F32)
        sigma = sigmoid(gate)
        activated = gate * sigma
        result_ref[0, rows] = (activated * up).astype(BF16)
        result_ref[1, rows] = (grad_hidden * up * sigma * (1.0 + gate * (1.0 - sigma))).astype(BF16)
        result_ref[2, rows] = (grad_hidden * activated).astype(BF16)


def feed_forward(second, upstream, w_ffn):
    length, model = second.shape
    units = w_ffn.shape[1] // 3
    tile = 256 if units % 256 == 0 else 128
    tiles = units // tile
    whole = pl.BlockSpec((length, model), lambda j: (0, 0))
    weights = [pl.BlockSpec((model, tile), lambda j, k=k: (0, k * tiles + j)) for k in range(3)]
    return pl.pallas_call(
        feed_forward_kernel,
        grid=(tiles,),
        in_specs=[whole, whole] + weights,
        out_specs=pl.BlockSpec((3, length, tile), lambda j: (0, 0, j)),
        out_shape=jax.ShapeDtypeStruct((3, length, units), BF16),
        compiler_params=pltpu.CompilerParams(vmem_limit_bytes=32 * 2**20),
        name="feed_forward",
    )(second, upstream, w_ffn, w_ffn, w_ffn)


def backward_all(size, heads, block_heads, up_t, second_t, first_t, ffn_right, mixed, conv, gain, norm_ffn, w_mixer,
                 w_ffn, qkv, out, fresh, state, solve, middle, upstream, tokens, scale, passes=3):
    length = qkv.shape[0]
    model = up_t.shape[0]
    units = ffn_right.shape[2]
    block = model // size
    groups = heads // block_heads
    span = 3 * block_heads * WIDTH
    columns = heads * WIDTH
    raw_columns = groups * span + LANES
    mix_columns = raw_columns + columns
    ffn_tile = 256 if units % 256 == 0 else 128
    shapes = []
    mix_tile = 256 if columns % 256 == 0 else 128
    for total, tile in ((3 * units, ffn_tile), (4 * columns, mix_tile), (LANES, LANES)):
        tiles = next(t for t in (3, 2, 1) if total // tile % t == 0)
        shapes.append((total // tile // tiles, tiles, tile))
    landed, scratch = [], []
    for number, tiles, tile in shapes:
        more_landed, more_scratch = Scatter.scratch(size, block, number, tiles * tile)
        landed += more_landed
        scratch += more_scratch
    tiles = model // LANES
    stages = len(orders(size)[0])
    small_columns = max(groups * span, model)
    scratch += [
        pltpu.VMEM((4, model, length), BF16),
        pltpu.VMEM((length, mix_columns), BF16),
        pltpu.VMEM((2, LANES, max(2 * units, raw_columns)), BF16),
        pltpu.SemaphoreType.DMA((2,)),
        pltpu.VMEM((tiles, length, LANES), BF16),
        pltpu.SemaphoreType.DMA((tiles,)),
        pltpu.SemaphoreType.DMA((tiles,)),
        pltpu.SemaphoreType.DMA((3, tiles)),
        pltpu.VMEM((model, columns), BF16),
        pltpu.VMEM((length, columns), F32),
        pltpu.VMEM((model, length), BF16),
        pltpu.VMEM((block_heads, WIDTH, WIDTH), F32),
        pltpu.VMEM((8, span), F32),
        pltpu.SemaphoreType.DMA((3, size)),
        pltpu.SemaphoreType.DMA((2,)),
        pltpu.SemaphoreType.DMA((7,)),
        pltpu.VMEM((4, groups * span), F32),
        pltpu.VMEM((1, WIDTH), F32),
        pltpu.VMEM((1, model), F32),
        pltpu.VMEM((2, length, LANES), BF16),
        pltpu.SemaphoreType.DMA((2,)),
        pltpu.VMEM((2, 8, model), F32),
        pltpu.VMEM((stages, 8, small_columns), F32),
        pltpu.VMEM((stages, 8, small_columns), F32),
        pltpu.SemaphoreType.DMA((2,)),
        pltpu.SemaphoreType.DMA((stages,)),
        pltpu.SemaphoreType.DMA((stages,)),
    ]
    vmem, hbm = pl.BlockSpec(memory_space=pltpu.VMEM), pl.BlockSpec(memory_space=pl.ANY)
    shape = jax.ShapeDtypeStruct
    exchanged = [shape((length, model), BF16)] * 6
    return pl.pallas_call(
        functools.partial(backward_kernel, (size, heads, block_heads, units, passes, shapes)),
        in_specs=[hbm] * 3 + [vmem, hbm] + [vmem] * 3 + [hbm] * 10 + [vmem],
        out_specs=[hbm] * 10 + [vmem] + [hbm] * len(landed),
        out_shape=[shape((block, 3 * units), F32), shape((block, 4 * columns), F32),
                   shape((block, LANES), F32), shape((length, model), F32)]
        + exchanged
        + [shape((8, small_columns), F32)]
        + landed,
        scratch_shapes=scratch,
        compiler_params=pltpu.CompilerParams(
            collective_id=0, has_side_effects=True, vmem_limit_bytes=62 * 2**20
        ),
        name="backward_all",
    )(up_t, second_t, first_t, ffn_right, mixed, conv, gain, norm_ffn, w_mixer, w_ffn, qkv, out, fresh, state, solve,
      middle, upstream, tokens, scale)[:11]


def matmul(left, right):
    return jnp.dot(left, right, preferred_element_type=F32)


def right_inner(left, right):
    return lax.dot_general(left, right, (((1,), (1,)), ((), ())), preferred_element_type=F32)


def row_norm(values, gain):
    return values * lax.rsqrt(jnp.mean(values * values, -1, keepdims=True) + epsilon) * gain


def swap(values, axis, size, by):
    return lax.ppermute(values, axis, [(d, d ^ by) for d in range(size)])


def exchange(partial):
    own = lax.reduce_precision(partial, 8, 7)
    return own, swap(own.astype(BF16), "tensor", 2, 1)


def by_groups(parts, block):
    span = block * WIDTH
    return [part[:, g * span : (g + 1) * span] for g in range(parts[0].shape[1] // span) for part in parts]


def from_groups(whole, block, index, columns):
    span = block * WIDTH
    return jnp.concatenate(
        [whole[:, (3 * g + index) * span : (3 * g + index + 1) * span] for g in range(columns // span)], 1
    )


def body(size, tokens, lengths, w_query, w_key, w_value, w_beta, conv_query, conv_key, conv_value, head_gain,
         w_out, norm_attn, norm_ffn, w_gate, w_up, w_down, cotangent):
    inputs = tokens.astype(F32)
    length, model = inputs.shape
    columns = w_query.shape[1]
    units = w_gate.shape[1]
    heads = w_beta.shape[1]
    block = 4 if heads % 4 == 0 else 1
    raw_columns = 3 * columns + LANES
    strengths = jnp.pad(w_beta.astype(BF16), ((0, 0), (0, LANES - heads)))
    low = [w.astype(BF16) for w in (w_query, w_key, w_value)]
    w_mixer = lax.all_gather(
        jnp.concatenate(by_groups(low, block) + [strengths, w_out.astype(BF16).T], 1), "dp", axis=0, tiled=True
    )
    w_ffn = lax.all_gather(
        jnp.concatenate([w_down.astype(BF16).T, w_gate.astype(BF16), w_up.astype(BF16)], 1), "dp", axis=0, tiled=True
    )
    conv = jnp.concatenate(by_groups([conv_query, conv_key, conv_value], block), 1)
    gain = head_gain[None]

    first_scale = lax.rsqrt(jnp.mean(inputs * inputs, -1, keepdims=True) + epsilon)
    first = (inputs * first_scale * norm_attn).astype(BF16)
    qkv = matmul(first, w_mixer[:, :raw_columns])
    mixed, out, fresh, state, solve = delta_forward(qkv, conv, gain, heads, block, (3, 3, 3, 3))
    own, other = exchange(right_inner(mixed, w_mixer[:, raw_columns:]))
    middle = inputs + (own + other.astype(F32))
    second = row_norm(middle, norm_ffn).astype(BF16)
    positions = lax.broadcasted_iota(jnp.int32, (length, 1), 0)
    valid = (positions < lengths[0]).astype(F32)
    upstream = (cotangent.astype(F32) * valid).astype(BF16)
    (ffn_grads, mixer_grads, beta_grads, grad_middle, _, _, final_own, final_other, first_own, first_other,
     small) = backward_all(
        size, heads, block, upstream.T, second.T, first.T,
        feed_forward(second, upstream, w_ffn),
        mixed, conv, gain, norm_ffn[None], w_mixer, w_ffn, qkv, out, fresh, state, solve, middle, upstream, tokens, first_scale,
    )
    final = middle + (final_own.astype(F32) + final_other.astype(F32))
    block_out = (final * valid).astype(BF16)
    normal = inputs * first_scale
    scaled = (first_own.astype(F32) + first_other.astype(F32)) * norm_attn
    grad_tokens = grad_middle + first_scale * (scaled - normal * jnp.mean(scaled * normal, -1, keepdims=True))
    convs = small[:4, : 3 * columns]
    return (
        block_out,
        grad_tokens,
        from_groups(mixer_grads, block, 0, columns),
        from_groups(mixer_grads, block, 1, columns),
        from_groups(mixer_grads, block, 2, columns),
        beta_grads[:, :heads],
        from_groups(convs, block, 0, columns),
        from_groups(convs, block, 1, columns),
        from_groups(convs, block, 2, columns),
        small[6, :WIDTH],
        mixer_grads[:, 3 * columns :].T,
        small[5, :model],
        small[4, :model],
        ffn_grads[:, units : 2 * units],
        ffn_grads[:, 2 * units :],
        ffn_grads[:, :units].T,
    )


def solution(mesh):
    rows, both, cols = P("dp", None), P("dp", "tensor"), P("tensor", "dp")
    taps = P(None, "tensor")
    in_specs = (rows, P("dp"), both, both, both, both, taps, taps, taps, P(), cols, P(), P(), both, both, cols, rows)
    out_specs = (rows, rows, both, both, both, both, taps, taps, taps, P(), cols, P(), P(), both, both, cols)
    return jax.shard_map(
        functools.partial(body, mesh.shape["dp"]), mesh=mesh, in_specs=in_specs, out_specs=out_specs, check_vma=False
    )
```

```python
import functools
import jax
import jax.numpy as jnp
from jax import lax
from jax.experimental import pallas as pl
from jax.experimental.pallas import tpu as pltpu
from jax.sharding import PartitionSpec as P

CHUNK = 128
WIDTH = 128
LANES = 128
epsilon = 1e-06
HIGH = lax.Precision.HIGHEST
F32 = jnp.float32
BF16 = jnp.bfloat16
MESH = pl.DeviceIdType.MESH


def dot(left, right, dims, passes):
    form = (dims, ((), ()))
    if passes == 6:
        return lax.dot_general(left, right, form, precision=HIGH, preferred_element_type=F32)
    left_hi, right_hi = left.astype(BF16), right.astype(BF16)
    total = lax.dot_general(left_hi, right_hi, form, preferred_element_type=F32)
    if passes == 3:
        left_lo = (left - left_hi.astype(F32)).astype(BF16)
        right_lo = (right - right_hi.astype(F32)).astype(BF16)
        total = total + (
            lax.dot_general(left_hi, right_lo, form, preferred_element_type=F32)
            + lax.dot_general(left_lo, right_hi, form, preferred_element_type=F32)
        )
    return total


def nn(left, right, passes):
    return dot(left, right, ((1,), (0,)), passes)


def nt(left, right, passes):
    return dot(left, right, ((1,), (1,)), passes)


def tn(left, right, passes):
    return dot(left, right, ((0,), (0,)), passes)


def sigmoid(x):
    return 1.0 / (1.0 + jnp.exp(-x))


def shift_down(cur, tail, by):
    rolled = pltpu.roll(cur, by, 0)
    rows = lax.broadcasted_iota(jnp.int32, tail.shape, 0)
    top = jnp.where(rows < by, pltpu.roll(tail, by, 0), rolled[:8])
    return jnp.concatenate([top, rolled[8:]], 0)


def shift_up(cur, head, by):
    size = cur.shape[0]
    rolled = pltpu.roll(cur, size - by, 0)
    rows = lax.broadcasted_iota(jnp.int32, head.shape, 0)
    bottom = jnp.where(rows >= 8 - by, pltpu.roll(head, 8 - by, 0), rolled[size - 8 :])
    return jnp.concatenate([rolled[: size - 8], bottom], 0)


def unit_scale(values):
    return lax.rsqrt(jnp.sum(values * values, -1, keepdims=True) + epsilon)


def masks(size):
    rows = lax.broadcasted_iota(jnp.int32, (size, size), 0)
    cols = lax.broadcasted_iota(jnp.int32, (size, size), 1)
    return rows, cols, rows ^ cols


def unit_lower_inverses(lowers, passes):
    size = lowers[0].shape[0]
    rows, cols, apart = masks(size)
    inverses = [jnp.where(rows == cols, 1.0, jnp.where(apart < 2, -lower, 0.0)) for lower in lowers]
    span = 2
    while span < size:
        corner = (apart < 2 * span) & (apart >= span)
        halves = [nn(jnp.where(corner, a, 0.0), x, passes) for a, x in zip(lowers, inverses)]
        inverses = [x - nn(x, half, passes) for x, half in zip(inverses, halves)]
        span *= 2
    return inverses


def pick(table, column):
    lanes = lax.broadcasted_iota(jnp.int32, table.shape, 1)
    return jnp.sum(jnp.where(lanes == column, table, 0.0), 1, keepdims=True)


def forward_kernel(heads, width, ps, qkv_ref, beta_ref, conv_ref, gain_ref,
                   mixed_ref, out_ref, fresh_ref, state_ref, solve_ref, carry):
    group = pl.program_id(0)
    chunk = CHUNK
    length = qkv_ref.shape[0]
    carry[...] = jnp.zeros_like(carry)
    p_gram, p_inv, p_state, p_out = ps

    def step(c, _):
        base = pl.multiple_of(c * chunk, chunk)
        rows = pl.ds(base, chunk)
        before = pl.ds(pl.multiple_of(jnp.maximum(base - 8, 0), 8), 8)
        beta = sigmoid(beta_ref[rows, :])
        row, col, _ = masks(chunk)
        gain = gain_ref[...]
        queries, keys, values, strengths = [], [], [], []
        for j in range(heads):
            parts = []
            for part in range(3):
                lanes = pl.ds((part * heads + j) * width, width)
                cur = qkv_ref[rows, lanes]
                tail = jnp.where(c > 0, qkv_ref[before, lanes], 0.0)
                taps = conv_ref[:, lanes]
                total = taps[3:4] * cur
                for by in (1, 2, 3):
                    total = total + taps[3 - by : 4 - by] * shift_down(cur, tail, by)
                parts.append(total * sigmoid(total))
            query, key, value = parts
            queries.append(query * (unit_scale(query) * width ** (-0.5)))
            keys.append(key * unit_scale(key))
            values.append(value)
            strengths.append(pick(beta, group * heads + j))
        grams = [nt(key, key, p_gram) for key in keys]
        solves = unit_lower_inverses(
            [jnp.where(row > col, gram * strength, 0.0) for gram, strength in zip(grams, strengths)], p_inv
        )
        states = [carry[j] for j in range(heads)]
        errors = [value - nn(key, state, p_state) for value, key, state in zip(values, keys, states)]
        freshes = [nn(solve, s * e, p_state) for solve, s, e in zip(solves, strengths, errors)]
        for j in range(heads):
            carry[j] = states[j] + tn(keys[j], freshes[j], p_state)
        scores = [jnp.where(row >= col, nt(q, k, p_out), 0.0) for q, k in zip(queries, keys)]
        outs = [
            nn(q, s, p_out) + nn(score, f, p_out) for q, s, score, f in zip(queries, states, scores, freshes)
        ]
        for j, out in enumerate(outs):
            state_ref[j, c] = states[j]
            solve_ref[j, c] = solves[j]
            lanes = pl.ds(j * width, width)
            fresh_ref[rows, lanes] = freshes[j]
            out_ref[rows, lanes] = out
            scale = lax.rsqrt(jnp.mean(out * out, -1, keepdims=True) + epsilon)
            mixed_ref[rows, lanes] = (out * scale * gain).astype(BF16)
        return 0

    lax.fori_loop(0, length // chunk, step, 0)


def delta_forward(qkv, conv, gain, heads, block, ps=(6, 6, 6, 6)):
    length = qkv.shape[0]
    width = gain.shape[1]
    groups = heads // block
    span = 3 * block * width
    last = groups * span // 128
    count = length // CHUNK
    return pl.pallas_call(
        functools.partial(forward_kernel, block, width, ps),
        grid=(groups,),
        in_specs=[
            pl.BlockSpec((length, span), lambda g: (0, g)),
            pl.BlockSpec((length, 128), lambda g: (0, last)),
            pl.BlockSpec((4, span), lambda g: (0, g)),
            pl.BlockSpec((1, width), lambda g: (0, 0)),
        ],
        out_specs=[
            pl.BlockSpec((length, block * width), lambda g: (0, g)),
            pl.BlockSpec((length, block * width), lambda g: (0, g)),
            pl.BlockSpec((length, block * width), lambda g: (0, g)),
            pl.BlockSpec((block, count, width, width), lambda g: (g, 0, 0, 0)),
            pl.BlockSpec((block, count, CHUNK, CHUNK), lambda g: (g, 0, 0, 0)),
        ],
        out_shape=[
            jax.ShapeDtypeStruct((length, heads * width), BF16),
            jax.ShapeDtypeStruct((length, heads * width), F32),
            jax.ShapeDtypeStruct((length, heads * width), F32),
            jax.ShapeDtypeStruct((heads, count, width, width), F32),
            jax.ShapeDtypeStruct((heads, count, CHUNK, CHUNK), F32),
        ],
        scratch_shapes=[pltpu.VMEM((block, width, width), F32)],
        compiler_params=pltpu.CompilerParams(vmem_limit_bytes=48 * 2**20),
        name="delta_forward",
    )(qkv, qkv, conv, gain)


def backward_piece(heads, width, passes, group, c, cur_ref, tail_ref, beta_ref, conv_ref, gain_ref, grad_ref, out_ref,
                   fresh_ref, state_ref, solve_ref, raw_ref, gbeta_ref, gconv_ref, ggain_ref, carry, ahead):
    chunk = CHUNK
    span = 3 * heads * width
    rows = pl.ds(pl.multiple_of(c * chunk, chunk), chunk)
    beta = sigmoid(beta_ref[...])
    row, col, _ = masks(chunk)
    gain = gain_ref[...]
    lane = lax.broadcasted_iota(jnp.int32, beta.shape, 1)
    every = range(heads)

    def lanes_of(part, j):
        return pl.ds((part * heads + j) * width, width)

    def wide_lanes(part, j):
        return pl.ds(pl.multiple_of(group * span + (part * heads + j) * width, width), width)

    def before_silu(part, j, keep):
        cur = cur_ref[:, lanes_of(part, j)]
        tail = jnp.where(c > 0, tail_ref[:, lanes_of(part, j)], 0.0)
        taps = conv_ref[:, wide_lanes(part, j)]
        moved = [cur] + [shift_down(cur, tail, by) for by in (1, 2, 3)]
        total = taps[3:4] * cur
        for by in (1, 2, 3):
            total = total + taps[3 - by : 4 - by] * moved[by]
        return moved if keep else total

    queries, keys, errors, strengths, grad_outs, freshes = [], [], [], [], [], []
    ggain = jnp.zeros_like(gain)
    for j in every:
        acts = []
        for part in range(3):
            pre = before_silu(part, j, False)
            acts.append(pre * sigmoid(pre))
        queries.append(acts[0] * (unit_scale(acts[0]) * width ** (-0.5)))
        keys.append(acts[1] * unit_scale(acts[1]))
        errors.append(acts[2])
        strengths.append(pick(beta, group * heads + j))
        lanes = pl.ds(j * width, width)
        out = out_ref[:, lanes]
        freshes.append(fresh_ref[:, lanes])
        grad_mixed = grad_ref[rows, pl.ds(pl.multiple_of((group * heads + j) * width, width), width)]
        scale = lax.rsqrt(jnp.mean(out * out, -1, keepdims=True) + epsilon)
        normal = out * scale
        ggain = ggain + jnp.sum(grad_mixed * normal, 0, keepdims=True)
        scaled = grad_mixed * gain
        grad_outs.append(scale * (scaled - normal * jnp.mean(scaled * normal, -1, keepdims=True)))
    ggain_ref[...] += ggain

    scores = [jnp.where(row >= col, nt(queries[j], keys[j], passes), 0.0) for j in every]
    grad_freshes = [tn(scores[j], grad_outs[j], passes) + nn(keys[j], carry[j], passes) for j in every]
    pulled = [tn(solve_ref[j], grad_freshes[j], passes) for j in every]
    grad_errors = [strengths[j] * pulled[j] for j in every]
    grad_keys = [nt(freshes[j], carry[j], passes) - nt(grad_errors[j], state_ref[j], passes) for j in every]
    for j in every:
        carry[j] = carry[j] + (tn(queries[j], grad_outs[j], passes) - tn(keys[j], grad_errors[j], passes))
    grams = [nt(keys[j], keys[j], passes) for j in every]
    errors = [errors[j] - nn(keys[j], state_ref[j], passes) for j in every]
    grad_scores = [jnp.where(row >= col, nt(grad_outs[j], freshes[j], passes), 0.0) for j in every]
    grad_lowers = [jnp.where(row > col, -nt(pulled[j], freshes[j], passes), 0.0) for j in every]
    grad_queries = [nt(grad_outs[j], state_ref[j], passes) + nn(grad_scores[j], keys[j], passes) for j in every]
    grad_grams = [grad_lowers[j] * strengths[j] for j in every]
    grad_keys = [
        grad_keys[j] + tn(grad_scores[j], queries[j], passes) + nn(grad_grams[j] + grad_grams[j].T, keys[j], passes)
        for j in every
    ]
    gbeta = jnp.zeros(beta.shape, F32)
    for j in every:
        grad_strength = jnp.sum(pulled[j] * errors[j] + grad_lowers[j] * grams[j], -1, keepdims=True)
        grad_strength = grad_strength * (strengths[j] * (1.0 - strengths[j]))
        gbeta = jnp.where(lane == group * heads + j, grad_strength, gbeta)
    gbeta_ref[rows, :] += gbeta.astype(BF16)

    for j in every:
        for part in range(3):
            moved = before_silu(part, j, True)
            taps = conv_ref[:, wide_lanes(part, j)]
            pre = taps[3:4] * moved[0]
            for by in (1, 2, 3):
                pre = pre + taps[3 - by : 4 - by] * moved[by]
            gate = sigmoid(pre)
            act = pre * gate
            if part == 0:
                scale = unit_scale(act)
                unit = act * scale
                grad = grad_queries[j] * width ** (-0.5)
                grad = scale * (grad - unit * jnp.sum(grad * unit, -1, keepdims=True))
            elif part == 1:
                grad = grad_keys[j]
                unit = keys[j]
                grad = unit_scale(act) * (grad - unit * jnp.sum(grad * unit, -1, keepdims=True))
            else:
                grad = grad_errors[j]
            grad = grad * gate * (1.0 + pre * (1.0 - gate))
            after = ahead[:, lanes_of(part, j)]
            total = taps[3:4] * grad
            for by in (1, 2, 3):
                total = total + taps[3 - by : 4 - by] * shift_up(grad, after, by)
            raw_ref[rows, wide_lanes(part, j)] = total.astype(BF16)
            ahead[:, lanes_of(part, j)] = grad[:8]
            sums = [jnp.sum(grad * moved[3 - tap], 0, keepdims=True) for tap in range(4)]
            gconv_ref[:, wide_lanes(part, j)] += jnp.concatenate(sums, 0)


def orders(size):
    bits, unit = [], 1
    while unit < size:
        bits.append(unit)
        unit *= 2
    return bits, bits[:1] + bits[2:] + bits[1:2]


def offsets(size):
    found = [0]
    for bit in orders(size)[0]:
        found = [old + value for old in found for value in (0, bit)]
    return found


def flipped(index, bits, size):
    result, unit = 0, 1
    while unit < size:
        result = result + (index // unit + bits // unit) % 2 * unit
        unit *= 2
    return result


def sent_places(size):
    owners = offsets(size)
    tables = []
    for order in orders(size):
        held, table = list(range(size)), []
        for bit in order:
            table.append([place for place in held if owners[place] & bit])
            held = [place for place in held if not owners[place] & bit]
        tables.append(table)
    stages = []
    for both in zip(*tables):
        length = len(both[0])
        while not all(
            places[at : at + length] == list(range(places[at], places[at] + length))
            for places in both
            for at in range(0, len(places), length)
        ):
            length //= 2
        stages.append((length, [places[::length] for places in both]))
    return stages, tables


def slots_of(stage):
    return 3 if stage == 1 else 2


class Scatter:
    def __init__(self, size, me, count, tiles, tile, which, left_ref, right_of, out_ref, refs):
        self.orders = orders(size)
        self.stages = stages = len(self.orders[0])
        self.runs, self.tables = sent_places(size)
        self.owners = offsets(size)
        self.size, self.me, self.count, self.tiles, self.tile, self.which = size, me, count, tiles, tile, which
        self.left_ref, self.right_of, self.out_ref = left_ref, right_of, out_ref
        self.landed, self.sent, self.early = refs[:stages], refs[stages : 2 * stages], refs[2 * stages : 3 * stages]
        self.send_sems, self.recv_sems, self.load_sems, self.staged, self.store_sem = refs[3 * stages : 3 * stages + 5]
        self.block = left_ref.shape[1] // size

    @staticmethod
    def scratch(size, block, count, wide):
        stages = len(orders(size)[0])
        sends = [(size >> (stage + 1)) * block for stage in range(stages)]
        landed = [jax.ShapeDtypeStruct((count, rows, wide), BF16) for rows in sends]
        rest = (
            [pltpu.VMEM((slots_of(stage), rows, wide), BF16) for stage, rows in enumerate(sends)]
            + [pltpu.VMEM((stage + 1, rows, wide), BF16) for stage, rows in enumerate(sends[1:] + [block])]
            + [
                pltpu.SemaphoreType.DMA((slots_of(1), stages)),
                pltpu.SemaphoreType.DMA((count, stages)),
                pltpu.SemaphoreType.DMA((stages, 2 * stages)),
                pltpu.VMEM((2, block, wide), F32),
                pltpu.SemaphoreType.DMA((2,)),
            ]
        )
        return landed, rest

    @staticmethod
    def other_order(chunk):
        return (chunk + 3) % 6 // 5

    def chosen(self, chunk, pair):
        first, second = pair
        return first if first == second else first + self.other_order(chunk) * (second - first)

    def remote(self, stage, chunk):
        bit = self.chosen(chunk, [order[stage] for order in self.orders])
        return pltpu.make_async_remote_copy(
            src_ref=self.sent[stage].at[chunk % slots_of(stage)],
            dst_ref=self.landed[stage].at[chunk],
            send_sem=self.send_sems.at[chunk % slots_of(stage), stage],
            recv_sem=self.recv_sems.at[chunk, stage],
            device_id={"dp": flipped(self.me, bit, self.size)},
            device_id_type=MESH,
        )

    def places(self, stage):
        return self.runs[stage] if stage < self.stages else (1, [[0], [0]])

    def loads(self, stage, chunk):
        length, both = self.places(stage)
        rows = length * self.block
        copies = []
        for early in range(stage):
            for k in range(len(both[0])):
                found = []
                for order in range(2):
                    bit = self.orders[order][early]
                    wanted = self.owners[both[order][k]] | bit
                    found.append([self.owners[p] for p in self.tables[order][early]].index(wanted))
                at = pl.multiple_of(self.chosen(chunk, found) * self.block, self.block)
                copies.append(
                    pltpu.make_async_copy(
                        self.landed[early].at[chunk, pl.ds(at, rows)],
                        self.early[stage - 1].at[early, pl.ds(k * rows, rows)],
                        self.load_sems.at[stage - 1, len(copies)],
                    )
                )
        return copies

    def begin(self, stage, chunk):
        self.remote(stage - 1, chunk).wait_recv()
        for copy in self.loads(stage, chunk):
            copy.start()

    def product(self, stage, chunk, store):
        tile = self.tile
        length, both = self.places(stage)
        rows = length * self.block
        part = rows if rows <= 512 else 512

        for t in range(self.tiles):
            at = chunk * self.tiles + t
            right = self.right_of(at)
            inside = slice(t * tile, (t + 1) * tile)
            for k, pair in enumerate(zip(*both)):
                first = self.chosen(chunk, pair) * self.block
                for begin in range(0, rows, part):
                    here = pl.ds(pl.multiple_of(first + begin, self.block), part)
                    there = slice(k * rows + begin, k * rows + begin + part)
                    total = jnp.dot(self.left_ref[self.which(at), here, :], right, preferred_element_type=F32)
                    for early in range(stage):
                        total = total + self.early[stage - 1][early, there, inside].astype(F32)
                    store(there, inside, total)

    def write(self, chunk):
        wide = self.tiles * self.tile
        return pltpu.make_async_copy(
            self.staged.at[chunk % 2],
            self.out_ref.at[:, pl.ds(pl.multiple_of(chunk * wide, LANES), wide)],
            self.store_sem.at[chunk % 2],
        )

    def run(self, stage, chunk):
        last = stage == self.stages
        slots = 2 if last else slots_of(stage)

        @pl.when(chunk >= slots)
        def _():
            if last:
                self.write(chunk - slots).wait()
            else:
                self.remote(stage, chunk - slots).wait_send()

        for copy in self.loads(stage, chunk):
            copy.wait()

        def store(there, inside, total):
            if last:
                self.staged[chunk % 2, there, inside] = total
            else:
                self.sent[stage][chunk % slots_of(stage), there, inside] = total.astype(BF16)

        self.product(stage, chunk, store)
        if last:
            self.write(chunk).start()
        else:
            self.remote(stage, chunk).start()

    def step(self, i, lags):
        for work in (self.begin, self.run):
            for stage, lag in enumerate(lags):
                if stage == 0 and work == self.begin:
                    continue

                @pl.when((i >= lag) & (i < self.count + lag))
                def _():
                    work(stage, i - lag)

    def drain(self):
        for stage in range(self.stages):
            for chunk in range(max(self.count - slots_of(stage), 0), self.count):
                self.remote(stage, chunk).wait_send()
        for chunk in range(max(self.count - 2, 0), self.count):
            self.write(chunk).wait()


class Streamed:
    def __init__(self, lefts, widths, weight_ref, weight_at, own_ref, other_ref, recv_sems, shared, aside=None):
        self.lefts, self.widths = lefts, widths
        self.weight_ref, self.weight_at = weight_ref, weight_at
        self.own_ref, self.other_ref, self.recv_sems, self.aside = own_ref, other_ref, recv_sems, aside
        self.slots, self.slot_sems, self.made, self.send_sems, self.own_sems = shared
        self.count, self.wide = self.made.shape[0], self.made.shape[2]

    def fetch(self, tile, piece):
        rows = pl.ds(pl.multiple_of(tile * self.wide, self.wide), self.wide)
        columns = pl.ds(self.weight_at + sum(self.widths[:piece]), self.widths[piece])
        slot = (tile * len(self.widths) + piece) % 2
        return pltpu.make_async_copy(
            self.weight_ref.at[rows, columns],
            self.slots.at[slot, :, pl.ds(0, self.widths[piece])],
            self.slot_sems.at[slot],
        )

    def columns(self, ref, tile):
        return ref.at[:, pl.ds(pl.multiple_of(tile * self.wide, self.wide), self.wide)]

    def keep(self, tile):
        return pltpu.make_async_copy(self.made.at[tile], self.columns(self.own_ref, tile), self.own_sems.at[tile])

    def send(self, tile):
        return pltpu.make_async_remote_copy(
            src_ref=self.made.at[tile],
            dst_ref=self.columns(self.other_ref, tile),
            send_sem=self.send_sems.at[tile],
            recv_sem=self.recv_sems.at[tile],
            device_id={"tensor": 1 - lax.axis_index("tensor")},
            device_id_type=MESH,
        )

    def run(self, first, number):
        @pl.when(first == 0)
        def _():
            self.fetch(0, 0).start()
            if self.aside:
                self.aside.fetch(0).start()

        @pl.loop(0, number)
        def _(k):
            tile = first + k
            more = tile + 1 < self.count
            total = 0.0
            for piece, (left, width) in enumerate(zip(self.lefts, self.widths)):
                self.fetch(tile, piece).wait()
                if piece + 1 < len(self.widths):
                    self.fetch(tile, piece + 1).start()
                else:

                    @pl.when(more)
                    def _():
                        self.fetch(tile + 1, 0).start()

                weights = self.slots[(tile * len(self.widths) + piece) % 2, :, pl.ds(0, width)]
                total = total + lax.dot_general(
                    left[...], weights, (((1,), (1,)), ((), ())), preferred_element_type=F32
                )
            self.made[tile] = total.astype(BF16)
            if self.aside:
                self.aside.fetch(tile).wait()

                @pl.when(more)
                def _():
                    self.aside.fetch(tile + 1).start()

                self.aside.use(tile, total)
            self.keep(tile).start()
            self.send(tile).start()

    def sent(self):
        @pl.loop(0, self.count)
        def _(tile):
            self.keep(tile).wait()
            self.send(tile).wait_send()

    def received(self):
        @pl.loop(0, self.count)
        def _(tile):
            self.send(tile).wait_recv()


class FirstGain:
    def __init__(self, tokens, scale_ref, slots, sems, target):
        self.tokens, self.scale_ref, self.slots, self.sems, self.target = tokens, scale_ref, slots, sems, target
        self.wide = slots.shape[2]

    def fetch(self, tile):
        columns = pl.ds(pl.multiple_of(tile * self.wide, self.wide), self.wide)
        return pltpu.make_async_copy(self.tokens.at[:, columns], self.slots.at[tile % 2], self.sems.at[tile % 2])

    def use(self, tile, grad):
        columns = pl.ds(pl.multiple_of(tile * self.wide, self.wide), self.wide)
        normal = self.slots[tile % 2].astype(F32) * self.scale_ref[...]
        self.target[0:1, columns] = jnp.sum(grad * normal, 0, keepdims=True)


class Smalls:
    def __init__(self, size, me, gconv_ref, gnorm_ref, ggain_ref, pair, sums, got, total_ref, sems):
        self.size, self.me, self.bits = size, me, orders(size)[0]
        self.gconv_ref, self.gnorm_ref, self.ggain_ref = gconv_ref, gnorm_ref, ggain_ref
        self.pair, self.sums, self.got, self.total_ref = pair, sums, got, total_ref
        self.pair_sems, self.send_sems, self.recv_sems = sems

    def across(self):
        return pltpu.make_async_remote_copy(
            src_ref=self.pair.at[0],
            dst_ref=self.pair.at[1],
            send_sem=self.pair_sems.at[0],
            recv_sem=self.pair_sems.at[1],
            device_id={"tensor": 1 - lax.axis_index("tensor")},
            device_id_type=MESH,
        )

    def swap(self, stage):
        return pltpu.make_async_remote_copy(
            src_ref=self.sums.at[stage],
            dst_ref=self.got.at[stage],
            send_sem=self.send_sems.at[stage],
            recv_sem=self.recv_sems.at[stage],
            device_id={"dp": flipped(self.me, self.bits[stage], self.size)},
            device_id_type=MESH,
        )

    def run(self, step):
        model, lanes = self.gnorm_ref.shape[1], self.ggain_ref.shape[1]

        @pl.when(step == 0)
        def _():
            self.pair[0, 1:2, 0:lanes] = self.ggain_ref[...]
            self.across().start()

        @pl.when(step == 1)
        def _():
            self.across().wait()
            self.sums[0, 0:4, 0 : self.gconv_ref.shape[1]] = self.gconv_ref[...]
            self.sums[0, 4:5, 0:model] = self.gnorm_ref[...]
            self.sums[0, 5:7, 0:model] = self.pair[0, 0:2] + self.pair[1, 0:2]
            self.swap(0).start()

        for stage in range(len(self.bits)):

            @pl.when(step == stage + 2)
            def _():
                self.swap(stage).wait()
                total = self.sums[stage] + self.got[stage]
                if stage + 1 < len(self.bits):
                    self.sums[stage + 1] = total
                    self.swap(stage + 1).start()
                else:
                    self.total_ref[...] = total


def backward_kernel(plan, *refs):
    size, heads, block_heads, units, passes, shapes = plan
    (up_t, second_t, first_t, ffn_right, mixed_hbm, conv_ref, gain_ref, norm_ref, w_mixer, w_ffn, qkv_hbm, out_hbm,
     fresh_hbm, state_hbm, solve_hbm, middle_hbm, upstream_hbm, tokens_hbm, scale_ref) = refs[:19]
    (ffn_out, mix_out, beta_out, gmiddle_hbm, gs_own, gs_other, final_own, final_other, gf_own, gf_other,
     small_ref) = refs[19:30]
    stages = len(orders(size)[0])
    landed_ffn, landed_mix, landed_beta = [refs[30 + k * stages : 30 + (k + 1) * stages] for k in range(3)]
    rest = list(refs[30 + 3 * stages :])
    take = lambda number: [rest.pop(0) for _ in range(number)]
    ffn_refs = list(landed_ffn) + take(2 * stages + 5)
    mix_refs = list(landed_mix) + take(2 * stages + 5)
    beta_refs = list(landed_beta) + take(2 * stages + 5)
    (lefts, mix_right, slots, slot_sems, made, send_sems, own_sems, recv_sems, w_out, grad_mixed, carry, ahead,
     place_sems, misc_sems, tile_sems, gconv_ref, ggain_ref, gnorm_ref, token_slots, token_sems, pair, sums, got,
     pair_sems, small_send, small_recv) = rest
    length = mix_right.shape[0]
    model = up_t.shape[0]
    block = model // size
    span = 3 * block_heads * WIDTH
    groups = heads // block_heads
    columns = heads * WIDTH
    raw_columns = groups * span + LANES
    count = length // CHUNK
    me = lax.axis_index("dp")

    barrier = pltpu.get_barrier_semaphore()
    peers = 1
    pl.semaphore_signal(barrier, inc=1, device_id={"tensor": 1 - lax.axis_index("tensor")}, device_id_type=MESH)
    for bit in orders(size)[0]:
        pl.semaphore_signal(barrier, inc=1, device_id={"dp": flipped(me, bit, size)}, device_id_type=MESH)
        peers += 1

    places = []
    for which, source in enumerate((up_t, second_t, first_t)):
        for place, bits in enumerate(offsets(size)):
            owner = pl.multiple_of(flipped(me, bits, size) * block, block)
            places.append(
                pltpu.make_async_copy(
                    source.at[pl.ds(owner, block)],
                    lefts.at[which, pl.ds(place * block, block)],
                    place_sems.at[which, place],
                )
            )
    for copy in places:
        copy.start()
    bring_mixed = pltpu.make_async_copy(mixed_hbm, mix_right.at[:, pl.ds(raw_columns, columns)], misc_sems.at[0])
    bring_mixed.start()
    bring_w_out = pltpu.make_async_copy(
        w_mixer.at[:, pl.ds(raw_columns, columns)], w_out, misc_sems.at[1]
    )
    bring_w_out.start()
    gconv_ref[...] = jnp.zeros_like(gconv_ref)
    ggain_ref[...] = jnp.zeros_like(ggain_ref)
    gnorm_ref[...] = jnp.zeros_like(gnorm_ref)
    pair[...] = jnp.zeros_like(pair)
    sums[...] = jnp.zeros_like(sums)
    strength_lanes = pl.ds(groups * span, LANES)
    mix_right[:, strength_lanes] = jnp.zeros((length, LANES), BF16)
    pl.semaphore_wait(barrier, peers)
    for copy in places:
        copy.wait()

    (ffn_count, ffn_tiles, ffn_tile), (mix_count, mix_tiles, mix_tile), _ = shapes
    per_matrix = units // ffn_tile

    def ffn_columns(at):
        return ffn_right[at // per_matrix, :, pl.ds(pl.multiple_of(at % per_matrix * ffn_tile, ffn_tile), ffn_tile)]

    ffn = Scatter(size, me, ffn_count, ffn_tiles, ffn_tile, lambda at: (at // per_matrix + 1) // 2, lefts, ffn_columns,
                  ffn_out, ffn_refs)
    raw_tiles = groups * span // mix_tile

    def mix_columns(at):
        return mix_right[:, pl.ds(pl.multiple_of(at * mix_tile + at // raw_tiles * LANES, LANES), mix_tile)]

    mix = Scatter(size, me, mix_count, mix_tiles, mix_tile, lambda at: 2 + at // raw_tiles, lefts, mix_columns,
                  mix_out, mix_refs)
    beta = Scatter(size, me, 1, 1, LANES, lambda at: 2, lefts, lambda at: mix_right[:, strength_lanes],
                   beta_out, beta_refs)
    shared = (slots, slot_sems, made, send_sems, own_sems)
    gs = Streamed([ffn_right.at[1], ffn_right.at[2]], [units] * 2, w_ffn, units, gs_own, gs_other, recv_sems.at[0],
                  shared)
    final = Streamed([ffn_right.at[0]], [units], w_ffn, 0, final_own, final_other, recv_sems.at[1], shared)
    gf = Streamed([mix_right.at[:, pl.ds(0, raw_columns)]], [raw_columns], w_mixer, 0, gf_own, gf_other,
                  recv_sems.at[2], shared, FirstGain(tokens_hbm, scale_ref, token_slots, token_sems, pair.at[0]))
    smalls = Smalls(size, me, gconv_ref, gnorm_ref, ggain_ref, pair, sums, got, small_ref,
                    (pair_sems, small_send, small_recv))

    def middle_part():
        gs.received()

        half = CHUNK // 2

        def scoped(own, other, middle, upstream, result, low, turned):
            def fetches(h, slot):
                rows = pl.ds(pl.multiple_of(h * half, half), half)
                return [
                    pltpu.make_async_copy(source.at[rows], target.at[slot], tile_sems.at[slot, k])
                    for k, (source, target) in enumerate(
                        ((gs_own, own), (gs_other, other), (middle_hbm, middle), (upstream_hbm, upstream))
                    )
                ]

            for copy in fetches(0, 0):
                copy.start()

            @pl.loop(0, count)
            def _(t):
                rows = pl.ds(pl.multiple_of(t * CHUNK, CHUNK), CHUNK)
                for slot in range(2):
                    for copy in fetches(2 * t + slot, slot):
                        copy.wait()

                    @pl.when(2 * t + slot + 1 < 2 * count)
                    def _():
                        for copy in fetches(2 * t + slot + 1, 1 - slot):
                            copy.start()

                    @pl.loop(0, half // 16)
                    def _(k):
                        here = pl.ds(pl.multiple_of(k * 16, 16), 16)
                        there = pl.ds(pl.multiple_of(slot * half + k * 16, 16), 16)
                        grad = own[slot, here].astype(F32) + other[slot, here].astype(F32)
                        values = middle[slot, here]
                        scale = lax.rsqrt(jnp.mean(values * values, -1, keepdims=True) + epsilon)
                        normal = values * scale
                        scaled = grad * norm_ref[...]
                        gnorm_ref[...] += jnp.sum(grad * normal, 0, keepdims=True)
                        total = upstream[slot, here].astype(F32) + scale * (
                            scaled - normal * jnp.mean(scaled * normal, -1, keepdims=True)
                        )
                        result[there] = total
                        low[there] = total.astype(BF16)

                write = pltpu.make_async_copy(result, gmiddle_hbm.at[rows], tile_sems.at[0, 4])
                write.start()
                grad_mixed[rows] = jnp.dot(low[...], w_out[...], preferred_element_type=F32)

                for k in range(model // LANES):
                    lanes = slice(k * LANES, (k + 1) * LANES)
                    turned[lanes, :] = result[:, lanes].T.astype(BF16)
                for place, bits in enumerate(offsets(size)):
                    owner = pl.multiple_of(flipped(me, bits, size) * block, block)
                    lefts[3, place * block : (place + 1) * block, rows] = turned[pl.ds(owner, block)]

                write.wait()

        pl.run_scoped(
            scoped,
            pltpu.VMEM((2, half, model), BF16),
            pltpu.VMEM((2, half, model), BF16),
            pltpu.VMEM((2, half, model), F32),
            pltpu.VMEM((2, half, model), BF16),
            pltpu.VMEM((CHUNK, model), F32),
            pltpu.VMEM((CHUNK, model), BF16),
            pltpu.VMEM((model, CHUNK), BF16),
        )

    def delta_parts(first):
        def scoped(cur, tail, beta, out, fresh, state, solve):
            def fetches(k):
                piece = first + k
                group, c = piece // count, count - 1 - piece % count
                rows = pl.ds(pl.multiple_of(c * CHUNK, CHUNK), CHUNK)
                before = pl.ds(pl.multiple_of((c * CHUNK + length - 8) % length // 8 * 8, 8), 8)
                lanes = pl.ds(pl.multiple_of(group * span, LANES), span)
                narrow = pl.ds(pl.multiple_of(group * block_heads * WIDTH, LANES), block_heads * WIDTH)
                ours = pl.ds(group * block_heads, block_heads)
                pairs = (
                    (qkv_hbm.at[rows, lanes], cur),
                    (qkv_hbm.at[before, lanes], tail),
                    (qkv_hbm.at[rows, strength_lanes], beta),
                    (out_hbm.at[rows, narrow], out),
                    (fresh_hbm.at[rows, narrow], fresh),
                    (state_hbm.at[ours, c], state),
                    (solve_hbm.at[ours, c], solve),
                )
                return [
                    pltpu.make_async_copy(source, target.at[k], tile_sems.at[k, place])
                    for place, (source, target) in enumerate(pairs)
                ]

            for k in range(2):

                @pl.when(first + k < pieces)
                def _():
                    for copy in fetches(k):
                        copy.start()

            @pl.loop(0, 2)
            def _(k):
                piece = first + k

                @pl.when(piece < pieces)
                def _():
                    @pl.when(piece % count == 0)
                    def _():
                        carry[...] = jnp.zeros_like(carry)
                        ahead[...] = jnp.zeros_like(ahead)

                    for copy in fetches(k):
                        copy.wait()
                    backward_piece(
                        block_heads, WIDTH, passes, piece // count, count - 1 - piece % count, cur.at[k], tail.at[k],
                        beta.at[k], conv_ref, gain_ref, grad_mixed, out.at[k], fresh.at[k], state.at[k], solve.at[k],
                        mix_right, mix_right.at[:, strength_lanes], gconv_ref, ggain_ref, carry, ahead,
                    )

        pl.run_scoped(
            scoped,
            pltpu.VMEM((2, CHUNK, span), F32),
            pltpu.VMEM((2, 8, span), F32),
            pltpu.VMEM((2, CHUNK, LANES), F32),
            pltpu.VMEM((2, CHUNK, block_heads * WIDTH), F32),
            pltpu.VMEM((2, CHUNK, block_heads * WIDTH), F32),
            pltpu.VMEM((2, block_heads, WIDTH, WIDTH), F32),
            pltpu.VMEM((2, block_heads, CHUNK, CHUNK), F32),
        )

    lags = [0, 1] + [4 + 3 * stage for stage in range(stages - 1)]
    quarter = gs.count // 4
    at_final, at_middle, at_delta = 16, 6, 7
    pieces = groups * count
    at_gf = at_delta + -(-pieces // 2)

    def step(i, carried):
        ffn.step(i, lags)
        mix.step(i - ffn_count - 0, lags)
        beta.step(i - at_gf - 1, lags)

        @pl.when(i < 4)
        def _():
            gs.run(i * quarter, quarter)

        @pl.when(i == at_middle)
        def _():
            gs.sent()
            bring_w_out.wait()
            bring_mixed.wait()
            middle_part()

        @pl.when((i >= at_delta) & (i < at_gf))
        def _():
            delta_parts((i - at_delta) * 2)

        @pl.when((i >= at_gf) & (i < at_gf + 4))
        def _():
            gf.run((i - at_gf) * quarter, quarter)

        smalls.run(i - at_gf - 4)

        @pl.when(i == at_final)
        def _():
            gf.sent()

        @pl.when((i >= at_final) & (i < at_final + 4))
        def _():
            final.run((i - at_final) * quarter, quarter)

        return carried

    steps = max(ffn_count + 0 + mix_count + lags[-1], at_final + 4, at_gf + 2 + lags[-1], at_gf + 6 + stages)
    lax.fori_loop(0, steps, step, 0)
    ffn.drain()
    mix.drain()
    beta.drain()
    final.sent()
    final.received()
    gf.received()


def pack_kernel(block, query_ref, key_ref, value_ref, beta_ref, out_ref, result_ref):
    span = block * WIDTH
    at = 0
    for group in range(query_ref.shape[1] // span):
        for part_ref in (query_ref, key_ref, value_ref):
            result_ref[:, at : at + span] = part_ref[:, group * span : (group + 1) * span].astype(BF16)
            at += span
    result_ref[:, at : at + LANES] = beta_ref[...].astype(BF16)
    at += LANES
    for begin in range(0, out_ref.shape[0], LANES):
        result_ref[:, at + begin : at + begin + LANES] = out_ref[begin : begin + LANES, :].T.astype(BF16)


def packed_mixer(block, w_query, w_key, w_value, w_beta, w_out):
    rows, columns = w_query.shape
    return pl.pallas_call(
        functools.partial(pack_kernel, block),
        out_shape=jax.ShapeDtypeStruct((rows, 4 * columns + LANES), BF16),
        name="packed_mixer",
    )(w_query, w_key, w_value, jnp.pad(w_beta, ((0, 0), (0, LANES - w_beta.shape[1]))), w_out)


def feed_forward_kernel(second_ref, upstream_ref, down_ref, gate_ref, up_ref, result_ref):
    part = 256
    for begin in range(0, second_ref.shape[0], part):
        rows = slice(begin, begin + part)
        gate = jnp.dot(second_ref[rows], gate_ref[...], preferred_element_type=F32)
        up = jnp.dot(second_ref[rows], up_ref[...], preferred_element_type=F32)
        grad_hidden = jnp.dot(upstream_ref[rows], down_ref[...], preferred_element_type=F32)
        sigma = sigmoid(gate)
        activated = gate * sigma
        result_ref[0, rows] = (activated * up).astype(BF16)
        result_ref[1, rows] = (grad_hidden * up * sigma * (1.0 + gate * (1.0 - sigma))).astype(BF16)
        result_ref[2, rows] = (grad_hidden * activated).astype(BF16)


def feed_forward(second, upstream, w_ffn):
    length, model = second.shape
    units = w_ffn.shape[1] // 3
    tile = 256 if units % 256 == 0 else 128
    tiles = units // tile
    whole = pl.BlockSpec((length, model), lambda j: (0, 0))
    weights = [pl.BlockSpec((model, tile), lambda j, k=k: (0, k * tiles + j)) for k in range(3)]
    return pl.pallas_call(
        feed_forward_kernel,
        grid=(tiles,),
        in_specs=[whole, whole] + weights,
        out_specs=pl.BlockSpec((3, length, tile), lambda j: (0, 0, j)),
        out_shape=jax.ShapeDtypeStruct((3, length, units), BF16),
        compiler_params=pltpu.CompilerParams(vmem_limit_bytes=32 * 2**20),
        name="feed_forward",
    )(second, upstream, w_ffn, w_ffn, w_ffn)


def backward_all(size, heads, block_heads, up_t, second_t, first_t, ffn_right, mixed, conv, gain, norm_ffn, w_mixer,
                 w_ffn, qkv, out, fresh, state, solve, middle, upstream, tokens, scale, passes=3):
    length = qkv.shape[0]
    model = up_t.shape[0]
    units = ffn_right.shape[2]
    block = model // size
    groups = heads // block_heads
    span = 3 * block_heads * WIDTH
    columns = heads * WIDTH
    raw_columns = groups * span + LANES
    mix_columns = raw_columns + columns
    ffn_tile = 256 if units % 256 == 0 else 128
    shapes = []
    mix_tile = 256 if columns % 256 == 0 else 128
    for total, tile in ((3 * units, ffn_tile), (4 * columns, mix_tile), (LANES, LANES)):
        tiles = next(t for t in (3, 2, 1) if total // tile % t == 0)
        shapes.append((total // tile // tiles, tiles, tile))
    landed, scratch = [], []
    for number, tiles, tile in shapes:
        more_landed, more_scratch = Scatter.scratch(size, block, number, tiles * tile)
        landed += more_landed
        scratch += more_scratch
    streamed = 256
    tiles = model // streamed
    stages = len(orders(size)[0])
    small_columns = max(groups * span, model)
    scratch += [
        pltpu.VMEM((4, model, length), BF16),
        pltpu.VMEM((length, mix_columns), BF16),
        pltpu.VMEM((2, streamed, max(units, raw_columns)), BF16),
        pltpu.SemaphoreType.DMA((2,)),
        pltpu.VMEM((tiles, length, streamed), BF16),
        pltpu.SemaphoreType.DMA((tiles,)),
        pltpu.SemaphoreType.DMA((tiles,)),
        pltpu.SemaphoreType.DMA((3, tiles)),
        pltpu.VMEM((model, columns), BF16),
        pltpu.VMEM((length, columns), F32),
        pltpu.VMEM((block_heads, WIDTH, WIDTH), F32),
        pltpu.VMEM((8, span), F32),
        pltpu.SemaphoreType.DMA((3, size)),
        pltpu.SemaphoreType.DMA((2,)),
        pltpu.SemaphoreType.DMA((2, 7)),
        pltpu.VMEM((4, groups * span), F32),
        pltpu.VMEM((1, WIDTH), F32),
        pltpu.VMEM((1, model), F32),
        pltpu.VMEM((2, length, streamed), BF16),
        pltpu.SemaphoreType.DMA((2,)),
        pltpu.VMEM((2, 8, model), F32),
        pltpu.VMEM((stages, 8, small_columns), F32),
        pltpu.VMEM((stages, 8, small_columns), F32),
        pltpu.SemaphoreType.DMA((2,)),
        pltpu.SemaphoreType.DMA((stages,)),
        pltpu.SemaphoreType.DMA((stages,)),
    ]
    vmem, hbm = pl.BlockSpec(memory_space=pltpu.VMEM), pl.BlockSpec(memory_space=pl.ANY)
    shape = jax.ShapeDtypeStruct
    exchanged = [shape((length, model), BF16)] * 6
    return pl.pallas_call(
        functools.partial(backward_kernel, (size, heads, block_heads, units, passes, shapes)),
        in_specs=[hbm] * 3 + [vmem, hbm] + [vmem] * 3 + [hbm] * 10 + [vmem],
        out_specs=[hbm] * 10 + [vmem] + [hbm] * len(landed),
        out_shape=[shape((block, 3 * units), F32), shape((block, 4 * columns), F32),
                   shape((block, LANES), F32), shape((length, model), F32)]
        + exchanged
        + [shape((8, small_columns), F32)]
        + landed,
        scratch_shapes=scratch,
        compiler_params=pltpu.CompilerParams(
            collective_id=0, has_side_effects=True, vmem_limit_bytes=63 * 2**20
        ),
        name="backward_all",
    )(up_t, second_t, first_t, ffn_right, mixed, conv, gain, norm_ffn, w_mixer, w_ffn, qkv, out, fresh, state, solve,
      middle, upstream, tokens, scale)[:11]


def matmul(left, right):
    return jnp.dot(left, right, preferred_element_type=F32)


def right_inner(left, right):
    return lax.dot_general(left, right, (((1,), (1,)), ((), ())), preferred_element_type=F32)


def row_norm(values, gain):
    return values * lax.rsqrt(jnp.mean(values * values, -1, keepdims=True) + epsilon) * gain


def swap(values, axis, size, by):
    return lax.ppermute(values, axis, [(d, d ^ by) for d in range(size)])


def exchange(partial):
    own = lax.reduce_precision(partial, 8, 7)
    return own, swap(own.astype(BF16), "tensor", 2, 1)


def by_groups(parts, block):
    span = block * WIDTH
    return [part[:, g * span : (g + 1) * span] for g in range(parts[0].shape[1] // span) for part in parts]


def from_groups(whole, block, index, columns):
    span = block * WIDTH
    return jnp.concatenate(
        [whole[:, (3 * g + index) * span : (3 * g + index + 1) * span] for g in range(columns // span)], 1
    )


def body(size, tokens, lengths, w_query, w_key, w_value, w_beta, conv_query, conv_key, conv_value, head_gain,
         w_out, norm_attn, norm_ffn, w_gate, w_up, w_down, cotangent):
    inputs = tokens.astype(F32)
    length, model = inputs.shape
    columns = w_query.shape[1]
    units = w_gate.shape[1]
    heads = w_beta.shape[1]
    block = 4 if heads % 4 == 0 else 1
    raw_columns = 3 * columns + LANES
    w_mixer = lax.all_gather(
        packed_mixer(block, w_query, w_key, w_value, w_beta, w_out), "dp", axis=0, tiled=True
    )
    w_ffn = lax.all_gather(
        jnp.concatenate([w_down.astype(BF16).T, w_gate.astype(BF16), w_up.astype(BF16)], 1), "dp", axis=0, tiled=True
    )
    conv = jnp.concatenate(by_groups([conv_query, conv_key, conv_value], block), 1)
    gain = head_gain[None]

    first_scale = lax.rsqrt(jnp.mean(inputs * inputs, -1, keepdims=True) + epsilon)
    first = (inputs * first_scale * norm_attn).astype(BF16)
    qkv = matmul(first, w_mixer[:, :raw_columns])
    mixed, out, fresh, state, solve = delta_forward(qkv, conv, gain, heads, block, (3, 3, 3, 3))
    own, other = exchange(right_inner(mixed, w_mixer[:, raw_columns:]))
    middle = inputs + (own + other.astype(F32))
    second = row_norm(middle, norm_ffn).astype(BF16)
    positions = lax.broadcasted_iota(jnp.int32, (length, 1), 0)
    valid = (positions < lengths[0]).astype(F32)
    upstream = (cotangent.astype(F32) * valid).astype(BF16)
    (ffn_grads, mixer_grads, beta_grads, grad_middle, _, _, final_own, final_other, first_own, first_other,
     small) = backward_all(
        size, heads, block, upstream.T, second.T, first.T,
        feed_forward(second, upstream, w_ffn),
        mixed, conv, gain, norm_ffn[None], w_mixer, w_ffn, qkv, out, fresh, state, solve, middle, upstream, tokens, first_scale,
    )
    final = middle + (final_own.astype(F32) + final_other.astype(F32))
    block_out = (final * valid).astype(BF16)
    normal = inputs * first_scale
    scaled = (first_own.astype(F32) + first_other.astype(F32)) * norm_attn
    grad_tokens = grad_middle + first_scale * (scaled - normal * jnp.mean(scaled * normal, -1, keepdims=True))
    convs = small[:4, : 3 * columns]
    return (
        block_out,
        grad_tokens,
        from_groups(mixer_grads, block, 0, columns),
        from_groups(mixer_grads, block, 1, columns),
        from_groups(mixer_grads, block, 2, columns),
        beta_grads[:, :heads],
        from_groups(convs, block, 0, columns),
        from_groups(convs, block, 1, columns),
        from_groups(convs, block, 2, columns),
        small[6, :WIDTH],
        mixer_grads[:, 3 * columns :].T,
        small[5, :model],
        small[4, :model],
        ffn_grads[:, units : 2 * units],
        ffn_grads[:, 2 * units :],
        ffn_grads[:, :units].T,
    )


def solution(mesh):
    rows, both, cols = P("dp", None), P("dp", "tensor"), P("tensor", "dp")
    taps = P(None, "tensor")
    in_specs = (rows, P("dp"), both, both, both, both, taps, taps, taps, P(), cols, P(), P(), both, both, cols, rows)
    out_specs = (rows, rows, both, both, both, both, taps, taps, taps, P(), cols, P(), P(), both, both, cols)
    return jax.shard_map(
        functools.partial(body, mesh.shape["dp"]), mesh=mesh, in_specs=in_specs, out_specs=out_specs, check_vma=False
    )
```

```python
import functools
import jax
import jax.numpy as jnp
from jax import lax
from jax.experimental import pallas as pl
from jax.experimental.pallas import tpu as pltpu
from jax.sharding import PartitionSpec as P

CHUNK = 128
WIDTH = 128
LANES = 128
epsilon = 1e-06
HIGH = lax.Precision.HIGHEST
F32 = jnp.float32
BF16 = jnp.bfloat16
MESH = pl.DeviceIdType.MESH


def dot(left, right, dims, passes):
    form = (dims, ((), ()))
    if passes == 6:
        return lax.dot_general(left, right, form, precision=HIGH, preferred_element_type=F32)
    left_hi, right_hi = left.astype(BF16), right.astype(BF16)
    total = lax.dot_general(left_hi, right_hi, form, preferred_element_type=F32)
    if passes == 3:
        left_lo = (left - left_hi.astype(F32)).astype(BF16)
        right_lo = (right - right_hi.astype(F32)).astype(BF16)
        total = total + (
            lax.dot_general(left_hi, right_lo, form, preferred_element_type=F32)
            + lax.dot_general(left_lo, right_hi, form, preferred_element_type=F32)
        )
    return total


def nn(left, right, passes):
    return dot(left, right, ((1,), (0,)), passes)


def nt(left, right, passes):
    return dot(left, right, ((1,), (1,)), passes)


def tn(left, right, passes):
    return dot(left, right, ((0,), (0,)), passes)


def sigmoid(x):
    return 1.0 / (1.0 + jnp.exp(-x))


def shift_down(cur, tail, by):
    rolled = pltpu.roll(cur, by, 0)
    rows = lax.broadcasted_iota(jnp.int32, tail.shape, 0)
    top = jnp.where(rows < by, pltpu.roll(tail, by, 0), rolled[:8])
    return jnp.concatenate([top, rolled[8:]], 0)


def shift_up(cur, head, by):
    size = cur.shape[0]
    rolled = pltpu.roll(cur, size - by, 0)
    rows = lax.broadcasted_iota(jnp.int32, head.shape, 0)
    bottom = jnp.where(rows >= 8 - by, pltpu.roll(head, 8 - by, 0), rolled[size - 8 :])
    return jnp.concatenate([rolled[: size - 8], bottom], 0)


def unit_scale(values):
    return lax.rsqrt(jnp.sum(values * values, -1, keepdims=True) + epsilon)


def masks(size):
    rows = lax.broadcasted_iota(jnp.int32, (size, size), 0)
    cols = lax.broadcasted_iota(jnp.int32, (size, size), 1)
    return rows, cols, rows ^ cols


def unit_lower_inverses(lowers, passes):
    size = lowers[0].shape[0]
    rows, cols, apart = masks(size)
    inverses = [jnp.where(rows == cols, 1.0, jnp.where(apart < 2, -lower, 0.0)) for lower in lowers]
    span = 2
    while span < size:
        corner = (apart < 2 * span) & (apart >= span)
        halves = [nn(jnp.where(corner, a, 0.0), x, passes) for a, x in zip(lowers, inverses)]
        inverses = [x - nn(x, half, passes) for x, half in zip(inverses, halves)]
        span *= 2
    return inverses


def pick(table, column):
    lanes = lax.broadcasted_iota(jnp.int32, table.shape, 1)
    return jnp.sum(jnp.where(lanes == column, table, 0.0), 1, keepdims=True)


def forward_kernel(heads, width, ps, qkv_ref, beta_ref, conv_ref, gain_ref,
                   mixed_ref, out_ref, fresh_ref, state_ref, solve_ref, carry):
    group = pl.program_id(0)
    chunk = CHUNK
    length = qkv_ref.shape[0]
    carry[...] = jnp.zeros_like(carry)
    p_gram, p_inv, p_state, p_out = ps

    def step(c, _):
        base = pl.multiple_of(c * chunk, chunk)
        rows = pl.ds(base, chunk)
        before = pl.ds(pl.multiple_of(jnp.maximum(base - 8, 0), 8), 8)
        beta = sigmoid(beta_ref[rows, :])
        row, col, _ = masks(chunk)
        gain = gain_ref[...]
        queries, keys, values, strengths = [], [], [], []
        for j in range(heads):
            parts = []
            for part in range(3):
                lanes = pl.ds((part * heads + j) * width, width)
                cur = qkv_ref[rows, lanes]
                tail = jnp.where(c > 0, qkv_ref[before, lanes], 0.0)
                taps = conv_ref[:, lanes]
                total = taps[3:4] * cur
                for by in (1, 2, 3):
                    total = total + taps[3 - by : 4 - by] * shift_down(cur, tail, by)
                parts.append(total * sigmoid(total))
            query, key, value = parts
            queries.append(query * (unit_scale(query) * width ** (-0.5)))
            keys.append(key * unit_scale(key))
            values.append(value)
            strengths.append(pick(beta, group * heads + j))
        grams = [nt(key, key, p_gram) for key in keys]
        solves = unit_lower_inverses(
            [jnp.where(row > col, gram * strength, 0.0) for gram, strength in zip(grams, strengths)], p_inv
        )
        states = [carry[j] for j in range(heads)]
        errors = [value - nn(key, state, p_state) for value, key, state in zip(values, keys, states)]
        freshes = [nn(solve, s * e, p_state) for solve, s, e in zip(solves, strengths, errors)]
        for j in range(heads):
            carry[j] = states[j] + tn(keys[j], freshes[j], p_state)
        scores = [jnp.where(row >= col, nt(q, k, p_out), 0.0) for q, k in zip(queries, keys)]
        outs = [
            nn(q, s, p_out) + nn(score, f, p_out) for q, s, score, f in zip(queries, states, scores, freshes)
        ]
        for j, out in enumerate(outs):
            state_ref[j, c] = states[j]
            solve_ref[j, c] = solves[j]
            lanes = pl.ds(j * width, width)
            fresh_ref[rows, lanes] = freshes[j]
            out_ref[rows, lanes] = out
            scale = lax.rsqrt(jnp.mean(out * out, -1, keepdims=True) + epsilon)
            mixed_ref[rows, lanes] = (out * scale * gain).astype(BF16)
        return 0

    lax.fori_loop(0, length // chunk, step, 0)


def delta_forward(qkv, conv, gain, heads, block, ps=(6, 6, 6, 6)):
    length = qkv.shape[0]
    width = gain.shape[1]
    groups = heads // block
    span = 3 * block * width
    last = groups * span // 128
    count = length // CHUNK
    return pl.pallas_call(
        functools.partial(forward_kernel, block, width, ps),
        grid=(groups,),
        in_specs=[
            pl.BlockSpec((length, span), lambda g: (0, g)),
            pl.BlockSpec((length, 128), lambda g: (0, last)),
            pl.BlockSpec((4, span), lambda g: (0, g)),
            pl.BlockSpec((1, width), lambda g: (0, 0)),
        ],
        out_specs=[
            pl.BlockSpec((length, block * width), lambda g: (0, g)),
            pl.BlockSpec((length, block * width), lambda g: (0, g)),
            pl.BlockSpec((length, block * width), lambda g: (0, g)),
            pl.BlockSpec((block, count, width, width), lambda g: (g, 0, 0, 0)),
            pl.BlockSpec((block, count, CHUNK, CHUNK), lambda g: (g, 0, 0, 0)),
        ],
        out_shape=[
            jax.ShapeDtypeStruct((length, heads * width), BF16),
            jax.ShapeDtypeStruct((length, heads * width), F32),
            jax.ShapeDtypeStruct((length, heads * width), F32),
            jax.ShapeDtypeStruct((heads, count, width, width), F32),
            jax.ShapeDtypeStruct((heads, count, CHUNK, CHUNK), F32),
        ],
        scratch_shapes=[pltpu.VMEM((block, width, width), F32)],
        compiler_params=pltpu.CompilerParams(vmem_limit_bytes=48 * 2**20),
        name="delta_forward",
    )(qkv, qkv, conv, gain)


def backward_piece(heads, width, passes, group, c, cur_ref, tail_ref, beta_ref, conv_ref, gain_ref, grad_ref, out_ref,
                   fresh_ref, state_ref, solve_ref, raw_ref, gbeta_ref, gconv_ref, ggain_ref, carry, ahead):
    chunk = CHUNK
    span = 3 * heads * width
    rows = pl.ds(pl.multiple_of(c * chunk, chunk), chunk)
    beta = sigmoid(beta_ref[...])
    row, col, _ = masks(chunk)
    gain = gain_ref[...]
    lane = lax.broadcasted_iota(jnp.int32, beta.shape, 1)
    every = range(heads)

    def lanes_of(part, j):
        return pl.ds((part * heads + j) * width, width)

    def wide_lanes(part, j):
        return pl.ds(pl.multiple_of(group * span + (part * heads + j) * width, width), width)

    def before_silu(part, j, keep):
        cur = cur_ref[:, lanes_of(part, j)]
        tail = jnp.where(c > 0, tail_ref[:, lanes_of(part, j)], 0.0)
        taps = conv_ref[:, wide_lanes(part, j)]
        moved = [cur] + [shift_down(cur, tail, by) for by in (1, 2, 3)]
        total = taps[3:4] * cur
        for by in (1, 2, 3):
            total = total + taps[3 - by : 4 - by] * moved[by]
        return moved if keep else total

    queries, keys, errors, strengths, grad_outs, freshes = [], [], [], [], [], []
    ggain = jnp.zeros_like(gain)
    for j in every:
        acts = []
        for part in range(3):
            pre = before_silu(part, j, False)
            acts.append(pre * sigmoid(pre))
        queries.append(acts[0] * (unit_scale(acts[0]) * width ** (-0.5)))
        keys.append(acts[1] * unit_scale(acts[1]))
        errors.append(acts[2])
        strengths.append(pick(beta, group * heads + j))
        lanes = pl.ds(j * width, width)
        out = out_ref[:, lanes]
        freshes.append(fresh_ref[:, lanes])
        grad_mixed = grad_ref[rows, pl.ds(pl.multiple_of((group * heads + j) * width, width), width)]
        scale = lax.rsqrt(jnp.mean(out * out, -1, keepdims=True) + epsilon)
        normal = out * scale
        ggain = ggain + jnp.sum(grad_mixed * normal, 0, keepdims=True)
        scaled = grad_mixed * gain
        grad_outs.append(scale * (scaled - normal * jnp.mean(scaled * normal, -1, keepdims=True)))
    ggain_ref[...] += ggain

    scores = [jnp.where(row >= col, nt(queries[j], keys[j], passes), 0.0) for j in every]
    grad_freshes = [tn(scores[j], grad_outs[j], passes) + nn(keys[j], carry[j], passes) for j in every]
    pulled = [tn(solve_ref[j], grad_freshes[j], passes) for j in every]
    grad_errors = [strengths[j] * pulled[j] for j in every]
    grad_keys = [nt(freshes[j], carry[j], passes) - nt(grad_errors[j], state_ref[j], passes) for j in every]
    for j in every:
        carry[j] = carry[j] + (tn(queries[j], grad_outs[j], passes) - tn(keys[j], grad_errors[j], passes))
    grams = [nt(keys[j], keys[j], passes) for j in every]
    errors = [errors[j] - nn(keys[j], state_ref[j], passes) for j in every]
    grad_scores = [jnp.where(row >= col, nt(grad_outs[j], freshes[j], passes), 0.0) for j in every]
    grad_lowers = [jnp.where(row > col, -nt(pulled[j], freshes[j], passes), 0.0) for j in every]
    grad_queries = [nt(grad_outs[j], state_ref[j], passes) + nn(grad_scores[j], keys[j], passes) for j in every]
    grad_grams = [grad_lowers[j] * strengths[j] for j in every]
    grad_keys = [
        grad_keys[j] + tn(grad_scores[j], queries[j], passes) + nn(grad_grams[j] + grad_grams[j].T, keys[j], passes)
        for j in every
    ]
    gbeta = jnp.zeros(beta.shape, F32)
    for j in every:
        grad_strength = jnp.sum(pulled[j] * errors[j] + grad_lowers[j] * grams[j], -1, keepdims=True)
        grad_strength = grad_strength * (strengths[j] * (1.0 - strengths[j]))
        gbeta = jnp.where(lane == group * heads + j, grad_strength, gbeta)
    gbeta_ref[rows, :] += gbeta.astype(BF16)

    for j in every:
        for part in range(3):
            moved = before_silu(part, j, True)
            taps = conv_ref[:, wide_lanes(part, j)]
            pre = taps[3:4] * moved[0]
            for by in (1, 2, 3):
                pre = pre + taps[3 - by : 4 - by] * moved[by]
            gate = sigmoid(pre)
            act = pre * gate
            if part == 0:
                scale = unit_scale(act)
                unit = act * scale
                grad = grad_queries[j] * width ** (-0.5)
                grad = scale * (grad - unit * jnp.sum(grad * unit, -1, keepdims=True))
            elif part == 1:
                grad = grad_keys[j]
                unit = keys[j]
                grad = unit_scale(act) * (grad - unit * jnp.sum(grad * unit, -1, keepdims=True))
            else:
                grad = grad_errors[j]
            grad = grad * gate * (1.0 + pre * (1.0 - gate))
            after = ahead[:, lanes_of(part, j)]
            total = taps[3:4] * grad
            for by in (1, 2, 3):
                total = total + taps[3 - by : 4 - by] * shift_up(grad, after, by)
            raw_ref[rows, wide_lanes(part, j)] = total.astype(BF16)
            ahead[:, lanes_of(part, j)] = grad[:8]
            sums = [jnp.sum(grad * moved[3 - tap], 0, keepdims=True) for tap in range(4)]
            gconv_ref[:, wide_lanes(part, j)] += jnp.concatenate(sums, 0)


def orders(size):
    bits, unit = [], 1
    while unit < size:
        bits.append(unit)
        unit *= 2
    return bits, bits[:1] + bits[2:] + bits[1:2]


def offsets(size):
    found = [0]
    for bit in orders(size)[0]:
        found = [old + value for old in found for value in (0, bit)]
    return found


def flipped(index, bits, size):
    result, unit = 0, 1
    while unit < size:
        result = result + (index // unit + bits // unit) % 2 * unit
        unit *= 2
    return result


def sent_places(size):
    owners = offsets(size)
    tables = []
    for order in orders(size):
        held, table = list(range(size)), []
        for bit in order:
            table.append([place for place in held if owners[place] & bit])
            held = [place for place in held if not owners[place] & bit]
        tables.append(table)
    stages = []
    for both in zip(*tables):
        length = len(both[0])
        while not all(
            places[at : at + length] == list(range(places[at], places[at] + length))
            for places in both
            for at in range(0, len(places), length)
        ):
            length //= 2
        stages.append((length, [places[::length] for places in both]))
    return stages, tables


def slots_of(stage):
    return 3 if stage == 1 else 2


class Scatter:
    def __init__(self, size, me, count, tiles, tile, which, left_ref, right_of, out_ref, refs):
        self.orders = orders(size)
        self.stages = stages = len(self.orders[0])
        self.runs, self.tables = sent_places(size)
        self.owners = offsets(size)
        self.size, self.me, self.count, self.tiles, self.tile, self.which = size, me, count, tiles, tile, which
        self.left_ref, self.right_of, self.out_ref = left_ref, right_of, out_ref
        self.landed, self.sent, self.early = refs[:stages], refs[stages : 2 * stages], refs[2 * stages : 3 * stages]
        self.send_sems, self.recv_sems, self.load_sems, self.staged, self.store_sem = refs[3 * stages : 3 * stages + 5]
        self.block = left_ref.shape[1] // size

    @staticmethod
    def scratch(size, block, count, wide):
        stages = len(orders(size)[0])
        sends = [(size >> (stage + 1)) * block for stage in range(stages)]
        landed = [jax.ShapeDtypeStruct((count, rows, wide), BF16) for rows in sends]
        rest = (
            [pltpu.VMEM((slots_of(stage), rows, wide), BF16) for stage, rows in enumerate(sends)]
            + [pltpu.VMEM((stage + 1, rows, wide), BF16) for stage, rows in enumerate(sends[1:] + [block])]
            + [
                pltpu.SemaphoreType.DMA((slots_of(1), stages)),
                pltpu.SemaphoreType.DMA((count, stages)),
                pltpu.SemaphoreType.DMA((stages, 2 * stages)),
                pltpu.VMEM((2, block, wide), F32),
                pltpu.SemaphoreType.DMA((2,)),
            ]
        )
        return landed, rest

    @staticmethod
    def other_order(chunk):
        return (chunk + 3) % 6 // 5

    def chosen(self, chunk, pair):
        first, second = pair
        return first if first == second else first + self.other_order(chunk) * (second - first)

    def remote(self, stage, chunk):
        bit = self.chosen(chunk, [order[stage] for order in self.orders])
        return pltpu.make_async_remote_copy(
            src_ref=self.sent[stage].at[chunk % slots_of(stage)],
            dst_ref=self.landed[stage].at[chunk],
            send_sem=self.send_sems.at[chunk % slots_of(stage), stage],
            recv_sem=self.recv_sems.at[chunk, stage],
            device_id={"dp": flipped(self.me, bit, self.size)},
            device_id_type=MESH,
        )

    def places(self, stage):
        return self.runs[stage] if stage < self.stages else (1, [[0], [0]])

    def loads(self, stage, chunk):
        length, both = self.places(stage)
        rows = length * self.block
        copies = []
        for early in range(stage):
            for k in range(len(both[0])):
                found = []
                for order in range(2):
                    bit = self.orders[order][early]
                    wanted = self.owners[both[order][k]] | bit
                    found.append([self.owners[p] for p in self.tables[order][early]].index(wanted))
                at = pl.multiple_of(self.chosen(chunk, found) * self.block, self.block)
                copies.append(
                    pltpu.make_async_copy(
                        self.landed[early].at[chunk, pl.ds(at, rows)],
                        self.early[stage - 1].at[early, pl.ds(k * rows, rows)],
                        self.load_sems.at[stage - 1, len(copies)],
                    )
                )
        return copies

    def begin(self, stage, chunk):
        self.remote(stage - 1, chunk).wait_recv()
        for copy in self.loads(stage, chunk):
            copy.start()

    def product(self, stage, chunk, store):
        tile = self.tile
        length, both = self.places(stage)
        rows = length * self.block
        part = rows if rows <= 512 else 512

        for t in range(self.tiles):
            at = chunk * self.tiles + t
            right = self.right_of(at)
            inside = slice(t * tile, (t + 1) * tile)
            for k, pair in enumerate(zip(*both)):
                first = self.chosen(chunk, pair) * self.block
                for begin in range(0, rows, part):
                    here = pl.ds(pl.multiple_of(first + begin, self.block), part)
                    there = slice(k * rows + begin, k * rows + begin + part)
                    total = jnp.dot(self.left_ref[self.which(at), here, :], right, preferred_element_type=F32)
                    for early in range(stage):
                        total = total + self.early[stage - 1][early, there, inside].astype(F32)
                    store(there, inside, total)

    def write(self, chunk):
        wide = self.tiles * self.tile
        return pltpu.make_async_copy(
            self.staged.at[chunk % 2],
            self.out_ref.at[:, pl.ds(pl.multiple_of(chunk * wide, LANES), wide)],
            self.store_sem.at[chunk % 2],
        )

    def run(self, stage, chunk):
        last = stage == self.stages
        slots = 2 if last else slots_of(stage)

        @pl.when(chunk >= slots)
        def _():
            if last:
                self.write(chunk - slots).wait()
            else:
                self.remote(stage, chunk - slots).wait_send()

        for copy in self.loads(stage, chunk):
            copy.wait()

        def store(there, inside, total):
            if last:
                self.staged[chunk % 2, there, inside] = total
            else:
                self.sent[stage][chunk % slots_of(stage), there, inside] = total.astype(BF16)

        self.product(stage, chunk, store)
        if last:
            self.write(chunk).start()
        else:
            self.remote(stage, chunk).start()

    def step(self, i, lags):
        for work in (self.begin, self.run):
            for stage, lag in enumerate(lags):
                if stage == 0 and work == self.begin:
                    continue

                @pl.when((i >= lag) & (i < self.count + lag))
                def _():
                    work(stage, i - lag)

    def drain(self):
        for stage in range(self.stages):
            for chunk in range(max(self.count - slots_of(stage), 0), self.count):
                self.remote(stage, chunk).wait_send()
        for chunk in range(max(self.count - 2, 0), self.count):
            self.write(chunk).wait()


class Streamed:
    def __init__(self, lefts, widths, weight_ref, weight_at, own_ref, other_ref, recv_sems, shared, aside=None):
        self.lefts, self.widths = lefts, widths
        self.weight_ref, self.weight_at = weight_ref, weight_at
        self.own_ref, self.other_ref, self.recv_sems, self.aside = own_ref, other_ref, recv_sems, aside
        self.slots, self.slot_sems, self.made, self.send_sems, self.own_sems = shared
        self.count, self.wide = self.made.shape[0], self.made.shape[2]

    def fetch(self, tile, piece):
        rows = pl.ds(pl.multiple_of(tile * self.wide, self.wide), self.wide)
        columns = pl.ds(self.weight_at + sum(self.widths[:piece]), self.widths[piece])
        slot = (tile * len(self.widths) + piece) % 2
        return pltpu.make_async_copy(
            self.weight_ref.at[rows, columns],
            self.slots.at[slot, :, pl.ds(0, self.widths[piece])],
            self.slot_sems.at[slot],
        )

    def columns(self, ref, tile):
        return ref.at[:, pl.ds(pl.multiple_of(tile * self.wide, self.wide), self.wide)]

    def keep(self, tile):
        return pltpu.make_async_copy(self.made.at[tile], self.columns(self.own_ref, tile), self.own_sems.at[tile])

    def send(self, tile):
        return pltpu.make_async_remote_copy(
            src_ref=self.made.at[tile],
            dst_ref=self.columns(self.other_ref, tile),
            send_sem=self.send_sems.at[tile],
            recv_sem=self.recv_sems.at[tile],
            device_id={"tensor": 1 - lax.axis_index("tensor")},
            device_id_type=MESH,
        )

    def run(self, first, number):
        @pl.when(first == 0)
        def _():
            self.fetch(0, 0).start()
            if self.aside:
                self.aside.fetch(0).start()

        @pl.loop(0, number)
        def _(k):
            tile = first + k
            more = tile + 1 < self.count
            total = 0.0
            for piece, (left, width) in enumerate(zip(self.lefts, self.widths)):
                self.fetch(tile, piece).wait()
                if piece + 1 < len(self.widths):
                    self.fetch(tile, piece + 1).start()
                else:

                    @pl.when(more)
                    def _():
                        self.fetch(tile + 1, 0).start()

                weights = self.slots[(tile * len(self.widths) + piece) % 2, :, pl.ds(0, width)]
                total = total + lax.dot_general(
                    left[...], weights, (((1,), (1,)), ((), ())), preferred_element_type=F32
                )
            self.made[tile] = total.astype(BF16)
            if self.aside:
                self.aside.fetch(tile).wait()

                @pl.when(more)
                def _():
                    self.aside.fetch(tile + 1).start()

                self.aside.use(tile, total)
            self.keep(tile).start()
            self.send(tile).start()

    def sent(self):
        @pl.loop(0, self.count)
        def _(tile):
            self.keep(tile).wait()
            self.send(tile).wait_send()

    def received(self):
        @pl.loop(0, self.count)
        def _(tile):
            self.send(tile).wait_recv()


class FirstGain:
    def __init__(self, tokens, scale_ref, slots, sems, target):
        self.tokens, self.scale_ref, self.slots, self.sems, self.target = tokens, scale_ref, slots, sems, target
        self.wide = slots.shape[2]

    def fetch(self, tile):
        columns = pl.ds(pl.multiple_of(tile * self.wide, self.wide), self.wide)
        return pltpu.make_async_copy(self.tokens.at[:, columns], self.slots.at[tile % 2], self.sems.at[tile % 2])

    def use(self, tile, grad):
        columns = pl.ds(pl.multiple_of(tile * self.wide, self.wide), self.wide)
        normal = self.slots[tile % 2].astype(F32) * self.scale_ref[...]
        self.target[0:1, columns] = jnp.sum(grad * normal, 0, keepdims=True)


class Smalls:
    def __init__(self, size, me, gconv_ref, gnorm_ref, ggain_ref, pair, sums, got, total_ref, sems):
        self.size, self.me, self.bits = size, me, orders(size)[0]
        self.gconv_ref, self.gnorm_ref, self.ggain_ref = gconv_ref, gnorm_ref, ggain_ref
        self.pair, self.sums, self.got, self.total_ref = pair, sums, got, total_ref
        self.pair_sems, self.send_sems, self.recv_sems = sems

    def across(self):
        return pltpu.make_async_remote_copy(
            src_ref=self.pair.at[0],
            dst_ref=self.pair.at[1],
            send_sem=self.pair_sems.at[0],
            recv_sem=self.pair_sems.at[1],
            device_id={"tensor": 1 - lax.axis_index("tensor")},
            device_id_type=MESH,
        )

    def swap(self, stage):
        return pltpu.make_async_remote_copy(
            src_ref=self.sums.at[stage],
            dst_ref=self.got.at[stage],
            send_sem=self.send_sems.at[stage],
            recv_sem=self.recv_sems.at[stage],
            device_id={"dp": flipped(self.me, self.bits[stage], self.size)},
            device_id_type=MESH,
        )

    def run(self, step):
        model, lanes = self.gnorm_ref.shape[1], self.ggain_ref.shape[1]

        @pl.when(step == 0)
        def _():
            self.pair[0, 1:2, 0:lanes] = self.ggain_ref[...]
            self.across().start()

        @pl.when(step == 1)
        def _():
            self.across().wait()
            self.sums[0, 0:4, 0 : self.gconv_ref.shape[1]] = self.gconv_ref[...]
            self.sums[0, 4:5, 0:model] = self.gnorm_ref[...]
            self.sums[0, 5:7, 0:model] = self.pair[0, 0:2] + self.pair[1, 0:2]
            self.swap(0).start()

        for stage in range(len(self.bits)):

            @pl.when(step == stage + 2)
            def _():
                self.swap(stage).wait()
                total = self.sums[stage] + self.got[stage]
                if stage + 1 < len(self.bits):
                    self.sums[stage + 1] = total
                    self.swap(stage + 1).start()
                else:
                    self.total_ref[...] = total


def backward_kernel(plan, *refs):
    size, heads, block_heads, units, passes, shapes = plan
    (up_t, second_t, first_t, ffn_right, mixed_hbm, conv_ref, gain_ref, norm_ref, w_mixer, w_ffn, qkv_hbm, out_hbm,
     fresh_hbm, state_hbm, solve_hbm, middle_hbm, upstream_hbm, tokens_hbm, scale_ref) = refs[:19]
    (ffn_out, mix_out, beta_out, gmiddle_hbm, gs_own, gs_other, final_own, final_other, gf_own, gf_other,
     small_ref) = refs[19:30]
    stages = len(orders(size)[0])
    landed_ffn, landed_mix, landed_beta = [refs[30 + k * stages : 30 + (k + 1) * stages] for k in range(3)]
    rest = list(refs[30 + 3 * stages :])
    take = lambda number: [rest.pop(0) for _ in range(number)]
    ffn_refs = list(landed_ffn) + take(2 * stages + 5)
    mix_refs = list(landed_mix) + take(2 * stages + 5)
    beta_refs = list(landed_beta) + take(2 * stages + 5)
    (lefts, mix_right, slots, slot_sems, made, send_sems, own_sems, recv_sems, w_out, grad_mixed, carry, ahead,
     place_sems, misc_sems, tile_sems, gconv_ref, ggain_ref, gnorm_ref, token_slots, token_sems, pair, sums, got,
     pair_sems, small_send, small_recv) = rest
    length = mix_right.shape[0]
    model = up_t.shape[0]
    block = model // size
    span = 3 * block_heads * WIDTH
    groups = heads // block_heads
    columns = heads * WIDTH
    raw_columns = groups * span + LANES
    count = length // CHUNK
    me = lax.axis_index("dp")

    barrier = pltpu.get_barrier_semaphore()
    peers = 1
    pl.semaphore_signal(barrier, inc=1, device_id={"tensor": 1 - lax.axis_index("tensor")}, device_id_type=MESH)
    for bit in orders(size)[0]:
        pl.semaphore_signal(barrier, inc=1, device_id={"dp": flipped(me, bit, size)}, device_id_type=MESH)
        peers += 1

    places = []
    for which, source in enumerate((up_t, second_t, first_t)):
        for place, bits in enumerate(offsets(size)):
            owner = pl.multiple_of(flipped(me, bits, size) * block, block)
            places.append(
                pltpu.make_async_copy(
                    source.at[pl.ds(owner, block)],
                    lefts.at[which, pl.ds(place * block, block)],
                    place_sems.at[which, place],
                )
            )
    for copy in places:
        copy.start()
    bring_mixed = pltpu.make_async_copy(mixed_hbm, mix_right.at[:, pl.ds(raw_columns, columns)], misc_sems.at[0])
    bring_mixed.start()
    bring_w_out = pltpu.make_async_copy(
        w_mixer.at[:, pl.ds(raw_columns, columns)], w_out, misc_sems.at[1]
    )
    bring_w_out.start()
    gconv_ref[...] = jnp.zeros_like(gconv_ref)
    ggain_ref[...] = jnp.zeros_like(ggain_ref)
    gnorm_ref[...] = jnp.zeros_like(gnorm_ref)
    pair[...] = jnp.zeros_like(pair)
    sums[...] = jnp.zeros_like(sums)
    strength_lanes = pl.ds(groups * span, LANES)
    mix_right[:, strength_lanes] = jnp.zeros((length, LANES), BF16)
    pl.semaphore_wait(barrier, peers)
    for copy in places:
        copy.wait()

    (ffn_count, ffn_tiles, ffn_tile), (mix_count, mix_tiles, mix_tile), _ = shapes
    per_matrix = units // ffn_tile

    def ffn_columns(at):
        return ffn_right[at // per_matrix, :, pl.ds(pl.multiple_of(at % per_matrix * ffn_tile, ffn_tile), ffn_tile)]

    ffn = Scatter(size, me, ffn_count, ffn_tiles, ffn_tile, lambda at: (at // per_matrix + 1) // 2, lefts, ffn_columns,
                  ffn_out, ffn_refs)
    raw_tiles = groups * span // mix_tile

    def mix_columns(at):
        return mix_right[:, pl.ds(pl.multiple_of(at * mix_tile + at // raw_tiles * LANES, LANES), mix_tile)]

    mix = Scatter(size, me, mix_count, mix_tiles, mix_tile, lambda at: 2 + at // raw_tiles, lefts, mix_columns,
                  mix_out, mix_refs)
    beta = Scatter(size, me, 1, 1, LANES, lambda at: 2, lefts, lambda at: mix_right[:, strength_lanes],
                   beta_out, beta_refs)
    shared = (slots, slot_sems, made, send_sems, own_sems)
    gs = Streamed([ffn_right.at[1], ffn_right.at[2]], [units] * 2, w_ffn, units, gs_own, gs_other, recv_sems.at[0],
                  shared)
    final = Streamed([ffn_right.at[0]], [units], w_ffn, 0, final_own, final_other, recv_sems.at[1], shared)
    gf = Streamed([mix_right.at[:, pl.ds(0, raw_columns)]], [raw_columns], w_mixer, 0, gf_own, gf_other,
                  recv_sems.at[2], shared, FirstGain(tokens_hbm, scale_ref, token_slots, token_sems, pair.at[0]))
    smalls = Smalls(size, me, gconv_ref, gnorm_ref, ggain_ref, pair, sums, got, small_ref,
                    (pair_sems, small_send, small_recv))

    def middle_part():
        gs.received()

        half = CHUNK // 2

        def scoped(own, other, middle, upstream, result, low, turned):
            def fetches(h, slot):
                rows = pl.ds(pl.multiple_of(h * half, half), half)
                return [
                    pltpu.make_async_copy(source.at[rows], target.at[slot], tile_sems.at[slot, k])
                    for k, (source, target) in enumerate(
                        ((gs_own, own), (gs_other, other), (middle_hbm, middle), (upstream_hbm, upstream))
                    )
                ]

            for copy in fetches(0, 0):
                copy.start()

            @pl.loop(0, count)
            def _(t):
                rows = pl.ds(pl.multiple_of(t * CHUNK, CHUNK), CHUNK)
                for slot in range(2):
                    for copy in fetches(2 * t + slot, slot):
                        copy.wait()

                    @pl.when(2 * t + slot + 1 < 2 * count)
                    def _():
                        for copy in fetches(2 * t + slot + 1, 1 - slot):
                            copy.start()

                    @pl.loop(0, half // 16)
                    def _(k):
                        here = pl.ds(pl.multiple_of(k * 16, 16), 16)
                        there = pl.ds(pl.multiple_of(slot * half + k * 16, 16), 16)
                        grad = own[slot, here].astype(F32) + other[slot, here].astype(F32)
                        values = middle[slot, here]
                        scale = lax.rsqrt(jnp.mean(values * values, -1, keepdims=True) + epsilon)
                        normal = values * scale
                        scaled = grad * norm_ref[...]
                        gnorm_ref[...] += jnp.sum(grad * normal, 0, keepdims=True)
                        total = upstream[slot, here].astype(F32) + scale * (
                            scaled - normal * jnp.mean(scaled * normal, -1, keepdims=True)
                        )
                        result[there] = total
                        low[there] = total.astype(BF16)

                write = pltpu.make_async_copy(result, gmiddle_hbm.at[rows], tile_sems.at[0, 4])
                write.start()
                grad_mixed[rows] = jnp.dot(low[...], w_out[...], preferred_element_type=F32)

                for k in range(model // LANES):
                    lanes = slice(k * LANES, (k + 1) * LANES)
                    turned[lanes, :] = result[:, lanes].T.astype(BF16)
                for place, bits in enumerate(offsets(size)):
                    owner = pl.multiple_of(flipped(me, bits, size) * block, block)
                    lefts[3, place * block : (place + 1) * block, rows] = turned[pl.ds(owner, block)]

                write.wait()

        pl.run_scoped(
            scoped,
            pltpu.VMEM((2, half, model), BF16),
            pltpu.VMEM((2, half, model), BF16),
            pltpu.VMEM((2, half, model), F32),
            pltpu.VMEM((2, half, model), BF16),
            pltpu.VMEM((CHUNK, model), F32),
            pltpu.VMEM((CHUNK, model), BF16),
            pltpu.VMEM((model, CHUNK), BF16),
        )

    def delta_parts(first):
        def scoped(cur, tail, beta, out, fresh, state, solve):
            def fetches(k):
                piece = first + k
                group, c = piece // count, count - 1 - piece % count
                rows = pl.ds(pl.multiple_of(c * CHUNK, CHUNK), CHUNK)
                before = pl.ds(pl.multiple_of((c * CHUNK + length - 8) % length // 8 * 8, 8), 8)
                lanes = pl.ds(pl.multiple_of(group * span, LANES), span)
                narrow = pl.ds(pl.multiple_of(group * block_heads * WIDTH, LANES), block_heads * WIDTH)
                ours = pl.ds(group * block_heads, block_heads)
                pairs = (
                    (qkv_hbm.at[rows, lanes], cur),
                    (qkv_hbm.at[before, lanes], tail),
                    (qkv_hbm.at[rows, strength_lanes], beta),
                    (out_hbm.at[rows, narrow], out),
                    (fresh_hbm.at[rows, narrow], fresh),
                    (state_hbm.at[ours, c], state),
                    (solve_hbm.at[ours, c], solve),
                )
                return [
                    pltpu.make_async_copy(source, target.at[k], tile_sems.at[k, place])
                    for place, (source, target) in enumerate(pairs)
                ]

            for k in range(2):

                @pl.when(first + k < pieces)
                def _():
                    for copy in fetches(k):
                        copy.start()

            @pl.loop(0, 2)
            def _(k):
                piece = first + k

                @pl.when(piece < pieces)
                def _():
                    @pl.when(piece % count == 0)
                    def _():
                        carry[...] = jnp.zeros_like(carry)
                        ahead[...] = jnp.zeros_like(ahead)

                    for copy in fetches(k):
                        copy.wait()
                    backward_piece(
                        block_heads, WIDTH, passes, piece // count, count - 1 - piece % count, cur.at[k], tail.at[k],
                        beta.at[k], conv_ref, gain_ref, grad_mixed, out.at[k], fresh.at[k], state.at[k], solve.at[k],
                        mix_right, mix_right.at[:, strength_lanes], gconv_ref, ggain_ref, carry, ahead,
                    )

        pl.run_scoped(
            scoped,
            pltpu.VMEM((2, CHUNK, span), F32),
            pltpu.VMEM((2, 8, span), F32),
            pltpu.VMEM((2, CHUNK, LANES), F32),
            pltpu.VMEM((2, CHUNK, block_heads * WIDTH), F32),
            pltpu.VMEM((2, CHUNK, block_heads * WIDTH), F32),
            pltpu.VMEM((2, block_heads, WIDTH, WIDTH), F32),
            pltpu.VMEM((2, block_heads, CHUNK, CHUNK), F32),
        )

    lags = [0, 1] + [4 + 3 * stage for stage in range(stages - 1)]
    quarter = gs.count // 4
    at_final, at_middle, at_delta = 16, 6, 7
    pieces = groups * count
    at_gf = at_delta + -(-pieces // 2)

    def step(i, carried):
        ffn.step(i, lags)
        mix.step(i - ffn_count - 0, lags)
        beta.step(i - at_gf - 1, lags)

        @pl.when(i < 4)
        def _():
            gs.run(i * quarter, quarter)

        @pl.when(i == at_middle)
        def _():
            gs.sent()
            bring_w_out.wait()
            bring_mixed.wait()
            middle_part()

        @pl.when((i >= at_delta) & (i < at_gf))
        def _():
            delta_parts((i - at_delta) * 2)

        @pl.when((i >= at_gf) & (i < at_gf + 4))
        def _():
            gf.run((i - at_gf) * quarter, quarter)

        smalls.run(i - at_gf - 4)

        @pl.when(i == at_final)
        def _():
            gf.sent()

        @pl.when((i >= at_final) & (i < at_final + 4))
        def _():
            final.run((i - at_final) * quarter, quarter)

        return carried

    steps = max(ffn_count + 0 + mix_count + lags[-1], at_final + 4, at_gf + 2 + lags[-1], at_gf + 6 + stages)
    lax.fori_loop(0, steps, step, 0)
    ffn.drain()
    mix.drain()
    beta.drain()
    final.sent()
    final.received()
    gf.received()


def pack_kernel(block, query_ref, key_ref, value_ref, beta_ref, out_ref, result_ref):
    span = block * WIDTH
    at = 0
    for group in range(query_ref.shape[1] // span):
        for part_ref in (query_ref, key_ref, value_ref):
            result_ref[:, at : at + span] = part_ref[:, group * span : (group + 1) * span].astype(BF16)
            at += span
    result_ref[:, at : at + LANES] = beta_ref[...].astype(BF16)
    at += LANES
    for begin in range(0, out_ref.shape[0], LANES):
        result_ref[:, at + begin : at + begin + LANES] = out_ref[begin : begin + LANES, :].T.astype(BF16)


def packed_mixer(block, w_query, w_key, w_value, w_beta, w_out):
    rows, columns = w_query.shape
    return pl.pallas_call(
        functools.partial(pack_kernel, block),
        out_shape=jax.ShapeDtypeStruct((rows, 4 * columns + LANES), BF16),
        name="packed_mixer",
    )(w_query, w_key, w_value, jnp.pad(w_beta, ((0, 0), (0, LANES - w_beta.shape[1]))), w_out)


def feed_forward_kernel(second_ref, upstream_ref, down_ref, gate_ref, up_ref, result_ref):
    part = 512
    for begin in range(0, second_ref.shape[0], part):
        rows = slice(begin, begin + part)
        gate = jnp.dot(second_ref[rows], gate_ref[...], preferred_element_type=F32)
        up = jnp.dot(second_ref[rows], up_ref[...], preferred_element_type=F32)
        grad_hidden = jnp.dot(upstream_ref[rows], down_ref[...], preferred_element_type=F32)
        sigma = sigmoid(gate)
        activated = gate * sigma
        result_ref[0, rows] = (activated * up).astype(BF16)
        result_ref[1, rows] = (grad_hidden * up * sigma * (1.0 + gate * (1.0 - sigma))).astype(BF16)
        result_ref[2, rows] = (grad_hidden * activated).astype(BF16)


def feed_forward(second, upstream, w_ffn):
    length, model = second.shape
    units = w_ffn.shape[1] // 3
    tile = 256 if units % 256 == 0 else 128
    tiles = units // tile
    whole = pl.BlockSpec((length, model), lambda j: (0, 0))
    weights = [pl.BlockSpec((model, tile), lambda j, k=k: (0, k * tiles + j)) for k in range(3)]
    return pl.pallas_call(
        feed_forward_kernel,
        grid=(tiles,),
        in_specs=[whole, whole] + weights,
        out_specs=pl.BlockSpec((3, length, tile), lambda j: (0, 0, j)),
        out_shape=jax.ShapeDtypeStruct((3, length, units), BF16),
        compiler_params=pltpu.CompilerParams(vmem_limit_bytes=32 * 2**20),
        name="feed_forward",
    )(second, upstream, w_ffn, w_ffn, w_ffn)


def backward_all(size, heads, block_heads, up_t, second_t, first_t, ffn_right, mixed, conv, gain, norm_ffn, w_mixer,
                 w_ffn, qkv, out, fresh, state, solve, middle, upstream, tokens, scale, passes=3):
    length = qkv.shape[0]
    model = up_t.shape[0]
    units = ffn_right.shape[2]
    block = model // size
    groups = heads // block_heads
    span = 3 * block_heads * WIDTH
    columns = heads * WIDTH
    raw_columns = groups * span + LANES
    mix_columns = raw_columns + columns
    ffn_tile = 256 if units % 256 == 0 else 128
    shapes = []
    mix_tile = 256 if columns % 256 == 0 else 128
    for total, tile in ((3 * units, ffn_tile), (4 * columns, mix_tile), (LANES, LANES)):
        tiles = next(t for t in (3, 2, 1) if total // tile % t == 0)
        shapes.append((total // tile // tiles, tiles, tile))
    landed, scratch = [], []
    for number, tiles, tile in shapes:
        more_landed, more_scratch = Scatter.scratch(size, block, number, tiles * tile)
        landed += more_landed
        scratch += more_scratch
    streamed = 256
    tiles = model // streamed
    stages = len(orders(size)[0])
    small_columns = max(groups * span, model)
    scratch += [
        pltpu.VMEM((4, model, length), BF16),
        pltpu.VMEM((length, mix_columns), BF16),
        pltpu.VMEM((2, streamed, max(units, raw_columns)), BF16),
        pltpu.SemaphoreType.DMA((2,)),
        pltpu.VMEM((tiles, length, streamed), BF16),
        pltpu.SemaphoreType.DMA((tiles,)),
        pltpu.SemaphoreType.DMA((tiles,)),
        pltpu.SemaphoreType.DMA((3, tiles)),
        pltpu.VMEM((model, columns), BF16),
        pltpu.VMEM((length, columns), F32),
        pltpu.VMEM((block_heads, WIDTH, WIDTH), F32),
        pltpu.VMEM((8, span), F32),
        pltpu.SemaphoreType.DMA((3, size)),
        pltpu.SemaphoreType.DMA((2,)),
        pltpu.SemaphoreType.DMA((2, 7)),
        pltpu.VMEM((4, groups * span), F32),
        pltpu.VMEM((1, WIDTH), F32),
        pltpu.VMEM((1, model), F32),
        pltpu.VMEM((2, length, streamed), BF16),
        pltpu.SemaphoreType.DMA((2,)),
        pltpu.VMEM((2, 8, model), F32),
        pltpu.VMEM((stages, 8, small_columns), F32),
        pltpu.VMEM((stages, 8, small_columns), F32),
        pltpu.SemaphoreType.DMA((2,)),
        pltpu.SemaphoreType.DMA((stages,)),
        pltpu.SemaphoreType.DMA((stages,)),
    ]
    vmem, hbm = pl.BlockSpec(memory_space=pltpu.VMEM), pl.BlockSpec(memory_space=pl.ANY)
    shape = jax.ShapeDtypeStruct
    exchanged = [shape((length, model), BF16)] * 6
    return pl.pallas_call(
        functools.partial(backward_kernel, (size, heads, block_heads, units, passes, shapes)),
        in_specs=[hbm] * 3 + [vmem, hbm] + [vmem] * 3 + [hbm] * 10 + [vmem],
        out_specs=[hbm] * 10 + [vmem] + [hbm] * len(landed),
        out_shape=[shape((block, 3 * units), F32), shape((block, 4 * columns), F32),
                   shape((block, LANES), F32), shape((length, model), F32)]
        + exchanged
        + [shape((8, small_columns), F32)]
        + landed,
        scratch_shapes=scratch,
        compiler_params=pltpu.CompilerParams(
            collective_id=0, has_side_effects=True, vmem_limit_bytes=63 * 2**20
        ),
        name="backward_all",
    )(up_t, second_t, first_t, ffn_right, mixed, conv, gain, norm_ffn, w_mixer, w_ffn, qkv, out, fresh, state, solve,
      middle, upstream, tokens, scale)[:11]


def matmul(left, right):
    return jnp.dot(left, right, preferred_element_type=F32)


def right_inner(left, right):
    return lax.dot_general(left, right, (((1,), (1,)), ((), ())), preferred_element_type=F32)


def row_norm(values, gain):
    return values * lax.rsqrt(jnp.mean(values * values, -1, keepdims=True) + epsilon) * gain


def swap(values, axis, size, by):
    return lax.ppermute(values, axis, [(d, d ^ by) for d in range(size)])


def exchange(partial):
    own = lax.reduce_precision(partial, 8, 7)
    return own, swap(own.astype(BF16), "tensor", 2, 1)


def by_groups(parts, block):
    span = block * WIDTH
    return [part[:, g * span : (g + 1) * span] for g in range(parts[0].shape[1] // span) for part in parts]


def from_groups(whole, block, index, columns):
    span = block * WIDTH
    return jnp.concatenate(
        [whole[:, (3 * g + index) * span : (3 * g + index + 1) * span] for g in range(columns // span)], 1
    )


def body(size, tokens, lengths, w_query, w_key, w_value, w_beta, conv_query, conv_key, conv_value, head_gain,
         w_out, norm_attn, norm_ffn, w_gate, w_up, w_down, cotangent):
    inputs = tokens.astype(F32)
    length, model = inputs.shape
    columns = w_query.shape[1]
    units = w_gate.shape[1]
    heads = w_beta.shape[1]
    block = 4 if heads % 4 == 0 else 1
    raw_columns = 3 * columns + LANES
    w_mixer = lax.all_gather(
        packed_mixer(block, w_query, w_key, w_value, w_beta, w_out), "dp", axis=0, tiled=True
    )
    w_ffn = lax.all_gather(
        jnp.concatenate([w_down.astype(BF16).T, w_gate.astype(BF16), w_up.astype(BF16)], 1), "dp", axis=0, tiled=True
    )
    conv = jnp.concatenate(by_groups([conv_query, conv_key, conv_value], block), 1)
    gain = head_gain[None]

    first_scale = lax.rsqrt(jnp.mean(inputs * inputs, -1, keepdims=True) + epsilon)
    first = (inputs * first_scale * norm_attn).astype(BF16)
    qkv = matmul(first, w_mixer[:, :raw_columns])
    mixed, out, fresh, state, solve = delta_forward(qkv, conv, gain, heads, block, (3, 3, 3, 3))
    own, other = exchange(right_inner(mixed, w_mixer[:, raw_columns:]))
    middle = inputs + (own + other.astype(F32))
    second = row_norm(middle, norm_ffn).astype(BF16)
    positions = lax.broadcasted_iota(jnp.int32, (length, 1), 0)
    valid = (positions < lengths[0]).astype(F32)
    upstream = (cotangent.astype(F32) * valid).astype(BF16)
    (ffn_grads, mixer_grads, beta_grads, grad_middle, _, _, final_own, final_other, first_own, first_other,
     small) = backward_all(
        size, heads, block, upstream.T, second.T, first.T,
        feed_forward(second, upstream, w_ffn),
        mixed, conv, gain, norm_ffn[None], w_mixer, w_ffn, qkv, out, fresh, state, solve, middle, upstream, tokens, first_scale,
    )
    final = middle + (final_own.astype(F32) + final_other.astype(F32))
    block_out = (final * valid).astype(BF16)
    normal = inputs * first_scale
    scaled = (first_own.astype(F32) + first_other.astype(F32)) * norm_attn
    grad_tokens = grad_middle + first_scale * (scaled - normal * jnp.mean(scaled * normal, -1, keepdims=True))
    convs = small[:4, : 3 * columns]
    return (
        block_out,
        grad_tokens,
        from_groups(mixer_grads, block, 0, columns),
        from_groups(mixer_grads, block, 1, columns),
        from_groups(mixer_grads, block, 2, columns),
        beta_grads[:, :heads],
        from_groups(convs, block, 0, columns),
        from_groups(convs, block, 1, columns),
        from_groups(convs, block, 2, columns),
        small[6, :WIDTH],
        mixer_grads[:, 3 * columns :].T,
        small[5, :model],
        small[4, :model],
        ffn_grads[:, units : 2 * units],
        ffn_grads[:, 2 * units :],
        ffn_grads[:, :units].T,
    )


def solution(mesh):
    rows, both, cols = P("dp", None), P("dp", "tensor"), P("tensor", "dp")
    taps = P(None, "tensor")
    in_specs = (rows, P("dp"), both, both, both, both, taps, taps, taps, P(), cols, P(), P(), both, both, cols, rows)
    out_specs = (rows, rows, both, both, both, both, taps, taps, taps, P(), cols, P(), P(), both, both, cols)
    return jax.shard_map(
        functools.partial(body, mesh.shape["dp"]), mesh=mesh, in_specs=in_specs, out_specs=out_specs, check_vma=False
    )
```
